32 devices in a mesh: dp: 8 (over y, x, core), mp: 4 (over z).
Axes of the slice: x: 2, y: 2, z: 4, core: 2. Of those that a mesh axis runs over, the one named last changes fastest.
Arguments:
- tokens: bfloat16 [32, 512, 768], P('dp'), may hold values from -6 to 6
- doc_lengths: int32 [32, 4], P('dp'), may hold values from 1 to 256, 512 in all within a row
- w_query: bfloat16 [768, 768], P(None, 'mp'), may hold values from -0.21875 to 0.21875
- b_query: bfloat16 [768], P('mp'), may hold values from -3 to 3
- w_key: bfloat16 [768, 768], P(None, 'mp'), may hold values from -0.21875 to 0.21875
- w_value: bfloat16 [768, 768], P(None, 'mp'), may hold values from -0.21875 to 0.21875
- b_value: bfloat16 [768], P('mp'), may hold values from -3 to 3
- w_output: bfloat16 [768, 768], P('mp'), may hold values from -0.875 to 0.875
- b_output: bfloat16 [768], replicated, may hold values from -3 to 3
- gain_attn: bfloat16 [768], replicated, may hold values from 0.5 to 1.5
- shift_attn: bfloat16 [768], replicated, may hold values from -2 to 2
- w_expand: bfloat16 [768, 3072], P(None, 'mp'), may hold values from -0.21875 to 0.21875
- b_expand: bfloat16 [3072], P('mp'), may hold values from -3 to 3
- w_reduce: bfloat16 [3072, 768], P('mp'), may hold values from -0.21875 to 0.21875
- b_reduce: bfloat16 [768], replicated, may hold values from -2 to 2
- gain_ffn: bfloat16 [768], replicated, may hold values from 0.5 to 1.5
- shift_ffn: bfloat16 [768], replicated, may hold values from -2 to 2
- cotangent: bfloat16 [32, 512, 768], P('dp'), may hold values from -6 to 6
Outputs:
- output: bfloat16 [32, 512, 768], P('dp')
- grad_tokens: bfloat16 [32, 512, 768], P('dp')
- grad_w_query: float32 [768, 768], P(None, 'mp')
- grad_b_query: float32 [768], P('mp')
- grad_w_key: float32 [768, 768], P(None, 'mp')
- grad_w_value: float32 [768, 768], P(None, 'mp')
- grad_b_value: float32 [768], P('mp')
- grad_w_output: float32 [768, 768], P('mp')
- grad_b_output: float32 [768], replicated
- grad_gain_attn: float32 [768], replicated
- grad_shift_attn: float32 [768], replicated
- grad_w_expand: float32 [768, 3072], P(None, 'mp')
- grad_b_expand: float32 [3072], P('mp')
- grad_w_reduce: float32 [3072, 768], P('mp')
- grad_b_reduce: float32 [768], replicated
- grad_gain_ffn: float32 [768], replicated
- grad_shift_ffn: float32 [768], replicated
The draws below stay inside these ranges and needn't reach their ends.
Inputs may be any that keep to these rules, and one draw needn't show every extreme that they name: `doc_lengths`: the 4 lengths of a row sum to 512, and the largest of every row is 256.
All inputs are finite; a program needn't handle non-finite values.
Results may differ from the reference program's by a relative error of at most 0.014.
Values sent between devices are 32-bit elements; how exact they have to be, the bound alone decides.
No kernel may reach another device: no remote copies, remote signals or barrier semaphores. Data moves between devices by JAX's collectives and lax.ppermute only.
A program may use at most 128 MiB of HBM per device.

```python
import math
from functools import partial
import jax
import jax.numpy as jnp
import numpy as np
from jax import lax

D = 768
HEADS = 12
HD = 64
FF = 3072
SEQ = 512
DOCS = 4
ROWS = 32


def steps_of(stream_key, shape, split, low, top_value):
    gain = 1.0
    for dim, blocks in split:
        heights = jax.random.uniform(jax.random.fold_in(jax.random.fold_in(stream_key, 6), dim), (blocks,), jnp.float32, low / len(split), top_value / len(split))
        gain = gain * jnp.repeat(jnp.exp(heights), shape[dim] // blocks).reshape((-1,) + (1,) * (len(shape) - 1 - dim))
    return gain


def length_profile(amount, total, bound, slope):
    weights = [(1 << 20) // math.isqrt(standing ** slope) + 1 for standing in range(2, amount + 1)]
    surplus, given = total - bound - (amount - 1), [1] * (amount - 1)
    while surplus > 0:
        candidates = [i for i in range(amount - 1) if given[i] < bound]
        pool, left = sum([weights[i] for i in candidates]), surplus
        for i in candidates:
            more = min(bound - given[i], max(1, left * weights[i] // pool), surplus)
            given[i] = given[i] + more
            surplus = surplus - more
    return np.array([bound] + given)


def uneven_parts(rng, number_of, total, limit, lean):
    if number_of == 2:
        one = jax.random.randint(rng, (), max(1, total - limit), min(limit, total - 1) + 1)
        return jnp.stack([one, total - one])
    lengths = jnp.asarray(length_profile(number_of, total, limit, lean), jnp.int32)
    twos = (number_of - 1) // 2
    source_of, taker = lengths[1:1 + 2 * twos:2], lengths[2:2 + 2 * twos:2]
    room = jnp.minimum(source_of - 1, limit - taker)
    shifted = jax.random.randint(jax.random.fold_in(rng, 1), (twos,), 0, 1 << 20) % (room + 1)
    lengths = lengths.at[1:1 + 2 * twos:2].set(source_of - shifted).at[2:2 + 2 * twos:2].set(taker + shifted)
    return lengths[jax.random.permutation(jax.random.fold_in(rng, 2), number_of)]


def scatter_about(stream_key, dims, scale, most, split=(), kind=jnp.bfloat16):
    values = scale * jax.random.normal(stream_key, dims, jnp.float32)
    if split:
        values = values * steps_of(stream_key, dims, split, -0.22, 0.18)
    return jnp.clip(values, -most, most).astype(kind)


def setup_inputs(seed: int = 0) -> dict:
    splits = jax.random.split(jax.random.key(seed), 19)
    return {
        "tokens": scatter_about(splits[0], (ROWS, SEQ, D), 1.0, 6.0, ((0, 8),)),
        "doc_lengths": jax.vmap(lambda own: uneven_parts(own, DOCS, SEQ, SEQ // 2, 2))(jax.random.split(splits[1], ROWS)).reshape((ROWS, DOCS)).astype(jnp.int32),
        "w_query": scatter_about(splits[2], (D, D), D ** -0.5, 0.21875, ((1, 4),)),
        "b_query": scatter_about(splits[3], (D,), 0.5, 3.0, ((0, 4),)),
        "w_key": scatter_about(splits[4], (D, D), D ** -0.5, 0.21875, ((1, 4),)),
        "w_value": scatter_about(splits[5], (D, D), D ** -0.5, 0.21875, ((1, 4),)),
        "b_value": scatter_about(splits[6], (D,), 0.5, 3.0, ((0, 4),)),
        "w_output": scatter_about(splits[7], (D, D), (D // 16) ** -0.5, 0.875, ((0, 4),)),
        "b_output": scatter_about(splits[8], (D,), 0.5, 3.0),
        "gain_attn": jnp.clip(1.0 + 0.1 * jax.random.normal(splits[9], (D,), jnp.float32), 0.5, 1.5).astype(jnp.bfloat16),
        "shift_attn": scatter_about(splits[10], (D,), 0.3, 2.0),
        "w_expand": scatter_about(splits[11], (D, FF), D ** -0.5, 0.21875, ((1, 4),)),
        "b_expand": scatter_about(splits[12], (FF,), 0.5, 3.0, ((0, 4),)),
        "w_reduce": scatter_about(splits[13], (FF, D), (FF // 4) ** -0.5, 0.21875, ((0, 4),)),
        "b_reduce": scatter_about(splits[14], (D,), 0.3, 2.0),
        "gain_ffn": jnp.clip(1.0 + 0.1 * jax.random.normal(splits[15], (D,), jnp.float32), 0.5, 1.5).astype(jnp.bfloat16),
        "shift_ffn": scatter_about(splits[16], (D,), 0.3, 2.0),
        "cotangent": scatter_about(splits[17], (ROWS, SEQ, D), 1.0, 6.0, ((0, 8),)),
    }


norm_eps = 1e-12
masked_score = -1000000000.0

@jax.custom_vjp
def low(v):
    return lax.optimization_barrier(v.astype(jnp.bfloat16)).astype(jnp.float32)

@jax.custom_vjp
def low_back(v):
    return v

def low_keep(v):
    return (low(v), None)

def low_pass(kept, grad):
    return (grad,)

def back_keep(v):
    return (v, None)

def back_low(kept, grad):
    return (low(grad),)
low.defvjp(low_keep, low_pass)
low_back.defvjp(back_keep, back_low)

def matmul_high(left_op, right_op):
    return jnp.matmul(left_op, right_op, precision=lax.Precision.HIGHEST)

def layer_norm(hidden, gain_vec, shift_vec):
    center = hidden - lax.optimization_barrier(jnp.mean(hidden, axis=-1, keepdims=True))
    spread = lax.optimization_barrier(jnp.mean(center * center, axis=-1, keepdims=True))
    return center * lax.rsqrt(spread + norm_eps) * gain_vec + shift_vec

def gelu_tanh(values):
    return jax.nn.gelu(values, approximate=True)

def segment_ids(doc_lengths):
    doc_ends = jnp.cumsum(doc_lengths, axis=-1).astype(jnp.int32)
    position = jnp.arange(SEQ, dtype=jnp.int32)
    return lax.optimization_barrier(jnp.sum((position[None, :, None] >= doc_ends[:, None, :]).astype(jnp.int32), axis=-1)).astype(jnp.int32)

def attend_row(packed):
    queries, keys_row, values_row, segment = packed
    scores = jnp.einsum('qhd,khd->hqk', queries, keys_row, precision=lax.Precision.HIGHEST) * HD ** (-0.5)
    scores = low_back(scores)
    same_doc = segment[:, None] == segment[None, :]
    scores = jnp.where(same_doc[None], scores, masked_score)
    attn_probs = jax.nn.softmax(scores, axis=-1)
    return jnp.einsum('hqk,khd->qhd', low(attn_probs), values_row, precision=lax.Precision.HIGHEST)

def forward(tokens, w_query, b_query, w_key, w_value, b_value, w_output, b_output, gain_attn, shift_attn, w_expand, b_expand, w_reduce, b_reduce, gain_ffn, shift_ffn, segment):
    inputs = tokens.reshape(ROWS * SEQ, D)
    queries = low(low_back(matmul_high(inputs, w_query) + b_query))
    keys_all = low(low_back(matmul_high(inputs, w_key)))
    values_all = low(low_back(matmul_high(inputs, w_value) + b_value))
    head_split = (ROWS, SEQ, HEADS, HD)
    context = lax.map(jax.checkpoint(attend_row), (queries.reshape(head_split), keys_all.reshape(head_split), values_all.reshape(head_split), segment))
    context = low(low_back(context.reshape(ROWS * SEQ, D)))
    attended = low_back(matmul_high(context, w_output)) + b_output
    normed = layer_norm(inputs + attended, gain_attn, shift_attn)
    hidden = low_back(matmul_high(low(normed), w_expand) + b_expand)
    mixed_out = low_back(matmul_high(low(gelu_tanh(hidden)), w_reduce)) + b_reduce
    return layer_norm(normed + mixed_out, gain_ffn, shift_ffn).reshape(ROWS, SEQ, D)

def reference(tokens, doc_lengths, w_query, b_query, w_key, w_value, b_value, w_output, b_output, gain_attn, shift_attn, w_expand, b_expand, w_reduce, b_reduce, gain_ffn, shift_ffn, cotangent):
    segment = segment_ids(doc_lengths)
    floats = [array_in.astype(jnp.float32) for array_in in (tokens, w_query, b_query, w_key, w_value, b_value, w_output, b_output, gain_attn, shift_attn, w_expand, b_expand, w_reduce, b_reduce, gain_ffn, shift_ffn)]
    output, backward = jax.vjp(partial(forward, segment=segment), *floats)
    gradients = backward(cotangent.astype(jnp.float32))
    return (output.astype(jnp.bfloat16), gradients[0].astype(jnp.bfloat16), gradients[1], gradients[2], gradients[3], gradients[4], gradients[5], gradients[6], gradients[7], gradients[8], gradients[9], gradients[10], gradients[11], gradients[12], gradients[13], gradients[14], gradients[15])
```

```python
import jax
import jax.numpy as jnp
from jax import lax
from jax.experimental import pallas as pl
from jax.experimental.pallas import tpu as pltpu
from jax.sharding import PartitionSpec as P

HD = 64
GROUP = 8
EXTRA = 16
MASK = -float(2**30)
EPS = 1e-12
F32 = jnp.float32
BF16 = jnp.bfloat16
LIMIT = 60 << 20


def dot(left, right, left_dim, right_dim):
    return lax.dot_general(
        left, right, (((left_dim,), (right_dim,)), ((), ())), preferred_element_type=F32
    )


def params():
    return pltpu.CompilerParams(vmem_limit_bytes=LIMIT)


def cost(flops, moved):
    return pl.CostEstimate(flops=int(flops), bytes_accessed=int(moved), transcendentals=0)


def whole(shape):
    zeros = (0,) * len(shape)
    return pl.BlockSpec(shape, lambda *_: zeros, pipeline_mode=pl.Buffered(1))


def split3(row):
    high = row.astype(BF16).astype(F32)
    rest = row - high
    mid = rest.astype(BF16).astype(F32)
    return high, mid, rest - mid


def rows_of(height, first, parts, width):
    place = lax.broadcasted_iota(jnp.int32, (height, width), 0)
    out = jnp.zeros((height, width), F32)
    for i, part in enumerate(parts):
        out = jnp.where(place == first + i, part, out)
    return out


def assemble_small_kernel(place_ref, mine_ref, other_ref, out_ref):
    rows = mine_ref.shape[2]
    for rel in range(4):
        for source, ref in enumerate((mine_ref, other_ref)):
            start = pl.multiple_of(place_ref[2 * rel + source] * rows, rows)
            for k in range(mine_ref.shape[1]):
                out_ref[k, pl.ds(start, rows), :] = ref[rel, k].astype(BF16)


def assemble_small(place, mine, other):
    _, peers, rows, width = mine.shape
    return pl.pallas_call(
        assemble_small_kernel,
        grid_spec=pltpu.PrefetchScalarGridSpec(
            num_scalar_prefetch=1,
            grid=(1,),
            in_specs=[whole(mine.shape), whole(other.shape)],
            out_specs=whole((peers, GROUP * rows, width)),
        ),
        out_shape=jax.ShapeDtypeStruct((peers, GROUP * rows, width), BF16),
        compiler_params=params(),
        cost_estimate=cost(0, mine.size * 12),
        name="assemble_heads",
    )(place, mine, other)


def assemble_big_kernel(place_ref, own_ref, mine_ref, other_ref, out_ref):
    rows = mine_ref.shape[2]
    shards = out_ref.shape[0]
    me = place_ref[8]
    out_ref[me] = own_ref[...]
    for k in range(mine_ref.shape[1]):
        shard = lax.rem(me + shards - 1 - k, shards)
        for rel in range(4):
            for source, ref in enumerate((mine_ref, other_ref)):
                start = pl.multiple_of(place_ref[2 * rel + source] * rows, rows)
                out_ref[shard, pl.ds(start, rows), :] = ref[rel, k].astype(BF16)


def assemble_big(place, own, mine, other):
    _, peers, rows, width = mine.shape
    shape = (peers + 1,) + own.shape
    return pl.pallas_call(
        assemble_big_kernel,
        grid_spec=pltpu.PrefetchScalarGridSpec(
            num_scalar_prefetch=1,
            grid=(1,),
            in_specs=[whole(own.shape), whole(mine.shape), whole(other.shape)],
            out_specs=whole(shape),
        ),
        out_shape=jax.ShapeDtypeStruct(shape, BF16),
        compiler_params=params(),
        cost_estimate=cost(0, mine.size * 12),
        name="assemble_ffn",
    )(place, own, mine, other)


def attend_forward_kernel(length, x_ref, w_ref, bias_ref, qf_ref, kf_ref, qkv_ref, ctx_ref, aug_ref):
    tokens = x_ref.shape[0]
    proj = dot(w_ref[0, : 3 * HD, :], x_ref[...], 1, 1) + bias_ref[0]
    scale = HD ** (-0.5)
    qkv_ref[0, :HD, :] = (proj[:HD] * scale).astype(BF16)
    qkv_ref[0, HD:, :] = proj[HD:].astype(BF16)
    ones_rows = rows_of(EXTRA, 0, (jnp.ones((1, length), F32),), length).astype(BF16)

    def row(r, carry):
        at = pl.ds(pl.multiple_of(r * length, length), length)
        queries = jnp.concatenate([qkv_ref[0, :HD, at], qf_ref[:, at]], axis=0)
        keys = jnp.concatenate([qkv_ref[0, HD : 2 * HD, at], kf_ref[:, at]], axis=0)
        values = jnp.concatenate([qkv_ref[0, 2 * HD :, at], ones_rows], axis=0)
        scores = dot(keys, queries, 0, 0)
        highest = jnp.max(scores, axis=0, keepdims=True)
        weight = jnp.exp(scores - highest).astype(BF16)
        context = dot(values, weight, 1, 0)
        total = context[HD : HD + 1]
        ctx_ref[0, :, at] = (context[:HD] * (1.0 / total)).astype(BF16)
        log_total = highest + jnp.log(total)
        extra = rows_of(EXTRA, 4, split3(-log_total), length)
        aug_ref[0, :, at] = (extra + qf_ref[:, at].astype(F32)).astype(BF16)
        return carry

    lax.fori_loop(0, tokens // length, row, 0, unroll=2)


def attend_forward(length, inputs, weights, bias, qf, kf):
    heads, height, width = weights.shape
    tokens = inputs.shape[0]
    by_head = lambda *shape: pl.BlockSpec((1,) + shape, lambda h: (h, 0, 0))
    return pl.pallas_call(
        lambda *refs: attend_forward_kernel(length, *refs),
        grid=(heads,),
        in_specs=[
            whole(inputs.shape),
            by_head(height, width),
            by_head(3 * HD, 1),
            whole(qf.shape),
            whole(kf.shape),
        ],
        out_specs=[by_head(3 * HD, tokens), by_head(HD, tokens), by_head(EXTRA, tokens)],
        out_shape=[
            jax.ShapeDtypeStruct((heads, 3 * HD, tokens), BF16),
            jax.ShapeDtypeStruct((heads, HD, tokens), BF16),
            jax.ShapeDtypeStruct((heads, EXTRA, tokens), BF16),
        ],
        compiler_params=params(),
        cost_estimate=cost(heads * tokens * (6 * HD * width + 16 * 64 * length), 12e6),
        name="attend_forward",
    )(inputs, weights, bias, qf, kf)


def attend_backward_kernel(length, qkv_ref, ctx_ref, aug_ref, grad_ref, kf_ref, out_ref):
    tokens = kf_ref.shape[1]
    scale = HD ** (-0.5)
    one = jnp.ones((1, length), F32)
    ones_rows = rows_of(EXTRA, 0, (one, one, one), length).astype(BF16)

    def row(r, carry):
        at = pl.ds(pl.multiple_of(r * length, length), length)
        queries = qkv_ref[0, :HD, at]
        keys = qkv_ref[0, HD : 2 * HD, at]
        values = qkv_ref[0, 2 * HD :, at]
        grad_context = grad_ref[0, :, at]
        inner = jnp.sum(
            grad_context.astype(F32) * ctx_ref[0, :, at].astype(F32), axis=0, keepdims=True
        )
        grad_extra = rows_of(EXTRA, 0, split3(-inner), length).astype(BF16)
        scores = dot(
            jnp.concatenate([keys, kf_ref[:, at]], axis=0),
            jnp.concatenate([queries, aug_ref[0, :, at]], axis=0),
            0,
            0,
        )
        probs = jnp.exp(scores)
        spread = dot(
            jnp.concatenate([values, ones_rows], axis=0),
            jnp.concatenate([grad_context, grad_extra], axis=0),
            0,
            0,
        )
        grad_scores = (probs * spread).astype(BF16)
        out_ref[0, 2 * HD :, at] = dot(grad_context, probs.astype(BF16), 1, 1).astype(BF16)
        out_ref[0, HD : 2 * HD, at] = dot(queries, grad_scores, 1, 1).astype(BF16)
        out_ref[0, :HD, at] = (dot(keys, grad_scores, 1, 0) * scale).astype(BF16)
        return carry

    lax.fori_loop(0, tokens // length, row, 0, unroll=2)


def attend_backward(length, qkv, ctx, aug, grad, kf):
    heads, _, tokens = qkv.shape
    by_head = lambda *shape: pl.BlockSpec((1,) + shape, lambda h: (h, 0, 0))
    return pl.pallas_call(
        lambda *refs: attend_backward_kernel(length, *refs),
        grid=(heads,),
        in_specs=[
            by_head(3 * HD, tokens),
            by_head(HD, tokens),
            by_head(EXTRA, tokens),
            by_head(HD, tokens),
            whole(kf.shape),
        ],
        out_specs=by_head(3 * HD, tokens),
        out_shape=jax.ShapeDtypeStruct((heads, 3 * HD, tokens), BF16),
        compiler_params=params(),
        cost_estimate=cost(heads * tokens * 40 * 64 * length, 12e6),
        name="attend_backward",
    )(qkv, ctx, aug, grad, kf)


def norm_forward(hidden):
    center = hidden - jnp.mean(hidden, axis=-1, keepdims=True)
    inverse = lax.rsqrt(jnp.mean(center * center, axis=-1, keepdims=True) + EPS)
    return center * inverse, inverse


def norm_backward(grad, gain, norm, inverse):
    scaled = grad * gain
    first = jnp.mean(scaled, axis=-1, keepdims=True)
    second = jnp.mean(scaled * norm, axis=-1, keepdims=True)
    return (scaled - first - norm * second) * inverse


def column_sum(values):
    return jnp.sum(values, axis=0, keepdims=True)


def dense_kernel(
    local_heads,
    place_ref,
    x_ref,
    cot_ref,
    ctx_own_ref,
    ctx_refs,
    wo_own_ref,
    wo_refs,
    we_ref,
    wr_ref,
    bias_ref,
    vec_ref,
    out_ref,
    g1_ref,
    dctx_own_ref,
    dctx_refs,
    dwe_ref,
    dwr_ref,
    dwo_ref,
    small_ref,
    wo_scr,
    ctx_scr,
    act_scr,
    slope_scr,
    gh_scr,
    dctx_scr,
):
    step = pl.program_id(0)
    shards = we_ref.shape[0]
    me = place_ref[8]
    span = local_heads * HD

    def start_of(k, j):
        shard = lax.rem(me + shards - k, shards)
        return pl.multiple_of(shard * span + j * HD, HD)

    @pl.when(step == 0)
    def _():
        for j in range(local_heads):
            wo_scr[pl.ds(start_of(0, j), HD), :] = wo_own_ref[j]
            for k in range(1, shards):
                wo_scr[pl.ds(start_of(k, j), HD), :] = wo_refs[j][k - 1]
        dwe_ref[...] = jnp.zeros_like(dwe_ref)
        dwr_ref[...] = jnp.zeros_like(dwr_ref)
        dwo_ref[...] = jnp.zeros_like(dwo_ref)
        small_ref[...] = jnp.zeros_like(small_ref)

    for j in range(local_heads):
        ctx_scr[pl.ds(start_of(0, j), HD), :] = ctx_own_ref[j]
        for k in range(1, shards):
            ctx_scr[pl.ds(start_of(k, j), HD), :] = ctx_refs[j][k - 1]

    b_output, gain_one, shift_one = vec_ref[0:1], vec_ref[1:2], vec_ref[2:3]
    b_reduce, gain_two, shift_two = vec_ref[3:4], vec_ref[4:5], vec_ref[5:6]

    attended = dot(ctx_scr[...], wo_scr[...], 0, 0) + b_output
    norm_one, inverse_one = norm_forward(x_ref[...].astype(F32) + attended)
    normed = norm_one * gain_one + shift_one
    normed_low = normed.astype(BF16)

    mixed = jnp.zeros_like(normed)
    for s in range(shards):
        b_expand = bias_ref[lax.rem(me + shards - s, shards), 1:2]
        hidden = dot(normed_low, we_ref[s], 1, 0) + b_expand
        square = hidden * hidden
        inner = 0.7978845608028654 * (hidden + 0.044715 * hidden * square)
        bent = jnp.tanh(inner)
        half = 0.5 * (1.0 + bent)
        active = (hidden * half).astype(BF16)
        act_scr[s] = active
        slope_scr[s] = half + 0.5 * hidden * (1.0 - bent * bent) * (
            0.7978845608028654 * (1.0 + 0.134145 * square)
        )
        mixed = mixed + dot(active, wr_ref[s], 1, 0)

    norm_two, inverse_two = norm_forward(normed + (mixed + b_reduce))
    out_ref[...] = (norm_two * gain_two + shift_two).astype(BF16)

    cot = cot_ref[...].astype(F32)
    grad_two = norm_backward(cot, gain_two, norm_two, inverse_two)
    grad_two_low = grad_two.astype(BF16)

    grad_normed = grad_two
    for s in range(shards):
        grad_active = dot(grad_two_low, wr_ref[s], 1, 1)
        grad_hidden = (grad_active * slope_scr[s]).astype(BF16)
        gh_scr[s] = grad_hidden
        grad_normed = grad_normed + dot(grad_hidden, we_ref[s], 1, 1)

    own = gh_scr[me]
    dwr_ref[...] += dot(act_scr[me], grad_two_low, 0, 0)
    dwe_ref[...] += dot(normed_low, own, 0, 0)

    grad_one = norm_backward(grad_normed, gain_one, norm_one, inverse_one)
    grad_one_low = grad_one.astype(BF16)
    g1_ref[...] = grad_one
    for j in range(local_heads):
        dwo_ref[j] += dot(ctx_own_ref[j], grad_one_low, 1, 0)
    dctx_scr[...] = dot(wo_scr[...], grad_one_low, 1, 1).astype(BF16)
    for j in range(local_heads):
        dctx_own_ref[j] = dctx_scr[pl.ds(start_of(0, j), HD), :]
        for k in range(1, shards):
            dctx_refs[j][k - 1] = dctx_scr[pl.ds(start_of(k, j), HD), :]

    small_ref[0:1] += column_sum(grad_one)
    small_ref[1:2] += column_sum(grad_normed * norm_one)
    small_ref[2:3] += column_sum(grad_normed)
    small_ref[3:4] += column_sum(grad_two)
    small_ref[4:5] += column_sum(cot * norm_two)
    small_ref[5:6] += column_sum(cot)
    small_ref[6:7] += column_sum(own.astype(F32))


def dense(place, inputs, cot, ctx_sets, weight_sets, w_expand, w_reduce, biases, vectors):
    tokens, width = inputs.shape
    shards, _, hidden = w_expand.shape
    local_heads = ctx_sets[0].shape[0]
    block = 256
    by_token = lambda: pl.BlockSpec((block, width), lambda i, *_: (i, 0))
    columns = lambda a: pl.BlockSpec((a.shape[0], HD, block), lambda i, *_: (0, 0, i))
    wo_spec = lambda a: pl.BlockSpec(
        (a.shape[0], HD, width), lambda i, *_: (0, 3, 0), pipeline_mode=pl.Buffered(1)
    )
    n = local_heads

    def body(place_ref, *refs):
        refs = list(refs)
        take = lambda count: [refs.pop(0) for _ in range(count)]
        x_ref, cot_ref, ctx_own = take(3)
        ctx_refs = take(n)
        (wo_own,) = take(1)
        wo_refs = take(n)
        we_ref, wr_ref, bias_ref, vec_ref, out_ref, g1_ref, dctx_own = take(7)
        dctx_refs = take(n)
        dense_kernel(
            n,
            place_ref,
            x_ref,
            cot_ref,
            ctx_own,
            ctx_refs,
            wo_own,
            wo_refs,
            we_ref,
            wr_ref,
            bias_ref,
            vec_ref,
            out_ref,
            g1_ref,
            dctx_own,
            dctx_refs,
            *refs,
        )

    shapes = [
        jax.ShapeDtypeStruct((tokens, width), BF16),
        jax.ShapeDtypeStruct((tokens, width), F32),
        *[jax.ShapeDtypeStruct(a.shape, BF16) for a in ctx_sets],
        jax.ShapeDtypeStruct((width, hidden), F32),
        jax.ShapeDtypeStruct((hidden, width), F32),
        jax.ShapeDtypeStruct((n, HD, width), F32),
        jax.ShapeDtypeStruct((8, width), F32),
    ]
    return pl.pallas_call(
        body,
        grid_spec=pltpu.PrefetchScalarGridSpec(
            num_scalar_prefetch=1,
            grid=(tokens // block,),
            in_specs=[
                by_token(),
                by_token(),
                *[columns(a) for a in ctx_sets],
                *[wo_spec(a) for a in weight_sets],
                whole(w_expand.shape),
                whole(w_reduce.shape),
                whole(biases.shape),
                whole(vectors.shape),
            ],
            out_specs=[
                by_token(),
                by_token(),
                *[columns(a) for a in ctx_sets],
                whole((width, hidden)),
                whole((hidden, width)),
                whole((n, HD, width)),
                whole((8, width)),
            ],
            scratch_shapes=[
                pltpu.VMEM((shards * n * HD, width), BF16),
                pltpu.VMEM((shards * n * HD, block), BF16),
                pltpu.VMEM((shards, block, hidden), BF16),
                pltpu.VMEM((shards, block, hidden), F32),
                pltpu.VMEM((shards, block, hidden), BF16),
                pltpu.VMEM((shards * n * HD, block), BF16),
            ],
        ),
        out_shape=shapes,
        compiler_params=params(),
        cost_estimate=cost(tokens * width * (8 * shards + 8) * hidden, 30e6),
        name="dense_middle",
    )(place, inputs, cot, *ctx_sets, *weight_sets, w_expand, w_reduce, biases, vectors)


def own_grads_kernel(dqkv_ref, x_ref, out_ref, sum_ref):
    for j in range(dqkv_ref.shape[0]):
        out_ref[j] = dot(dqkv_ref[j], x_ref[...], 1, 0)
        sums = jnp.sum(dqkv_ref[j].astype(F32), axis=1, keepdims=True)
        sum_ref[j] = jnp.broadcast_to(sums, sum_ref.shape[1:])


def own_grads(dqkv, inputs):
    heads, height, tokens = dqkv.shape
    width = inputs.shape[1]
    return pl.pallas_call(
        own_grads_kernel,
        out_shape=[
            jax.ShapeDtypeStruct((heads, height, width), F32),
            jax.ShapeDtypeStruct((heads, height, 128), F32),
        ],
        compiler_params=params(),
        cost_estimate=cost(2 * heads * height * tokens * width, 8e6),
        name="own_grads",
    )(dqkv, inputs)


def input_grads_kernel(place_ref, g1_ref, *refs):
    step = pl.program_id(0)
    me = place_ref[8]
    sets = (len(refs) - 3) // 2
    grads, weights = refs[:sets], refs[sets : 2 * sets]
    out_ref, grad_scr, w_scr = refs[2 * sets :]
    heads = grads[0].shape[0]
    height = 3 * HD
    shards = grad_scr.shape[0] // (heads * height)

    def start_of(k, j):
        shard = lax.rem(me + shards - k, shards)
        return pl.multiple_of((shard * heads + j) * height, HD)

    @pl.when(step == 0)
    def _():
        for j in range(heads):
            w_scr[pl.ds(start_of(0, j), height), :] = weights[0][j, :height, :]
            for k in range(1, shards):
                w_scr[pl.ds(start_of(k, j), height), :] = weights[j + 1][k - 1, :height, :]

    for j in range(heads):
        grad_scr[pl.ds(start_of(0, j), height), :] = grads[0][j]
        for k in range(1, shards):
            grad_scr[pl.ds(start_of(k, j), height), :] = grads[j + 1][k - 1]
    out_ref[...] = (g1_ref[...] + dot(grad_scr[...], w_scr[...], 0, 0)).astype(BF16)


def input_grads(place, grad_one, grad_sets, weight_sets):
    tokens, width = grad_one.shape
    block = 256
    count = sum(a.shape[0] for a in grad_sets) * 3 * HD
    by_token = lambda: pl.BlockSpec((block, width), lambda i, *_: (i, 0))
    return pl.pallas_call(
        input_grads_kernel,
        grid_spec=pltpu.PrefetchScalarGridSpec(
            num_scalar_prefetch=1,
            grid=(tokens // block,),
            in_specs=[
                by_token(),
                *[
                    pl.BlockSpec((a.shape[0], 3 * HD, block), lambda i, *_: (0, 0, i))
                    for a in grad_sets
                ],
                *[whole(a.shape) for a in weight_sets],
            ],
            out_specs=by_token(),
            scratch_shapes=[pltpu.VMEM((count, block), BF16), pltpu.VMEM((count, width), BF16)],
        ),
        out_shape=jax.ShapeDtypeStruct((tokens, width), BF16),
        compiler_params=params(),
        cost_estimate=cost(2 * tokens * width * count, 20e6),
        name="input_grads",
    )(place, grad_one, *grad_sets, *weight_sets)


def solution(mesh):
    peers = mesh.shape["mp"]
    lanes = mesh.shape["dp"]
    rotations = [[(i, (i + k) % peers) for i in range(peers)] for k in range(1, peers)]
    flips = lambda bit: [(i, i ^ bit) for i in range(lanes)]

    def flip(values, bit):
        return lax.ppermute(values, "dp", flips(bit))

    def gather(piece):
        mine = jnp.stack([lax.ppermute(piece, "mp", perm) for perm in rotations])
        half = piece.shape[0] // 2
        by_x, by_y = flip(mine, 2), flip(mine, 4)
        first, second = flip(by_y[:, :half], 2), flip(by_x[:, half:], 4)
        mine = jnp.stack([mine, by_x, by_y, jnp.concatenate([first, second], axis=1)])
        return mine, flip(mine, 1)

    def sum_over_dp(values, index):
        def part(array, bit_set):
            size = array.shape[0] // 2
            return lax.dynamic_slice_in_dim(array, bit_set * size, size, 0)

        bit = lambda b: jnp.where((index & b) != 0, 1, 0)

        def scatter(array, b):
            return part(array, bit(b)) + flip(part(array, 1 - bit(b)), b)

        def collect(array, b):
            other = flip(array, b)
            low = jnp.where(bit(b) == 0, array, other)
            high = jnp.where(bit(b) == 0, other, array)
            return jnp.concatenate([low, high], axis=0)

        chip = scatter(values, 1)
        half = chip.shape[0] // 2
        first, second = chip[:half], chip[half:]
        first, second = scatter(first, 2), scatter(second, 4)
        first, second = scatter(first, 4), scatter(second, 2)
        step = GROUP
        while step < lanes:
            first = first + flip(first, step)
            second = second + flip(second, step)
            step *= 2
        first, second = collect(first, 4), collect(second, 2)
        first, second = collect(first, 2), collect(second, 4)
        return collect(jnp.concatenate([first, second], axis=0), 1)

    def local(
        tokens,
        doc_lengths,
        w_query,
        b_query,
        w_key,
        w_value,
        b_value,
        w_output,
        b_output,
        gain_attn,
        shift_attn,
        w_expand,
        b_expand,
        w_reduce,
        b_reduce,
        gain_ffn,
        shift_ffn,
        cotangent,
    ):
        row_count, length, width = tokens.shape
        heads = w_query.shape[1] // HD
        count = row_count * length
        inputs = tokens.reshape(count, width)
        cot = cotangent.reshape(count, width)
        index = lax.axis_index("dp")
        me = lax.axis_index("mp")
        inside = index % GROUP
        place = jnp.stack(
            [inside ^ flipped for rel in (0, 2, 4, 6) for flipped in (rel, rel ^ 1)] + [me]
        ).astype(jnp.int32)

        by_head = lambda w: w.T.reshape(heads, HD, width)
        own_heads = jnp.concatenate(
            [by_head(w_query), by_head(w_key), by_head(w_value), w_output.reshape(heads, HD, width)],
            axis=1,
        )
        blank = jnp.zeros((width - 2 * heads * HD,), BF16)
        own_bias = jnp.stack(
            [jnp.concatenate([b_query, b_value, blank]), b_expand]
            + [jnp.zeros((width,), BF16)] * 6
        ).astype(F32)

        def piece_of(array):
            size = array.shape[0] // GROUP
            return lax.dynamic_slice_in_dim(array, inside * size, size, 0).astype(F32)

        peer_bias = [lax.ppermute(own_bias, "mp", perm) for perm in rotations]
        gathered = [gather(piece_of(own_heads[j])) for j in range(heads)]
        gathered_expand = gather(piece_of(w_expand))
        gathered_reduce = gather(piece_of(w_reduce))

        biases = jnp.stack([own_bias] + peer_bias)
        parts = biases[:, 0, : 2 * heads * HD].reshape(peers, 2, heads, HD)
        columns = jnp.concatenate(
            [parts[:, 0], jnp.zeros((peers, heads, HD), F32), parts[:, 1]], axis=-1
        )[..., None]

        ends = jnp.cumsum(doc_lengths, axis=-1)
        position = jnp.arange(length, dtype=jnp.int32)
        segment = jnp.sum((position[None, :, None] >= ends[:, None, :]).astype(jnp.int32), axis=-1)
        segment = segment.reshape(1, count)
        docs = doc_lengths.shape[1]
        label = jnp.arange(EXTRA, dtype=jnp.int32)[:, None]
        is_doc = label < docs
        qf = jnp.where(is_doc & (segment == label), 1.0, 0.0).astype(BF16)
        kf = jnp.where(
            is_doc,
            jnp.where(segment == label, 0.0, MASK),
            jnp.where(label < docs + 3, 1.0, 0.0),
        ).astype(BF16)

        forward = [attend_forward(length, inputs, own_heads, columns[0], qf, kf)]
        weight_sets = [own_heads]
        for j in range(heads):
            weights = assemble_small(place, *gathered[j])
            weight_sets.append(weights)
            forward.append(attend_forward(length, inputs, weights, columns[1:, j], qf, kf))
        all_expand = assemble_big(place, w_expand, *gathered_expand)
        all_reduce = assemble_big(place, w_reduce, *gathered_reduce)

        vectors = jnp.stack(
            [b_output, gain_attn, shift_attn, b_reduce, gain_ffn, shift_ffn]
            + [jnp.zeros((width,), BF16)] * 2
        ).astype(F32)
        results = dense(
            place,
            inputs,
            cot,
            [f[1] for f in forward],
            weight_sets,
            all_expand,
            all_reduce,
            biases,
            vectors,
        )
        output, grad_one = results[0], results[1]
        dctx = results[2 : 3 + heads]
        dwe, dwr, dwo, small = results[3 + heads :]

        first = jnp.concatenate([dwe, dwr, dwo.reshape(heads * HD, width), small], axis=0)
        first = jnp.pad(first, ((0, -first.shape[0] % 128), (0, 0)))
        first = sum_over_dp(first, inside)

        backward = [attend_backward(length, *forward[0], dctx[0], kf)]
        own_dw, own_sum = own_grads(backward[0], inputs)
        second = own_dw.reshape(heads * 3 * HD, width)
        bias_row = own_sum[:, :, 0].reshape(1, heads * 3 * HD)
        bias_row = jnp.pad(bias_row, ((0, 7), (0, width - heads * 3 * HD)))
        second = jnp.concatenate([second, bias_row], axis=0)
        second = jnp.pad(second, ((0, -second.shape[0] % 128), (0, 0)))
        second = sum_over_dp(second, inside)

        for j in range(heads):
            backward.append(attend_backward(length, *forward[j + 1], dctx[j + 1], kf))
        grad_tokens = input_grads(place, grad_one, backward, weight_sets)

        hidden = w_expand.shape[1]
        edge = width + hidden
        dwe, dwr = first[:width], first[width:edge]
        dwo, small = first[edge : edge + heads * HD], first[edge + heads * HD :]
        dqkv = second[: heads * 3 * HD].reshape(heads, 3, HD, width)
        dbias = second[heads * 3 * HD, : heads * 3 * HD].reshape(heads, 3, HD)
        turned = lambda i: dqkv[:, i].reshape(heads * HD, width).T
        flat = lambda i: dbias[:, i].reshape(heads * HD)
        shape = (row_count, length, width)
        return (
            output.reshape(shape),
            grad_tokens.reshape(shape),
            turned(0),
            flat(0),
            turned(1),
            turned(2),
            flat(2),
            dwo,
            small[0],
            small[1],
            small[2],
            dwe,
            small[6],
            dwr,
            small[3],
            small[4],
            small[5],
        )

    rows, split = P("dp", None, None), P(None, "mp")
    return jax.shard_map(
        local,
        mesh=mesh,
        in_specs=(
            rows,
            P("dp", None),
            split,
            P("mp"),
            split,
            split,
            P("mp"),
            P("mp", None),
            P(),
            P(),
            P(),
            split,
            P("mp"),
            P("mp", None),
            P(),
            P(),
            P(),
            rows,
        ),
        out_specs=(
            rows,
            rows,
            split,
            P("mp"),
            split,
            split,
            P("mp"),
            P("mp", None),
            P(),
            P(),
            P(),
            split,
            P("mp"),
            P("mp", None),
            P(),
            P(),
            P(),
        ),
        check_vma=False,
    )
```

```python
import jax
import jax.numpy as jnp
from jax import lax
from jax.experimental import pallas as pl
from jax.experimental.pallas import tpu as pltpu
from jax.sharding import PartitionSpec as P

HD = 64
GROUP = 8
EXTRA = 16
MASK = -float(2**30)
EPS = 1e-12
F32 = jnp.float32
BF16 = jnp.bfloat16
LIMIT = 60 << 20


def dot(left, right, left_dim, right_dim):
    return lax.dot_general(
        left, right, (((left_dim,), (right_dim,)), ((), ())), preferred_element_type=F32
    )


def params():
    return pltpu.CompilerParams(vmem_limit_bytes=LIMIT)


def cost(flops, moved):
    return pl.CostEstimate(flops=int(flops), bytes_accessed=int(moved), transcendentals=0)


def whole(shape):
    zeros = (0,) * len(shape)
    return pl.BlockSpec(shape, lambda *_: zeros, pipeline_mode=pl.Buffered(1))


def split3(row):
    high = row.astype(BF16).astype(F32)
    rest = row - high
    mid = rest.astype(BF16).astype(F32)
    return high, mid, rest - mid


def rows_of(height, first, parts, width):
    place = lax.broadcasted_iota(jnp.int32, (height, width), 0)
    out = jnp.zeros((height, width), F32)
    for i, part in enumerate(parts):
        out = jnp.where(place == first + i, part, out)
    return out


def put_pieces(place_ref, pieces, out_ref, lead, width, take):
    for ref, index, offset in pieces:
        values = take(ref)
        start = pl.multiple_of(place_ref[index] * width + offset, 16)
        out_ref[lead, pl.ds(start, values.shape[0]), :] = values.astype(BF16)


def attend_forward_kernel(length, spots, place_ref, x_ref, bias_ref, qf_ref, kf_ref, *refs):
    weights, outs = refs[:-3], refs[-3:]
    tokens = x_ref.shape[0]
    if spots is None:
        w_ref = weights[0]
    else:
        w_ref, weights = weights[-1], weights[:-1]
        pieces = [(ref, index, offset) for ref, (index, offset) in zip(weights, spots)]
        put_pieces(place_ref, pieces, w_ref, 0, w_ref.shape[1] // GROUP, lambda ref: ref[0, 0])
    qkv_ref, ctx_ref, aug_ref = outs
    proj = dot(w_ref[0, : 3 * HD, :], x_ref[...], 1, 1) + bias_ref[0]
    scale = HD ** (-0.5)
    qkv_ref[0, :HD, :] = (proj[:HD] * scale).astype(BF16)
    qkv_ref[0, HD:, :] = proj[HD:].astype(BF16)
    ones_rows = rows_of(EXTRA, 0, (jnp.ones((1, length), F32),), length).astype(BF16)

    def row(r, carry):
        at = pl.ds(pl.multiple_of(r * length, length), length)
        queries = jnp.concatenate([qkv_ref[0, :HD, at], qf_ref[:, at]], axis=0)
        keys = jnp.concatenate([qkv_ref[0, HD : 2 * HD, at], kf_ref[:, at]], axis=0)
        values = jnp.concatenate([qkv_ref[0, 2 * HD :, at], ones_rows], axis=0)
        scores = dot(keys, queries, 0, 0)
        highest = jnp.max(scores, axis=0, keepdims=True)
        weight = jnp.exp(scores - highest).astype(BF16)
        context = dot(values, weight, 1, 0)
        total = context[HD : HD + 1]
        ctx_ref[0, :, at] = (context[:HD] * (1.0 / total)).astype(BF16)
        log_total = highest + jnp.log(total)
        extra = rows_of(EXTRA, 4, split3(-log_total), length)
        aug_ref[0, :, at] = (extra + qf_ref[:, at].astype(F32)).astype(BF16)
        return carry

    lax.fori_loop(0, tokens // length, row, 0, unroll=2)


def attend_forward(length, place, inputs, bias, qf, kf, own=None, pieces=None, slot=0):
    heads = bias.shape[0]
    tokens, width = inputs.shape
    height = 4 * HD
    by_head = lambda *shape: pl.BlockSpec((1,) + shape, lambda h, *_: (h, 0, 0))
    out_specs = [by_head(3 * HD, tokens), by_head(HD, tokens), by_head(EXTRA, tokens)]
    out_shape = [
        jax.ShapeDtypeStruct((heads, rows, tokens), BF16) for rows in (3 * HD, HD, EXTRA)
    ]
    if pieces is None:
        spots, arrays, specs = None, [own], [by_head(height, width)]
    else:
        spots = [(index, offset) for _, index, offset in pieces]
        arrays = [array for array, _, _ in pieces]
        specs = [
            pl.BlockSpec((1, 1) + a.shape[2:], lambda h, *_: (h, slot, 0, 0)) for a in arrays
        ]
        out_specs = [by_head(height, width)] + out_specs
        out_shape = [jax.ShapeDtypeStruct((heads, height, width), BF16)] + out_shape
    return pl.pallas_call(
        lambda *refs: attend_forward_kernel(length, spots, *refs),
        grid_spec=pltpu.PrefetchScalarGridSpec(
            num_scalar_prefetch=1,
            grid=(heads,),
            in_specs=[
                whole(inputs.shape),
                by_head(3 * HD, 1),
                whole(qf.shape),
                whole(kf.shape),
                *specs,
            ],
            out_specs=out_specs,
        ),
        out_shape=out_shape,
        compiler_params=params(),
        cost_estimate=cost(heads * tokens * (6 * HD * width + 16 * 64 * length), 12e6),
        name="attend_forward",
    )(place, inputs, bias, qf, kf, *arrays)


def attend_backward_kernel(length, qkv_ref, ctx_ref, aug_ref, grad_ref, kf_ref, out_ref):
    tokens = kf_ref.shape[1]
    scale = HD ** (-0.5)
    one = jnp.ones((1, length), F32)
    ones_rows = rows_of(EXTRA, 0, (one, one, one), length).astype(BF16)

    def row(r, carry):
        at = pl.ds(pl.multiple_of(r * length, length), length)
        queries = qkv_ref[0, :HD, at]
        keys = qkv_ref[0, HD : 2 * HD, at]
        values = qkv_ref[0, 2 * HD :, at]
        grad_context = grad_ref[0, :, at]
        inner = jnp.sum(
            grad_context.astype(F32) * ctx_ref[0, :, at].astype(F32), axis=0, keepdims=True
        )
        grad_extra = rows_of(EXTRA, 0, split3(-inner), length).astype(BF16)
        scores = dot(
            jnp.concatenate([keys, kf_ref[:, at]], axis=0),
            jnp.concatenate([queries, aug_ref[0, :, at]], axis=0),
            0,
            0,
        )
        probs = jnp.exp(scores)
        spread = dot(
            jnp.concatenate([values, ones_rows], axis=0),
            jnp.concatenate([grad_context, grad_extra], axis=0),
            0,
            0,
        )
        grad_scores = (probs * spread).astype(BF16)
        out_ref[0, 2 * HD :, at] = dot(grad_context, probs.astype(BF16), 1, 1).astype(BF16)
        out_ref[0, HD : 2 * HD, at] = dot(queries, grad_scores, 1, 1).astype(BF16)
        out_ref[0, :HD, at] = (dot(keys, grad_scores, 1, 0) * scale).astype(BF16)
        return carry

    lax.fori_loop(0, tokens // length, row, 0, unroll=2)


def attend_backward(length, qkv, ctx, aug, grad, kf):
    heads, _, tokens = qkv.shape
    by_head = lambda *shape: pl.BlockSpec((1,) + shape, lambda h: (h, 0, 0))
    return pl.pallas_call(
        lambda *refs: attend_backward_kernel(length, *refs),
        grid=(heads,),
        in_specs=[
            by_head(3 * HD, tokens),
            by_head(HD, tokens),
            by_head(EXTRA, tokens),
            by_head(HD, tokens),
            whole(kf.shape),
        ],
        out_specs=by_head(3 * HD, tokens),
        out_shape=jax.ShapeDtypeStruct((heads, 3 * HD, tokens), BF16),
        compiler_params=params(),
        cost_estimate=cost(heads * tokens * 40 * 64 * length, 12e6),
        name="attend_backward",
    )(qkv, ctx, aug, grad, kf)


def norm_forward(hidden):
    center = hidden - jnp.mean(hidden, axis=-1, keepdims=True)
    inverse = lax.rsqrt(jnp.mean(center * center, axis=-1, keepdims=True) + EPS)
    return center * inverse, inverse


def norm_backward(grad, gain, norm, inverse):
    scaled = grad * gain
    first = jnp.mean(scaled, axis=-1, keepdims=True)
    second = jnp.mean(scaled * norm, axis=-1, keepdims=True)
    return (scaled - first - norm * second) * inverse


def column_sum(values):
    return jnp.sum(values, axis=0, keepdims=True)


def head_start(place_ref, shards, k, j, heads, height):
    shard = lax.rem(place_ref[GROUP] + shards - k, shards)
    return pl.multiple_of((shard * heads + j) * height, HD)


def gather_heads(place_ref, shards, heads, sets, refs, out_ref, height):
    for members, ref in zip(sets, refs):
        for i, (k, j) in enumerate(members):
            start = head_start(place_ref, shards, k, j, heads, height)
            out_ref[pl.ds(start, height), :] = ref[i, :height, :]


def fill_shards(place_ref, own_ref, refs, spots, out_ref):
    shards, height, _ = out_ref.shape
    out_ref[place_ref[GROUP]] = own_ref[...]
    for k in range(1, shards):
        shard = lax.rem(place_ref[GROUP] + shards - k, shards)
        pieces = [(ref, index, offset) for ref, (index, offset) in zip(refs, spots)]
        put_pieces(place_ref, pieces, out_ref, shard, height // GROUP, lambda ref: ref[k - 1])


def expand_kernel(sets, heads, shards, place_ref, x_ref, *refs):
    refs = list(refs)
    take = lambda count: [refs.pop(0) for _ in range(count)]
    ctx_refs, wo_refs = take(len(sets)), take(len(sets))
    bias_ref, vec_ref, full_ref = take(3)
    sum_ref, act_ref, slope_ref, we_ref, wo_ref, ctx_scr = refs

    @pl.when(pl.program_id(0) == 0)
    def _():
        gather_heads(place_ref, shards, heads, sets, wo_refs, wo_ref, HD)
        for s in range(shards):
            we_ref[s] = full_ref[s].astype(BF16)

    gather_heads(place_ref, shards, heads, sets, ctx_refs, ctx_scr, HD)
    b_output, gain_one, shift_one = vec_ref[0:1], vec_ref[1:2], vec_ref[2:3]
    attended = dot(ctx_scr[...], wo_ref[...], 0, 0) + b_output
    residual = x_ref[...].astype(F32) + attended
    sum_ref[...] = residual
    norm_one, _ = norm_forward(residual)
    normed_low = (norm_one * gain_one + shift_one).astype(BF16)
    for s in range(shards):
        b_expand = bias_ref[lax.rem(place_ref[GROUP] + shards - s, shards), 1:2]
        hidden = dot(normed_low, we_ref[s], 1, 0) + b_expand
        square = hidden * hidden
        bent = jnp.tanh(hidden * (0.7978845608028654 + 0.035677408136300125 * square))
        gate = 0.5 + 0.5 * bent
        active = hidden * gate
        act_ref[s] = active.astype(BF16)
        slope = gate + (active * (1.0 - gate)) * (1.5957691216057308 + 0.21406444881780075 * square)
        slope_ref[s] = slope.astype(BF16)


def expand(place, inputs, sets, ctx_sets, weight_sets, biases, vectors, full):
    tokens, width = inputs.shape
    shards, _, hidden = full.shape
    heads = sum(len(s) for s in sets) // shards
    block = 256
    by_token = lambda: pl.BlockSpec((block, width), lambda i, *_: (i, 0))
    by_shard = lambda: pl.BlockSpec((shards, block, hidden), lambda i, *_: (0, i, 0))
    features = shards * heads * HD
    return pl.pallas_call(
        lambda *refs: expand_kernel(sets, heads, shards, *refs),
        grid_spec=pltpu.PrefetchScalarGridSpec(
            num_scalar_prefetch=1,
            grid=(tokens // block,),
            in_specs=[
                by_token(),
                *[
                    pl.BlockSpec((a.shape[0], HD, block), lambda i, *_: (0, 0, i))
                    for a in ctx_sets
                ],
                *[
                    pl.BlockSpec(
                        (a.shape[0], HD, width),
                        lambda i, *_: (0, 3, 0),
                        pipeline_mode=pl.Buffered(1),
                    )
                    for a in weight_sets
                ],
                whole(biases.shape),
                whole(vectors.shape),
                whole(full.shape),
            ],
            out_specs=[
                by_token(),
                by_shard(),
                by_shard(),
                whole((shards, width, hidden)),
                whole((features, width)),
            ],
            scratch_shapes=[pltpu.VMEM((features, block), BF16)],
        ),
        out_shape=[
            jax.ShapeDtypeStruct((tokens, width), F32),
            jax.ShapeDtypeStruct((shards, tokens, hidden), BF16),
            jax.ShapeDtypeStruct((shards, tokens, hidden), BF16),
            jax.ShapeDtypeStruct((shards, width, hidden), BF16),
            jax.ShapeDtypeStruct((features, width), BF16),
        ],
        compiler_params=params(),
        cost_estimate=cost(2 * tokens * width * (shards * hidden + features), 40e6),
        name="expand",
    )(place, inputs, *ctx_sets, *weight_sets, biases, vectors, full)


def reduce_kernel(sets, spots, heads, place_ref, sum_ref, cot_ref, act_ref, slope_ref, *refs):
    refs = list(refs)
    take = lambda count: [refs.pop(0) for _ in range(count)]
    ctx_ref, we_ref, wo_ref, vec_ref, own_ref = take(5)
    piece_refs = take(len(spots))
    out_ref, g1_ref = take(2)
    dctx_refs = take(len(sets))
    mine_ref, send_ref = take(2)
    wr_scr, dwe_scr, dwr_scr, dwo_scr, small_scr, gh_scr, dctx_scr = refs
    step = pl.program_id(0)
    shards = we_ref.shape[0]
    me = place_ref[GROUP]

    @pl.when(step == 0)
    def _():
        fill_shards(place_ref, own_ref, piece_refs, spots, wr_scr)
        for scr in (dwe_scr, dwr_scr, dwo_scr, small_scr):
            scr[...] = jnp.zeros_like(scr)

    gain_one, shift_one = vec_ref[1:2], vec_ref[2:3]
    b_reduce, gain_two, shift_two = vec_ref[3:4], vec_ref[4:5], vec_ref[5:6]
    norm_one, inverse_one = norm_forward(sum_ref[...])
    normed = norm_one * gain_one + shift_one
    normed_low = normed.astype(BF16)
    mixed = dot(act_ref[0], wr_scr[0], 1, 0)
    for s in range(1, shards):
        mixed = mixed + dot(act_ref[s], wr_scr[s], 1, 0)
    norm_two, inverse_two = norm_forward(normed + (mixed + b_reduce))
    out_ref[...] = (norm_two * gain_two + shift_two).astype(BF16)

    cot = cot_ref[...].astype(F32)
    grad_two = norm_backward(cot, gain_two, norm_two, inverse_two)
    grad_two_low = grad_two.astype(BF16)
    grad_normed = grad_two
    for s in range(shards):
        grad_active = dot(grad_two_low, wr_scr[s], 1, 1)
        grad_hidden = (grad_active * slope_ref[s].astype(F32)).astype(BF16)
        gh_scr[s] = grad_hidden
        grad_normed = grad_normed + dot(grad_hidden, we_ref[s], 1, 1)

    own = gh_scr[me]
    dwr_scr[...] += dot(act_ref[me], grad_two_low, 0, 0)
    dwe_scr[...] += dot(normed_low, own, 0, 0)

    grad_one = norm_backward(grad_normed, gain_one, norm_one, inverse_one)
    grad_one_low = grad_one.astype(BF16)
    g1_ref[...] = grad_one
    for j in range(heads):
        dwo_scr[j * HD : (j + 1) * HD] += dot(ctx_ref[j], grad_one_low, 1, 0)
    dctx_scr[...] = dot(wo_ref[...], grad_one_low, 1, 1).astype(BF16)
    for members, ref in zip(sets, dctx_refs):
        for i, (k, j) in enumerate(members):
            ref[i] = dctx_scr[pl.ds(head_start(place_ref, shards, k, j, heads, HD), HD), :]

    small_scr[0:1] += column_sum(grad_one)
    small_scr[1:2] += column_sum(grad_normed * norm_one)
    small_scr[2:3] += column_sum(grad_normed)
    small_scr[3:4] += column_sum(grad_two)
    small_scr[4:5] += column_sum(cot * norm_two)
    small_scr[5:6] += column_sum(cot)
    small_scr[6:7] += column_sum(own.astype(F32))

    @pl.when(step == pl.num_programs(0) - 1)
    def _():
        for rel in range(4):
            for source, ref in enumerate((mine_ref, send_ref)):
                owner = place_ref[2 * rel + source]
                top = 0
                for scr in (dwe_scr, dwr_scr, dwo_scr):
                    size = scr.shape[0] // GROUP
                    start = pl.multiple_of(owner * size, 8)
                    ref[rel, top : top + size, :] = scr[pl.ds(start, size), :]
                    top += size
                ref[rel, top:, :] = jnp.where(owner == 0, small_scr[...], 0.0)


def reduce(place, residual, cot, act, slope, sets, ctx, w_expand, w_output, vectors, own, pieces):
    tokens, width = residual.shape
    shards, _, hidden = act.shape
    heads = sum(len(s) for s in sets) // shards
    block = 256
    spots = [(index, offset) for _, index, offset in pieces]
    arrays = [array for array, _, _ in pieces]
    by_token = lambda: pl.BlockSpec((block, width), lambda i, *_: (i, 0))
    by_shard = lambda: pl.BlockSpec((shards, block, hidden), lambda i, *_: (0, i, 0))
    columns = lambda count: pl.BlockSpec((count, HD, block), lambda i, *_: (0, 0, i))
    share = (width + hidden + heads * HD) // GROUP + 8
    flops = tokens * width * (6 * shards * hidden + 4 * hidden + 2 * width + 2 * heads * HD)
    return pl.pallas_call(
        lambda *refs: reduce_kernel(sets, spots, heads, *refs),
        grid_spec=pltpu.PrefetchScalarGridSpec(
            num_scalar_prefetch=1,
            grid=(tokens // block,),
            in_specs=[
                by_token(),
                by_token(),
                by_shard(),
                by_shard(),
                columns(heads),
                whole(w_expand.shape),
                whole(w_output.shape),
                whole(vectors.shape),
                whole(own.shape),
                *[whole(a.shape) for a in arrays],
            ],
            out_specs=[
                by_token(),
                by_token(),
                *[columns(len(s)) for s in sets],
                whole((4, share, width)),
                whole((4, share, width)),
            ],
            scratch_shapes=[
                pltpu.VMEM((shards, hidden, width), BF16),
                pltpu.VMEM((width, hidden), F32),
                pltpu.VMEM((hidden, width), F32),
                pltpu.VMEM((heads * HD, width), F32),
                pltpu.VMEM((8, width), F32),
                pltpu.VMEM((shards, block, hidden), BF16),
                pltpu.VMEM((shards * heads * HD, block), BF16),
            ],
        ),
        out_shape=[
            jax.ShapeDtypeStruct((tokens, width), BF16),
            jax.ShapeDtypeStruct((tokens, width), F32),
            *[jax.ShapeDtypeStruct((len(s), HD, tokens), BF16) for s in sets],
            jax.ShapeDtypeStruct((4, share, width), F32),
            jax.ShapeDtypeStruct((4, share, width), F32),
        ],
        compiler_params=params(),
        cost_estimate=cost(flops, 60e6),
        name="reduce",
    )(place, residual, cot, act, slope, ctx, w_expand, w_output, vectors, own, *arrays)


def own_grads_kernel(place_ref, dqkv_ref, x_ref, mine_ref, send_ref, grad_scr):
    heads = dqkv_ref.shape[0]
    height = heads * HD
    ones = jnp.ones((8, x_ref.shape[0]), BF16)
    row = lax.broadcasted_iota(jnp.int32, (8, 3 * HD), 0)
    sums = jnp.zeros((8, 3 * HD), F32)
    for j in range(heads):
        grad = dot(dqkv_ref[j], x_ref[...], 1, 0)
        for i in range(3):
            grad_scr[i * height + j * HD : i * height + (j + 1) * HD, :] = grad[i * HD : (i + 1) * HD]
        sums = jnp.where(row == j, dot(ones, dqkv_ref[j], 1, 1), sums)
    size = 3 * height // GROUP
    for rel in range(4):
        for source, ref in enumerate((mine_ref, send_ref)):
            owner = place_ref[2 * rel + source]
            ref[rel, :size, :] = grad_scr[pl.ds(pl.multiple_of(owner * size, 8), size), :]
            ref[rel, size:, :] = jnp.zeros((8, x_ref.shape[1]), F32)
            ref[rel, size:, : 3 * HD] = jnp.where(owner == 0, sums, 0.0)


def own_grads(place, dqkv, inputs):
    heads, height, tokens = dqkv.shape
    width = inputs.shape[1]
    share = heads * height // GROUP + 8
    return pl.pallas_call(
        own_grads_kernel,
        grid_spec=pltpu.PrefetchScalarGridSpec(
            num_scalar_prefetch=1,
            grid=(1,),
            in_specs=[whole(dqkv.shape), whole(inputs.shape)],
            out_specs=[whole((4, share, width)), whole((4, share, width))],
            scratch_shapes=[pltpu.VMEM((heads * height, width), F32)],
        ),
        out_shape=[jax.ShapeDtypeStruct((4, share, width), F32)] * 2,
        compiler_params=params(),
        cost_estimate=cost(2 * heads * height * tokens * width, 8e6),
        name="own_grads",
    )(place, dqkv, inputs)


def spread_kernel(sizes, place_ref, *refs):
    parts, outs = refs[:GROUP], refs[GROUP:]
    for i, ref in enumerate(parts):
        owner = place_ref[i]
        top = 0
        for size, out_ref in zip(sizes, outs):
            out_ref[pl.ds(pl.multiple_of(owner * size, 8), size), :] = ref[top : top + size, :]
            top += size

        @pl.when(owner == 0)
        def _():
            outs[-1][...] = ref[top:, :]


def spread(place, parts, sizes):
    width = parts[0].shape[1]
    shapes = [(GROUP * size, width) for size in sizes] + [(8, width)]
    return pl.pallas_call(
        lambda *refs: spread_kernel(sizes, *refs),
        grid_spec=pltpu.PrefetchScalarGridSpec(
            num_scalar_prefetch=1,
            grid=(1,),
            in_specs=[whole(a.shape) for a in parts],
            out_specs=[whole(s) for s in shapes],
        ),
        out_shape=[jax.ShapeDtypeStruct(s, F32) for s in shapes],
        compiler_params=params(),
        cost_estimate=cost(0, 8 * parts[0].size * 8),
        name="spread",
    )(place, *parts)


def input_grads_kernel(sets, heads, shards, place_ref, g1_ref, *refs):
    count = len(sets)
    grads, weights = refs[:count], refs[count : 2 * count]
    out_ref, grad_scr, w_scr = refs[2 * count :]
    height = 3 * HD

    @pl.when(pl.program_id(0) == 0)
    def _():
        gather_heads(place_ref, shards, heads, sets, weights, w_scr, height)

    gather_heads(place_ref, shards, heads, sets, grads, grad_scr, height)
    out_ref[...] = (g1_ref[...] + dot(grad_scr[...], w_scr[...], 0, 0)).astype(BF16)


def input_grads(place, grad_one, sets, grad_sets, weight_sets, shards):
    tokens, width = grad_one.shape
    block = 256
    heads = sum(len(s) for s in sets) // shards
    count = shards * heads * 3 * HD
    by_token = lambda: pl.BlockSpec((block, width), lambda i, *_: (i, 0))
    return pl.pallas_call(
        lambda *refs: input_grads_kernel(sets, heads, shards, *refs),
        grid_spec=pltpu.PrefetchScalarGridSpec(
            num_scalar_prefetch=1,
            grid=(tokens // block,),
            in_specs=[
                by_token(),
                *[
                    pl.BlockSpec((a.shape[0], 3 * HD, block), lambda i, *_: (0, 0, i))
                    for a in grad_sets
                ],
                *[whole(a.shape) for a in weight_sets],
            ],
            out_specs=by_token(),
            scratch_shapes=[pltpu.VMEM((count, block), BF16), pltpu.VMEM((count, width), BF16)],
        ),
        out_shape=jax.ShapeDtypeStruct((tokens, width), BF16),
        compiler_params=params(),
        cost_estimate=cost(2 * tokens * width * count, 20e6),
        name="input_grads",
    )(place, grad_one, *grad_sets, *weight_sets)


def after(values, *others):
    return lax.optimization_barrier((values, others))[0]


def solution(mesh):
    peers = mesh.shape["mp"]
    lanes = mesh.shape["dp"]
    rotations = [[(i, (i + k) % peers) for i in range(peers)] for k in range(1, peers)]

    def flip(values, bits):
        return lax.ppermute(values, "dp", [(i, i ^ bits) for i in range(lanes)])

    def from_peers(piece):
        return jnp.stack([lax.ppermute(piece, "mp", perm) for perm in rotations])

    def swapped(piece):
        copies = jnp.broadcast_to(piece[None], (peers,) + piece.shape)
        got = lax.all_to_all(copies, "mp", 0, 0, tiled=True)
        me = lax.axis_index("mp")
        return jnp.concatenate(
            [
                lax.dynamic_slice_in_dim(got, lax.rem(me + peers - k, peers), 1, 0)
                for k in range(1, peers)
            ]
        )

    def with_core(pieces):
        out = []
        for array, rel, offset in pieces:
            out.append((array, 2 * rel, offset))
            out.append((flip(array, 1), 2 * rel + 1, offset))
        return out

    def scatter(mine, got, *ready):
        got = after(got, *ready)
        parts = [mine[rel] + got[rel] for rel in range(4)]
        return parts[0], [flip(parts[rel], 2 * rel) for rel in (1, 2, 3)]

    def collect(first, rest, *ready):
        rest = after(rest, *ready)
        total = first + rest[0] + rest[1] + rest[2]
        step = GROUP
        while step < lanes:
            total = total + flip(total, step)
            step *= 2
        return [total] + [flip(total, bits) for bits in (2, 4, 6)]

    def finish(arrays, *ready):
        out = []
        for array in after(arrays, *ready):
            out += [array, flip(array, 1)]
        return out

    def local(
        tokens,
        doc_lengths,
        w_query,
        b_query,
        w_key,
        w_value,
        b_value,
        w_output,
        b_output,
        gain_attn,
        shift_attn,
        w_expand,
        b_expand,
        w_reduce,
        b_reduce,
        gain_ffn,
        shift_ffn,
        cotangent,
    ):
        row_count, length, width = tokens.shape
        heads = w_query.shape[1] // HD
        hidden = w_expand.shape[1]
        count = row_count * length
        inputs = tokens.reshape(count, width)
        cot = cotangent.reshape(count, width)
        inside = lax.axis_index("dp") % GROUP
        me = lax.axis_index("mp")
        place = jnp.stack([inside ^ i for i in range(GROUP)] + [me]).astype(jnp.int32)
        sets = [[(0, j) for j in range(heads)]]
        sets += [[(k, j) for k in range(1, peers)] for j in range(heads)]

        by_head = lambda w: w.T.reshape(heads, HD, width)
        own_heads = jnp.concatenate(
            [by_head(w_query), by_head(w_key), by_head(w_value), w_output.reshape(heads, HD, width)],
            axis=1,
        )
        blank = jnp.zeros((width - 2 * heads * HD,), BF16)
        own_bias = jnp.stack(
            [jnp.concatenate([b_query, b_value, blank]), b_expand]
            + [jnp.zeros((width,), BF16)] * 6
        ).astype(F32)

        def piece_of(array, which=0, axis=0):
            size = array.shape[axis] // GROUP
            start = (inside ^ which) * size
            return lax.dynamic_slice_in_dim(array, start, size, axis).astype(F32)

        def both(near):
            return flip(near, 2), flip(near, 4)

        def corner(by_x, by_y, axis):
            half = by_x.shape[axis] // 2
            first = flip(lax.slice_in_dim(by_y, 0, half, axis=axis), 2)
            second = flip(lax.slice_in_dim(by_x, half, 2 * half, axis=axis), 4)
            return first, second

        def listed(near, by_x, by_y, first, second, axis):
            half = first.shape[axis]
            return with_core(
                [(near, 0, 0), (by_x, 1, 0), (by_y, 2, 0), (first, 3, 0), (second, 3, half)]
            )

        early = piece_of(own_heads[:1], axis=1)
        near = from_peers(jnp.concatenate([early[0], own_bias]))
        near_early, biases = near[:, None, : early.shape[1]], near[:, early.shape[1] :]
        near_late = swapped(after(piece_of(own_heads[1:], axis=1), near))
        start = lax.axis_index("dp") * (width // lanes)
        share = lax.dynamic_slice_in_dim(w_expand, start, width // lanes, 0).astype(F32)
        all_expand = lax.all_gather(after(share, near), ("mp", "dp")).reshape(peers, width, hidden)

        def columns(rows):
            parts = rows[:, 0, : 2 * heads * HD].reshape(-1, 2, heads, HD)
            blank = jnp.zeros((rows.shape[0], heads, HD), F32)
            return jnp.concatenate([parts[:, 0], blank, parts[:, 1]], axis=-1)[..., None]

        own_columns, peer_columns = columns(own_bias[None]), columns(biases)
        biases = jnp.concatenate([own_bias[None], biases])

        ends = jnp.cumsum(doc_lengths, axis=-1)
        position = jnp.arange(length, dtype=jnp.int32)
        segment = jnp.sum((position[None, :, None] >= ends[:, None, :]).astype(jnp.int32), axis=-1)
        segment = segment.reshape(1, count)
        docs = doc_lengths.shape[1]
        label = jnp.arange(EXTRA, dtype=jnp.int32)[:, None]
        is_doc = label < docs
        qf = jnp.where(is_doc & (segment == label), 1.0, 0.0).astype(BF16)
        kf = jnp.where(
            is_doc,
            jnp.where(segment == label, 0.0, MASK),
            jnp.where(label < docs + 3, 1.0, 0.0),
        ).astype(BF16)

        attend = lambda bias, **w: attend_forward(length, place, inputs, bias, qf, kf, **w)
        ready = [(near_early, 0, 0)]
        ready += [(flip(near_early, 2 * rel), rel, 0) for rel in (1, 2, 3)]
        saved = [None]
        weight_sets = [own_heads]
        weights, *kept = attend(peer_columns[:, 0], pieces=with_core(ready))
        saved.append(kept)
        weight_sets.append(weights)
        sides_late = both(after(near_late, kept))
        near_reduce = swapped(after(piece_of(w_reduce), kept, near_late))
        saved[0] = own = attend(after(own_columns[0], kept, near_late), own=own_heads)
        sides_late = after(sides_late, own)
        corner_late = corner(*sides_late, 2)
        pieces_late = listed(near_late, *sides_late, *corner_late, 2)

        weights, *kept = attend(peer_columns[:, 1], pieces=pieces_late, slot=0)
        saved.append(kept)
        weight_sets.append(weights)
        near_reduce = after(near_reduce, kept)
        sides_reduce = both(near_reduce)
        weights, *kept = attend(
            after(peer_columns[:, 2], near_reduce), pieces=pieces_late, slot=1
        )
        saved.append(kept)
        weight_sets.append(weights)
        sides_reduce = after(sides_reduce, kept)
        corner_reduce = corner(*sides_reduce, 1)
        pieces_reduce = listed(near_reduce, *sides_reduce, *corner_reduce, 1)
        biases = after(biases, sides_reduce)

        vectors = jnp.stack(
            [b_output, gain_attn, shift_attn, b_reduce, gain_ffn, shift_ffn]
            + [jnp.zeros((width,), BF16)] * 2
        ).astype(F32)
        residual, act, slope, all_expand, all_output = expand(
            place,
            inputs,
            sets,
            [s[1] for s in saved],
            weight_sets,
            biases,
            vectors,
            all_expand,
        )
        output, grad_one, *dctx, mine, send = reduce(
            place,
            residual,
            cot,
            act,
            slope,
            sets,
            saved[0][1],
            all_expand,
            all_output,
            vectors,
            w_reduce,
            pieces_reduce,
        )
        got = flip(send, 1)
        step = lambda i: attend_backward(length, *saved[i], dctx[i], kf)
        backward = [step(0)]
        first, rest = scatter(mine, got, backward[0])
        mine, send = own_grads(place, backward[0], inputs)
        got = flip(send, 1)
        backward.append(step(1))
        second, rest_two = scatter(mine, got, backward[1])
        backward += [step(i) for i in range(2, heads + 1)]
        first = collect(first, rest, backward[-1])
        second = collect(second, rest_two, backward[-1])
        grad_tokens = input_grads(place, grad_one, sets, backward, weight_sets, peers)
        first = finish(first, grad_tokens)
        other = finish(second, grad_tokens)

        dwe, dwr, dwo, small = spread(
            place, first, [width // GROUP, hidden // GROUP, heads * HD // GROUP]
        )
        dqkv, dbias = spread(place, other, [3 * heads * HD // GROUP])
        turned = lambda i: dqkv[i * heads * HD : (i + 1) * heads * HD].T
        flat = lambda i: dbias[:heads, i * HD : (i + 1) * HD].reshape(heads * HD)
        shape = (row_count, length, width)
        return (
            output.reshape(shape),
            grad_tokens.reshape(shape),
            turned(0),
            flat(0),
            turned(1),
            turned(2),
            flat(2),
            dwo,
            small[0],
            small[1],
            small[2],
            dwe,
            small[6],
            dwr,
            small[3],
            small[4],
            small[5],
        )

    rows, split = P("dp", None, None), P(None, "mp")
    return jax.shard_map(
        local,
        mesh=mesh,
        in_specs=(
            rows,
            P("dp", None),
            split,
            P("mp"),
            split,
            split,
            P("mp"),
            P("mp", None),
            P(),
            P(),
            P(),
            split,
            P("mp"),
            P("mp", None),
            P(),
            P(),
            P(),
            rows,
        ),
        out_specs=(
            rows,
            rows,
            split,
            P("mp"),
            split,
            split,
            P("mp"),
            P("mp", None),
            P(),
            P(),
            P(),
            split,
            P("mp"),
            P("mp", None),
            P(),
            P(),
            P(),
        ),
        check_vma=False,
    )
```

```python
import jax
import jax.numpy as jnp
from jax import lax
from jax.experimental import pallas as pl
from jax.experimental.pallas import tpu as pltpu
from jax.sharding import PartitionSpec as P

HD = 64
GROUP = 8
EXTRA = 16
MASK = -float(2**30)
EPS = 1e-12
F32 = jnp.float32
BF16 = jnp.bfloat16
LIMIT = 60 << 20


def dot(left, right, left_dim, right_dim):
    return lax.dot_general(
        left, right, (((left_dim,), (right_dim,)), ((), ())), preferred_element_type=F32
    )


def params():
    return pltpu.CompilerParams(vmem_limit_bytes=LIMIT)


def cost(flops, moved):
    return pl.CostEstimate(flops=int(flops), bytes_accessed=int(moved), transcendentals=0)


def whole(shape):
    zeros = (0,) * len(shape)
    return pl.BlockSpec(shape, lambda *_: zeros, pipeline_mode=pl.Buffered(1))


def split3(row):
    high = row.astype(BF16).astype(F32)
    rest = row - high
    mid = rest.astype(BF16).astype(F32)
    return high, mid, rest - mid


def rows_of(height, first, parts, width):
    place = lax.broadcasted_iota(jnp.int32, (height, width), 0)
    out = jnp.zeros((height, width), F32)
    for i, part in enumerate(parts):
        out = jnp.where(place == first + i, part, out)
    return out


def put(out_ref, start, values, step):
    rows = pl.ds(pl.multiple_of(start, step), values.shape[0])
    out_ref[rows, :] = values.astype(out_ref.dtype)


def peer_shard(place_ref, shards, k):
    return lax.rem(place_ref[GROUP] + shards - k, shards)


def own_block(*shape):
    return pl.BlockSpec(shape, lambda i, p: (p[GROUP],) + (0,) * (len(shape) - 2) + (i,))


def peer_block(peers, first, *shape):
    middle = (0,) * (len(shape) - 2)
    return pl.BlockSpec(
        shape, lambda k, i, p: (lax.rem(p[GROUP] + peers - first - k, peers),) + middle + (i,)
    )


ANY = pl.BlockSpec(memory_space=pl.ANY)


def shift_matrix(amount, length, forward):
    row = lax.broadcasted_iota(jnp.int32, (length, length), 0)
    column = lax.broadcasted_iota(jnp.int32, (length, length), 1)
    apart = column - row if forward else row - column
    return jnp.where((apart == amount) | (apart == amount - length), 1.0, 0.0).astype(BF16)


def shift_kernel(place_ref, first_ref, second_ref, first_out, second_out):
    length = first_ref.shape[0]
    amount = place_ref[GROUP + 1 + pl.program_id(0)]
    matrix = shift_matrix(amount, length, True)
    first_out[...] = dot(matrix, first_ref[...], 1, 0).astype(BF16)
    second_out[...] = dot(matrix, second_ref[...], 1, 0).astype(BF16)


def shift(place, length, first, second):
    tokens, width = first.shape
    by_row = lambda: pl.BlockSpec((length, width), lambda i, *_: (i, 0))
    return pl.pallas_call(
        shift_kernel,
        grid_spec=pltpu.PrefetchScalarGridSpec(
            num_scalar_prefetch=1,
            grid=(tokens // length,),
            in_specs=[by_row(), by_row()],
            out_specs=[by_row(), by_row()],
        ),
        out_shape=[jax.ShapeDtypeStruct((tokens, width), BF16)] * 2,
        compiler_params=params(),
        cost_estimate=cost(4 * tokens * length * width, 12e6),
        name="shift",
    )(place, first, second)


def unshift_kernel(place_ref, in_ref, out_ref):
    length = in_ref.shape[0]
    matrix = shift_matrix(place_ref[GROUP + 1 + pl.program_id(0)], length, False)
    out_ref[...] = dot(matrix, in_ref[...], 1, 0).astype(BF16)


def unshift(place, length, shifted):
    tokens, width = shifted.shape
    by_row = lambda: pl.BlockSpec((length, width), lambda i, *_: (i, 0))
    return pl.pallas_call(
        unshift_kernel,
        grid_spec=pltpu.PrefetchScalarGridSpec(
            num_scalar_prefetch=1,
            grid=(tokens // length,),
            in_specs=[by_row()],
            out_specs=by_row(),
        ),
        out_shape=jax.ShapeDtypeStruct((tokens, width), BF16),
        compiler_params=params(),
        cost_estimate=cost(2 * tokens * length * width, 6e6),
        name="unshift",
    )(place, shifted)


def tiles(heads, block):
    return [(h, slice(i * block, (i + 1) * block)) for h in range(heads) for i in range(2)]


def attend_rows(x_ref, bias_ref, qf_ref, kf_ref, w_scr, qkv_ref, ctx_ref, aug_ref):
    heads = ctx_ref.shape[0]
    length = x_ref.shape[0]
    block = length // 2
    span = 3 * HD
    proj = dot(w_scr[...], x_ref[...], 1, 1)
    scale = HD ** (-0.5)
    for h in range(heads):
        part = proj[h * span : (h + 1) * span] + bias_ref[h]
        qkv_ref[h, :HD, :] = (part[:HD] * scale).astype(BF16)
        qkv_ref[h, HD:, :] = part[HD:].astype(BF16)
    ones_rows = rows_of(EXTRA, 0, (jnp.ones((1, block), F32),), block).astype(BF16)
    items = tiles(heads, block)
    scores = []
    for h, at in items:
        queries = jnp.concatenate([qkv_ref[h, :HD, at], qf_ref[:, at]], axis=0)
        keys = jnp.concatenate([qkv_ref[h, HD : 2 * HD, at], kf_ref[:, at]], axis=0)
        scores.append(dot(keys, queries, 0, 0))
    highest = [jnp.max(part, axis=0, keepdims=True) for part in scores]
    weight = [jnp.exp(part - top).astype(BF16) for part, top in zip(scores, highest)]
    context = []
    for (h, at), part in zip(items, weight):
        values = jnp.concatenate([qkv_ref[h, 2 * HD :, at], ones_rows], axis=0)
        context.append(dot(values, part, 1, 0))
    for (h, at), part, top in zip(items, context, highest):
        total = part[HD : HD + 1]
        ctx_ref[h, :, at] = (part[:HD] * (1.0 / total)).astype(BF16)
        log_total = top + jnp.log(total)
        extra = rows_of(EXTRA, 4, split3(-log_total), block)
        aug_ref[h, :, at] = (extra + qf_ref[:, at].astype(F32)).astype(BF16)


def attend_own_kernel(place_ref, x_ref, bias_ref, qf_ref, kf_ref, own_ref, *refs):
    w_ref, qkv_ref, ctx_ref, aug_ref = refs

    @pl.when(pl.program_id(0) == 0)
    def _():
        w_ref[...] = own_ref[...]

    attend_rows(x_ref, bias_ref, qf_ref, kf_ref, own_ref, qkv_ref, ctx_ref, aug_ref)


def attend_own(length, peers, place, inputs, bias, qf, kf, own):
    height = own.shape[0]
    heads = height // (3 * HD)
    tokens, width = inputs.shape
    every = peers * heads
    shapes = [(peers * height, width)] + [(every, n, tokens) for n in (3 * HD, HD, EXTRA)]
    by_row = pl.BlockSpec((EXTRA, length), lambda i, *_: (0, i))
    return pl.pallas_call(
        attend_own_kernel,
        grid_spec=pltpu.PrefetchScalarGridSpec(
            num_scalar_prefetch=1,
            grid=(tokens // length,),
            in_specs=[
                pl.BlockSpec((length, width), lambda i, *_: (i, 0)),
                whole(bias.shape),
                by_row,
                by_row,
                whole(own.shape),
            ],
            out_specs=[
                pl.BlockSpec((height, width), lambda i, p: (p[GROUP], 0)),
                *[own_block(heads, n, length) for n in (3 * HD, HD, EXTRA)],
            ],
        ),
        out_shape=[jax.ShapeDtypeStruct(shape, BF16) for shape in shapes],
        compiler_params=params(),
        cost_estimate=cost(heads * tokens * (6 * HD * width + 16 * 64 * length), 12e6),
        name="attend_own",
    )(place, inputs, bias, qf, kf, own)


def attend_peers_kernel(spots, place_ref, x_ref, bias_ref, qf_ref, kf_ref, *refs):
    count = len(spots)
    parts = refs[:count]
    w_ref, qkv_ref, ctx_ref, aug_ref, wide_scr = refs[count + 4 :]

    @pl.when(pl.program_id(1) == 0)
    def _():
        size = w_ref.shape[0] // GROUP
        for ref, (index, offset) in zip(parts, spots):
            put(wide_scr, place_ref[index] * size + offset, ref[0], 8)
        w_ref[...] = wide_scr[...].astype(BF16)

    attend_rows(x_ref, bias_ref.at[0], qf_ref, kf_ref, w_ref, qkv_ref, ctx_ref, aug_ref)


def attend_peers(length, peers, place, inputs, bias, qf, kf, pieces, arrays):
    heads = arrays[1].shape[0] // peers
    height = arrays[0].shape[0] // peers
    tokens, width = inputs.shape
    spots = [(index, offset) for _, index, offset in pieces]
    parts = [array for array, _, _ in pieces]
    by_row = pl.BlockSpec((EXTRA, length), lambda k, i, *_: (0, i))
    return pl.pallas_call(
        lambda *refs: attend_peers_kernel(spots, *refs),
        grid_spec=pltpu.PrefetchScalarGridSpec(
            num_scalar_prefetch=1,
            grid=(peers - 1, tokens // length),
            in_specs=[
                pl.BlockSpec((length, width), lambda k, i, *_: (i, 0)),
                pl.BlockSpec((1,) + bias.shape[1:], lambda k, i, *_: (k, 0, 0, 0)),
                by_row,
                by_row,
                *[
                    pl.BlockSpec((1,) + a.shape[1:], lambda k, i, *_: (k, 0, 0)) for a in parts
                ],
                *[ANY] * 4,
            ],
            out_specs=[
                pl.BlockSpec(
                    (height, width), lambda k, i, p: (lax.rem(p[GROUP] + peers - 1 - k, peers), 0)
                ),
                *[peer_block(peers, 1, heads, n, length) for n in (3 * HD, HD, EXTRA)],
            ],
            scratch_shapes=[pltpu.VMEM((height, width), F32)],
        ),
        out_shape=[jax.ShapeDtypeStruct(a.shape, a.dtype) for a in arrays],
        input_output_aliases={5 + len(parts) + i: i for i in range(4)},
        compiler_params=params(),
        cost_estimate=cost(
            (peers - 1) * heads * tokens * (6 * HD * width + 16 * 64 * length), 30e6
        ),
        name="attend_peers",
    )(place, inputs, bias, qf, kf, *parts, *arrays)


def attend_back_rows(qkv_ref, ctx_ref, aug_ref, grad_ref, kf_ref, out_ref):
    heads, _, length = ctx_ref.shape
    block = length // 2
    scale = HD ** (-0.5)
    one = jnp.ones((1, block), F32)
    ones_rows = rows_of(EXTRA, 0, (one, one, one), block).astype(BF16)
    items = tiles(heads, block)
    scores, spreads = [], []
    for h, at in items:
        scores.append(
            dot(
                jnp.concatenate([qkv_ref[h, HD : 2 * HD, at], kf_ref[:, at]], axis=0),
                jnp.concatenate([qkv_ref[h, :HD, at], aug_ref[h, :, at]], axis=0),
                0,
                0,
            )
        )
    for h, at in items:
        grad = grad_ref[h, :, at]
        inner = jnp.sum(grad.astype(F32) * ctx_ref[h, :, at].astype(F32), axis=0, keepdims=True)
        grad_extra = rows_of(EXTRA, 0, split3(-inner), block).astype(BF16)
        spreads.append(
            dot(
                jnp.concatenate([qkv_ref[h, 2 * HD :, at], ones_rows], axis=0),
                jnp.concatenate([grad, grad_extra], axis=0),
                0,
                0,
            )
        )
    probs = [jnp.exp(part) for part in scores]
    slopes = [(part * spread).astype(BF16) for part, spread in zip(probs, spreads)]
    probs = [part.astype(BF16) for part in probs]
    for (h, at), part in zip(items, probs):
        out_ref[h, 2 * HD :, at] = dot(grad_ref[h, :, at], part, 1, 1).astype(BF16)
    for (h, at), part in zip(items, slopes):
        out_ref[h, HD : 2 * HD, at] = dot(qkv_ref[h, :HD, at], part, 1, 1).astype(BF16)
    for (h, at), part in zip(items, slopes):
        grad = dot(qkv_ref[h, HD : 2 * HD, at], part, 1, 0)
        out_ref[h, :HD, at] = (grad * scale).astype(BF16)


def attend_back_own_kernel(place_ref, qkv_ref, ctx_ref, aug_ref, grad_ref, kf_ref, *refs):
    x_ref, dwo_ref, small_ref, early_ref, out_ref, mine_ref, send_ref, grad_scr, sum_scr = refs
    heads = ctx_ref.shape[0]
    height = heads * HD
    step = pl.program_id(0)

    @pl.when(step == 0)
    def _():
        grad_scr[...] = jnp.zeros_like(grad_scr)
        sum_scr[...] = jnp.zeros_like(sum_scr)

    attend_back_rows(qkv_ref, ctx_ref, aug_ref, grad_ref, kf_ref, out_ref)
    ones = jnp.ones((8, x_ref.shape[0]), BF16)
    row = lax.broadcasted_iota(jnp.int32, (8, 3 * HD), 0)
    sums = jnp.zeros((8, 3 * HD), F32)
    for h in range(heads):
        grad = dot(out_ref[h], x_ref[...], 1, 0)
        for i in range(3):
            grad_scr[i * height + h * HD : i * height + (h + 1) * HD, :] += grad[
                i * HD : (i + 1) * HD
            ]
        sums = jnp.where(row == 3 + h, dot(ones, out_ref[h], 1, 1), sums)
    sum_scr[:, : 3 * HD] += sums

    @pl.when(step == pl.num_programs(0) - 1)
    def _():
        size, size_two = 3 * height // GROUP, height // GROUP
        top = size + size_two
        for rel in range(4):
            for source, ref in enumerate((mine_ref, send_ref)):
                owner = place_ref[2 * rel + source]
                ref[rel, :size, :] = grad_scr[pl.ds(pl.multiple_of(owner * size, 8), size), :]
                start = pl.multiple_of(owner * size_two, 8)
                ref[rel, size:top, :] = dwo_ref[pl.ds(start, size_two), :]
                ref[rel, top : top + 8, :] = jnp.where(
                    owner == 0, small_ref[...] + sum_scr[...], 0.0
                )
                ref[rel, top + 8 :, :] = jnp.where(owner == 0, early_ref[...], 0.0)


def attend_back_own(length, place, qkv, ctx, aug, grad, kf, inputs, dwo, small, early):
    height, width = dwo.shape
    heads = height // HD
    tokens = inputs.shape[0]
    share = 4 * height // GROUP + 16
    return pl.pallas_call(
        attend_back_own_kernel,
        grid_spec=pltpu.PrefetchScalarGridSpec(
            num_scalar_prefetch=1,
            grid=(tokens // length,),
            in_specs=[
                own_block(heads, 3 * HD, length),
                own_block(heads, HD, length),
                own_block(heads, EXTRA, length),
                own_block(heads, HD, length),
                pl.BlockSpec((EXTRA, length), lambda i, *_: (0, i)),
                pl.BlockSpec((length, width), lambda i, *_: (i, 0)),
                whole(dwo.shape),
                whole(small.shape),
                whole(early.shape),
            ],
            out_specs=[
                own_block(heads, 3 * HD, length),
                whole((4, share, width)),
                whole((4, share, width)),
            ],
            scratch_shapes=[pltpu.VMEM((3 * height, width), F32), pltpu.VMEM((8, width), F32)],
        ),
        out_shape=[jax.ShapeDtypeStruct(qkv.shape, BF16)]
        + [jax.ShapeDtypeStruct((4, share, width), F32)] * 2,
        compiler_params=params(),
        cost_estimate=cost(heads * tokens * (20 * 64 * length + 6 * HD * width), 12e6),
        name="attend_back_own",
    )(place, qkv, ctx, aug, grad, kf, inputs, dwo, small, early)


def attend_back_kernel(place_ref, qkv_ref, ctx_ref, aug_ref, grad_ref, kf_ref, old_ref, out_ref):
    attend_back_rows(qkv_ref, ctx_ref, aug_ref, grad_ref, kf_ref, out_ref)


def attend_back(length, peers, first, count, place, qkv, ctx, aug, grad, kf, out):
    every, _, tokens = qkv.shape
    heads = every // peers
    by_peer = lambda n: peer_block(peers, first, heads, n, length)
    return pl.pallas_call(
        attend_back_kernel,
        grid_spec=pltpu.PrefetchScalarGridSpec(
            num_scalar_prefetch=1,
            grid=(count, tokens // length),
            in_specs=[
                by_peer(3 * HD),
                by_peer(HD),
                by_peer(EXTRA),
                by_peer(HD),
                pl.BlockSpec((EXTRA, length), lambda k, i, *_: (0, i)),
                ANY,
            ],
            out_specs=by_peer(3 * HD),
        ),
        out_shape=jax.ShapeDtypeStruct(out.shape, BF16),
        input_output_aliases={6: 0},
        compiler_params=params(),
        cost_estimate=cost(count * heads * tokens * 20 * 64 * length, 12e6),
        name="attend_back",
    )(place, qkv, ctx, aug, grad, kf, out)


def norm_forward(hidden):
    center = hidden - jnp.mean(hidden, axis=-1, keepdims=True)
    inverse = lax.rsqrt(jnp.mean(center * center, axis=-1, keepdims=True) + EPS)
    return center * inverse, inverse


def norm_backward(grad, gain, norm, inverse):
    scaled = grad * gain
    first = jnp.mean(scaled, axis=-1, keepdims=True)
    second = jnp.mean(scaled * norm, axis=-1, keepdims=True)
    return (scaled - first - norm * second) * inverse


def column_sum(values):
    return jnp.sum(values, axis=0, keepdims=True)


def flat(values):
    return values.reshape(-1, values.shape[-1])


def expand_kernel(spots, place_ref, x_ref, ctx_ref, bias_ref, vec_ref, own_ref, own_wo_ref, *refs):
    parts, refs = refs[: len(spots)], refs[len(spots) :]
    sum_ref, act_ref, slope_ref, we_ref, wo_ref, wide_scr = refs
    shards, width, _ = we_ref.shape
    size, size_two = width // GROUP, wo_ref.shape[0] // (shards * GROUP)

    @pl.when(pl.program_id(0) == 0)
    def _():
        me = place_ref[GROUP]
        we_ref[me] = own_ref[...]
        put(wide_scr, me * size_two * GROUP, own_wo_ref[...], 8)
        for k in range(1, shards):
            shard = peer_shard(place_ref, shards, k)
            for ref, (index, offset) in zip(parts, spots):
                part = ref[k - 1]
                count = min(part.shape[0], size - offset)
                put(we_ref.at[shard], place_ref[index] * size + offset, part[:count], 16)
                if count < part.shape[0]:
                    start = (shard * GROUP + place_ref[index]) * size_two
                    put(wide_scr, start, part[count:], 8)
        wo_ref[...] = wide_scr[...].astype(BF16)

    b_output, gain_one, shift_one = vec_ref[0:1], vec_ref[1:2], vec_ref[2:3]
    half = x_ref.shape[0] // 2
    halves = [slice(0, half), slice(half, 2 * half)]
    attended = [dot(flat(ctx_ref[:, :, at]), wo_ref[...], 0, 0) for at in halves]
    low = []
    for at, part in zip(halves, attended):
        residual = x_ref[at, :].astype(F32) + (part + b_output)
        sum_ref[at, :] = residual
        norm_one, _ = norm_forward(residual)
        low.append((norm_one * gain_one + shift_one).astype(BF16))
    items = [(s, i) for s in range(shards) for i in range(2)]
    ahead = dot(low[0], we_ref[0], 1, 0)
    for n, (s, i) in enumerate(items):
        hidden = ahead + bias_ref[peer_shard(place_ref, shards, s), 1:2]
        if n + 1 < len(items):
            s_next, i_next = items[n + 1]
            ahead = dot(low[i_next], we_ref[s_next], 1, 0)
        square = hidden * hidden
        bent = jnp.tanh(hidden * (0.7978845608028654 + 0.035677408136300125 * square))
        gate = 0.5 + 0.5 * bent
        active = hidden * gate
        act_ref[s, halves[i], :] = active.astype(BF16)
        slope = gate + (active * (1.0 - gate)) * (1.5957691216057308 + 0.21406444881780075 * square)
        slope_ref[s, halves[i], :] = slope.astype(BF16)


def expand(place, inputs, ctx, biases, vectors, own, own_wo, pieces, shards):
    tokens, width = inputs.shape
    hidden = own.shape[1]
    every = ctx.shape[0]
    block = 512
    spots = [(index, offset) for _, index, offset in pieces]
    parts = [array for array, _, _ in pieces]
    full = (shards, width, hidden)
    by_token = lambda: pl.BlockSpec((block, width), lambda i, *_: (i, 0))
    by_shard = lambda: pl.BlockSpec((shards, block, hidden), lambda i, *_: (0, i, 0))
    return pl.pallas_call(
        lambda *refs: expand_kernel(spots, *refs),
        grid_spec=pltpu.PrefetchScalarGridSpec(
            num_scalar_prefetch=1,
            grid=(tokens // block,),
            in_specs=[
                by_token(),
                pl.BlockSpec((every, HD, block), lambda i, *_: (0, 0, i)),
                whole(biases.shape),
                whole(vectors.shape),
                whole(own.shape),
                whole(own_wo.shape),
                *[whole(a.shape) for a in parts],
            ],
            out_specs=[
                by_token(),
                by_shard(),
                by_shard(),
                whole(full),
                whole((every * HD, width)),
            ],
            scratch_shapes=[pltpu.VMEM((every * HD, width), F32)],
        ),
        out_shape=[
            jax.ShapeDtypeStruct((tokens, width), F32),
            jax.ShapeDtypeStruct((shards, tokens, hidden), BF16),
            jax.ShapeDtypeStruct((shards, tokens, hidden), BF16),
            jax.ShapeDtypeStruct(full, BF16),
            jax.ShapeDtypeStruct((every * HD, width), BF16),
        ],
        compiler_params=params(),
        cost_estimate=cost(2 * tokens * width * (shards * hidden + every * HD), 40e6),
        name="expand",
    )(place, inputs, ctx, biases, vectors, own, own_wo, *parts)


def reduce_kernel(spots, place_ref, sum_ref, cot_ref, act_ref, slope_ref, vec_ref, *refs):
    own_ref, refs = refs[0], refs[1:]
    piece_refs, refs = refs[: len(spots)], refs[len(spots) :]
    out_ref, g2_ref, wr_ref, mine_ref, send_ref, small_scr, dwe_scr, dwr_scr = refs
    step = pl.program_id(0)
    shards = act_ref.shape[0]
    me = place_ref[GROUP]

    @pl.when(step == 0)
    def _():
        wr_ref[me] = own_ref[...]
        for k in range(1, shards):
            shard = peer_shard(place_ref, shards, k)
            for ref, (index, offset) in zip(piece_refs, spots):
                start = place_ref[index] * (wr_ref.shape[1] // GROUP) + offset
                put(wr_ref.at[shard], start, ref[k - 1], 16)
        for scr in (dwe_scr, dwr_scr, small_scr):
            scr[...] = jnp.zeros_like(scr)

    gain_one, shift_one = vec_ref[1:2], vec_ref[2:3]
    b_reduce, gain_two, shift_two = vec_ref[3:4], vec_ref[4:5], vec_ref[5:6]
    half = sum_ref.shape[0] // 2
    halves = [slice(0, half), slice(half, 2 * half)]
    mixed = []
    for at in halves:
        part = dot(act_ref[0, at, :], wr_ref[0], 1, 0)
        for s in range(1, shards):
            part = part + dot(act_ref[s, at, :], wr_ref[s], 1, 0)
        mixed.append(part)
    small = [jnp.zeros((1, sum_ref.shape[1]), F32)] * 4
    low, normed_low, active = [], [], []
    for at, part in zip(halves, mixed):
        norm_one, _ = norm_forward(sum_ref[at, :])
        normed = norm_one * gain_one + shift_one
        normed_low.append(normed.astype(BF16))
        norm_two, inverse_two = norm_forward(normed + (part + b_reduce))
        out_ref[at, :] = (norm_two * gain_two + shift_two).astype(BF16)
        cot = cot_ref[at, :].astype(F32)
        grad_two = norm_backward(cot, gain_two, norm_two, inverse_two)
        g2_ref[at, :] = grad_two
        low.append(grad_two.astype(BF16))
        active.append(dot(low[-1], own_ref[...], 1, 1))
        small[0] = small[0] + column_sum(grad_two)
        small[1] = small[1] + column_sum(cot * norm_two)
        small[2] = small[2] + column_sum(cot)
    dwr_scr[...] += dot(act_ref[me], jnp.concatenate(low, axis=0), 0, 0)
    own = []
    for at, part in zip(halves, active):
        own.append((part * slope_ref[0, at, :].astype(F32)).astype(BF16))
        small[3] = small[3] + column_sum(own[-1].astype(F32))
    dwe_scr[...] += dot(
        jnp.concatenate(normed_low, axis=0), jnp.concatenate(own, axis=0), 0, 0
    )
    for n, part in enumerate(small):
        small_scr[n : n + 1] += part

    @pl.when(step == pl.num_programs(0) - 1)
    def _():
        for plane in range(4):
            for ref, core in ((mine_ref, place_ref[0]), (send_ref, place_ref[1])):
                owner = 2 * plane + lax.rem(core, 2)
                top = 0
                for scr in (dwe_scr, dwr_scr):
                    size = scr.shape[0] // GROUP
                    start = pl.multiple_of(owner * size, 8)
                    ref[plane, top : top + size, :] = scr[pl.ds(start, size), :]
                    top += size


def reduce(place, residual, cot, act, slope, vectors, own, pieces):
    tokens, width = residual.shape
    shards, _, hidden = act.shape
    block = 512
    share = (width + hidden) // GROUP
    spots = [(index, offset) for _, index, offset in pieces]
    arrays = [array for array, _, _ in pieces]
    by_token = lambda: pl.BlockSpec((block, width), lambda i, *_: (i, 0))
    return pl.pallas_call(
        lambda *refs: reduce_kernel(spots, *refs),
        grid_spec=pltpu.PrefetchScalarGridSpec(
            num_scalar_prefetch=1,
            grid=(tokens // block,),
            in_specs=[
                by_token(),
                by_token(),
                pl.BlockSpec((shards, block, hidden), lambda i, *_: (0, i, 0)),
                pl.BlockSpec((1, block, hidden), lambda i, p: (p[GROUP], i, 0)),
                whole(vectors.shape),
                whole(own.shape),
                *[whole(a.shape) for a in arrays],
            ],
            out_specs=[
                by_token(),
                by_token(),
                whole((shards, hidden, width)),
                whole((4, share, width)),
                whole((4, share, width)),
                whole((8, width)),
            ],
            scratch_shapes=[pltpu.VMEM((width, hidden), F32), pltpu.VMEM((hidden, width), F32)],
        ),
        out_shape=[
            jax.ShapeDtypeStruct((tokens, width), BF16),
            jax.ShapeDtypeStruct((tokens, width), F32),
            jax.ShapeDtypeStruct((shards, hidden, width), BF16),
            jax.ShapeDtypeStruct((4, share, width), F32),
            jax.ShapeDtypeStruct((4, share, width), F32),
            jax.ShapeDtypeStruct((8, width), F32),
        ],
        compiler_params=params(),
        cost_estimate=cost(tokens * width * hidden * (2 * shards + 6), 40e6),
        name="reduce",
    )(place, residual, cot, act, slope, vectors, own, *arrays)


def return_kernel(place_ref, sum_ref, g2_ref, slope_ref, ctx_ref, we_ref, wr_ref, w_ref, *refs):
    vec_ref, g1_ref, dctx_ref, dwo_ref, small_ref = refs
    shards = we_ref.shape[0]

    @pl.when(pl.program_id(0) == 0)
    def _():
        dwo_ref[...] = jnp.zeros_like(dwo_ref)
        small_ref[...] = jnp.zeros_like(small_ref)

    half = sum_ref.shape[0] // 2
    halves = [slice(0, half), slice(half, 2 * half)]
    gain_one = vec_ref[1:2]
    low = [g2_ref[at, :].astype(BF16) for at in halves]
    items = [(s, i) for s in range(shards) for i in range(2)]
    total = [g2_ref[at, :] for at in halves]
    ahead = dot(low[0], wr_ref[0], 1, 1)
    for n, (s, i) in enumerate(items):
        grad_active = ahead
        if n + 1 < len(items):
            s_next, i_next = items[n + 1]
            ahead = dot(low[i_next], wr_ref[s_next], 1, 1)
        grad_hidden = (grad_active * slope_ref[s, halves[i], :].astype(F32)).astype(BF16)
        total[i] = total[i] + dot(grad_hidden, we_ref[s], 1, 1)
    small = [jnp.zeros((1, sum_ref.shape[1]), F32)] * 3
    one = []
    for at, grad_normed in zip(halves, total):
        norm_one, inverse_one = norm_forward(sum_ref[at, :])
        grad_one = norm_backward(grad_normed, gain_one, norm_one, inverse_one)
        g1_ref[at, :] = grad_one
        one.append(grad_one.astype(BF16))
        small[0] = small[0] + column_sum(grad_one)
        small[1] = small[1] + column_sum(grad_normed * norm_one)
        small[2] = small[2] + column_sum(grad_normed)
    one = jnp.concatenate(one, axis=0)
    dctx = dot(w_ref[...], one, 1, 1)
    dwo_ref[...] += dot(flat(ctx_ref[...]), one, 1, 0)
    dctx_ref[...] = dctx.astype(BF16).reshape(dctx_ref.shape)
    for n, part in enumerate(small):
        small_ref[n : n + 1] += part


def back_to_context(place, residual, grad_two, slope, ctx, w_expand, w_reduce, weights, vectors):
    tokens, width = residual.shape
    shards, _, hidden = w_expand.shape
    every = ctx.shape[0]
    heads = every // shards
    block = 512
    by_token = lambda: pl.BlockSpec((block, width), lambda i, *_: (i, 0))
    return pl.pallas_call(
        return_kernel,
        grid_spec=pltpu.PrefetchScalarGridSpec(
            num_scalar_prefetch=1,
            grid=(tokens // block,),
            in_specs=[
                by_token(),
                by_token(),
                pl.BlockSpec((shards, block, hidden), lambda i, *_: (0, i, 0)),
                own_block(heads, HD, block),
                whole(w_expand.shape),
                whole(w_reduce.shape),
                whole(weights.shape),
                whole(vectors.shape),
            ],
            out_specs=[
                by_token(),
                pl.BlockSpec((every, HD, block), lambda i, *_: (0, 0, i)),
                whole((heads * HD, width)),
                whole((8, width)),
            ],
        ),
        out_shape=[
            jax.ShapeDtypeStruct((tokens, width), F32),
            jax.ShapeDtypeStruct(ctx.shape, BF16),
            jax.ShapeDtypeStruct((heads * HD, width), F32),
            jax.ShapeDtypeStruct((8, width), F32),
        ],
        compiler_params=params(),
        cost_estimate=cost(tokens * width * (4 * shards * hidden + 2 * every * HD), 40e6),
        name="back_to_context",
    )(place, residual, grad_two, slope, ctx, w_expand, w_reduce, weights, vectors)


def spread_kernel(sizes, place_ref, mine_ref, other_ref, *outs):
    for plane in range(4):
        for ref, core in ((mine_ref, place_ref[0]), (other_ref, place_ref[1])):
            owner = 2 * plane + lax.rem(core, 2)
            top = 0
            for size, out_ref in zip(sizes, outs):
                put(out_ref, owner * size, ref[plane, top : top + size, :], 8)
                top += size


def spread(place, mine, other, sizes):
    width = mine.shape[2]
    shapes = [(GROUP * size, width) for size in sizes]
    return pl.pallas_call(
        lambda *refs: spread_kernel(sizes, *refs),
        grid_spec=pltpu.PrefetchScalarGridSpec(
            num_scalar_prefetch=1,
            grid=(1,),
            in_specs=[whole(mine.shape), whole(other.shape)],
            out_specs=[whole(s) for s in shapes],
        ),
        out_shape=[jax.ShapeDtypeStruct(s, F32) for s in shapes],
        compiler_params=params(),
        cost_estimate=cost(0, 16 * mine.size),
        name="spread",
    )(place, mine, other)


def spread_late_kernel(heads, place_ref, *refs):
    parts = refs[:GROUP]
    dq_ref, dk_ref, dv_ref, dwo_ref, small_ref, grad_scr = refs[GROUP:]
    height = heads * HD
    size, size_two = 3 * height // GROUP, height // GROUP
    top = size + size_two
    for i, ref in enumerate(parts):
        owner = place_ref[i]
        put(grad_scr, owner * size, ref[:size, :], 8)
        put(dwo_ref, owner * size_two, ref[size:top, :], 8)

        @pl.when(owner == 0)
        def _():
            small_ref[...] = ref[top:, :]

    for i, out_ref in enumerate((dq_ref, dk_ref, dv_ref)):
        out_ref[...] = grad_scr[i * height : (i + 1) * height, :]


def spread_late(place, parts, heads):
    share, width = parts[0].shape
    height = heads * HD
    shapes = [(height, width)] * 4 + [(16, width)]
    return pl.pallas_call(
        lambda *refs: spread_late_kernel(heads, *refs),
        grid_spec=pltpu.PrefetchScalarGridSpec(
            num_scalar_prefetch=1,
            grid=(1,),
            in_specs=[whole(a.shape) for a in parts],
            out_specs=[whole(s) for s in shapes],
            scratch_shapes=[pltpu.VMEM((3 * height, width), F32)],
        ),
        out_shape=[jax.ShapeDtypeStruct(s, F32) for s in shapes],
        compiler_params=params(),
        cost_estimate=cost(0, 8 * parts[0].size * 8),
        name="spread_late",
    )(place, *parts)


def input_grads_kernel(place_ref, g1_ref, grad_ref, w_ref, out_ref):
    amount = place_ref[GROUP + 1 + pl.program_id(0)]
    matrix = shift_matrix(amount, g1_ref.shape[0], False)
    total = g1_ref[...] + dot(flat(grad_ref[...]), w_ref[...], 0, 0)
    out_ref[...] = dot(matrix, total.astype(BF16), 1, 0).astype(BF16)


def input_grads(place, length, grad_one, grads, weights):
    tokens, width = grad_one.shape
    every = grads.shape[0]
    by_row = lambda: pl.BlockSpec((length, width), lambda i, *_: (i, 0))
    return pl.pallas_call(
        input_grads_kernel,
        grid_spec=pltpu.PrefetchScalarGridSpec(
            num_scalar_prefetch=1,
            grid=(tokens // length,),
            in_specs=[
                by_row(),
                pl.BlockSpec((every, 3 * HD, length), lambda i, *_: (0, 0, i)),
                whole(weights.shape),
            ],
            out_specs=by_row(),
        ),
        out_shape=jax.ShapeDtypeStruct((tokens, width), BF16),
        compiler_params=params(),
        cost_estimate=cost(2 * tokens * width * (every * 3 * HD + length), 20e6),
        name="input_grads",
    )(place, grad_one, grads, weights)


def after(values, *others):
    return lax.optimization_barrier((values, others))[0]


def solution(mesh):
    peers = mesh.shape["mp"]
    lanes = mesh.shape["dp"]
    rotations = [[(i, (i + k) % peers) for i in range(peers)] for k in range(1, peers)]

    def flip(values, bits):
        return lax.ppermute(values, "dp", [(i, i ^ bits) for i in range(lanes)])

    def from_peers(piece):
        return jnp.stack([lax.ppermute(piece, "mp", perm) for perm in rotations])

    def swapped(piece, *ready):
        copies = jnp.broadcast_to(piece[None], (peers,) + piece.shape)
        got = lax.all_to_all(after(copies, *ready), "mp", 0, 0, tiled=True)
        me = lax.axis_index("mp")
        return jnp.concatenate(
            [
                lax.dynamic_slice_in_dim(got, lax.rem(me + peers - k, peers), 1, 0)
                for k in range(1, peers)
            ]
        )

    def both(near):
        return flip(near, 2), flip(near, 4)

    def corner(by_x, by_y, cut):
        return flip(by_y[:, :cut], 2), flip(by_x[:, cut:], 4)

    def listed(near, by_x, by_y, first, second, cut):
        places = ((near, 0, 0), (by_x, 1, 0), (by_y, 2, 0), (first, 3, 0), (second, 3, cut))
        return with_core(places)

    def with_core(places):
        out = []
        for array, rel, offset in places:
            out.append((array, 2 * rel, offset))
            out.append((flip(array, 1), 2 * rel + 1, offset))
        return out

    planes = [[g + c + i for i in (0, 2, 4, 6)] for g in range(0, lanes, GROUP) for c in (0, 1)]

    def swap_plane(values):
        return lax.all_to_all(values, "dp", 0, 0, tiled=True, axis_index_groups=planes)

    def sum_groups(total):
        step = GROUP
        while step < lanes:
            total = total + flip(total, step)
            step *= 2
        return total

    def partial_sums(mine, got, *ready):
        got = after(got, *ready)
        return [mine[rel] + got[rel] for rel in range(4)]

    def exchange(parts):
        return [flip(parts[rel], 2 * rel) for rel in (1, 2, 3)]

    def total_of(first, rest, *ready):
        rest = after(rest, *ready)
        return sum_groups(first + rest[0] + rest[1] + rest[2])

    def finish(arrays, *ready):
        out = []
        for array in after(arrays, *ready):
            out += [array, flip(array, 1)]
        return out

    def local(
        tokens,
        doc_lengths,
        w_query,
        b_query,
        w_key,
        w_value,
        b_value,
        w_output,
        b_output,
        gain_attn,
        shift_attn,
        w_expand,
        b_expand,
        w_reduce,
        b_reduce,
        gain_ffn,
        shift_ffn,
        cotangent,
    ):
        row_count, length, width = tokens.shape
        heads = w_query.shape[1] // HD
        hidden = w_expand.shape[1]
        count = row_count * length
        inside = lax.axis_index("dp") % GROUP
        me = lax.axis_index("mp")
        ends = jnp.cumsum(doc_lengths, axis=-1)
        longest = jnp.max(doc_lengths, axis=-1, keepdims=True)
        offset = jnp.max(jnp.where(doc_lengths == longest, ends - doc_lengths, 0), axis=-1)
        place = jnp.stack([inside ^ i for i in range(GROUP)] + [me])
        place = jnp.concatenate([place, offset]).astype(jnp.int32)

        by_head = lambda w: w.T.reshape(heads, HD, width)
        own_heads = jnp.concatenate([by_head(w_query), by_head(w_key), by_head(w_value)], axis=1)
        own_heads = own_heads.reshape(3 * heads * HD, width)
        blank = jnp.zeros((width - 2 * heads * HD,), BF16)
        own_bias = jnp.stack(
            [jnp.concatenate([b_query, b_value, blank]), b_expand]
            + [jnp.zeros((width,), BF16)] * 6
        ).astype(F32)

        def piece_of(array):
            size = array.shape[0] // GROUP
            return lax.dynamic_slice_in_dim(array, inside * size, size, 0).astype(F32)

        piece = piece_of(own_heads)
        near = from_peers(jnp.concatenate([piece, own_bias]))

        def columns(rows):
            parts = rows[:, 0, : 2 * heads * HD].reshape(-1, 2, heads, HD)
            blank = jnp.zeros((rows.shape[0], heads, HD), F32)
            return jnp.concatenate([parts[:, 0], blank, parts[:, 1]], axis=-1)[..., None]

        position = (jnp.arange(length, dtype=jnp.int32)[None] + offset[:, None]) % length
        segment = jnp.sum((position[:, :, None] >= ends[:, None, :]).astype(jnp.int32), axis=-1)
        segment = segment.reshape(1, count)
        docs = doc_lengths.shape[1]
        label = jnp.arange(EXTRA, dtype=jnp.int32)[:, None]
        is_doc = label < docs
        qf = jnp.where(is_doc & (segment == label), 1.0, 0.0).astype(BF16)
        kf = jnp.where(
            is_doc,
            jnp.where(segment == label, 0.0, MASK),
            jnp.where(label < docs + 3, 1.0, 0.0),
        ).astype(BF16)
        inputs, cot = shift(
            place, length, tokens.reshape(count, width), cotangent.reshape(count, width)
        )
        own = attend_own(
            length, peers, place, inputs, columns(own_bias[None])[0], qf, kf, own_heads
        )

        near = after(near, own)
        biases = near[:, -own_bias.shape[0] :]
        peer_columns = columns(biases)
        biases = jnp.concatenate([own_bias[None], biases])
        near = near[:, : -own_bias.shape[0]]
        cut = piece.shape[0] // 16 * 8
        share = jnp.concatenate([piece_of(w_expand), piece_of(w_output)])
        near_expand = swapped(share, near)
        sides = both(near)
        corners = corner(*sides, cut)
        pieces = listed(near, *sides, *corners, cut)
        near_reduce = swapped(piece_of(w_reduce), near_expand)
        sides_expand = both(after(near_expand, corners))
        weights, qkv, ctx, aug = attend_peers(
            length, peers, place, inputs, after(peer_columns, near_expand), qf, kf, pieces, own
        )

        sides_expand = after(sides_expand, ctx)
        cut = width // GROUP // 2
        corners = corner(*sides_expand, cut)
        pieces = listed(near_expand, *sides_expand, *corners, cut)
        far_reduce = [flip(near_reduce, bits) for bits in (2, 4, 6)]
        vectors = jnp.stack(
            [b_output, gain_attn, shift_attn, b_reduce, gain_ffn, shift_ffn]
            + [jnp.zeros((width,), BF16)] * 2
        ).astype(F32)
        residual, act, slope, all_expand, all_output = expand(
            place,
            inputs,
            ctx,
            after(biases, near_reduce),
            vectors,
            w_expand,
            w_output,
            pieces,
            peers,
        )
        far_reduce = after(far_reduce, residual)
        pieces = with_core([(array, rel, 0) for rel, array in enumerate([near_reduce] + far_reduce)])
        shifted, grad_two, all_reduce, mine, send, small_one = reduce(
            place, residual, cot, act, slope, vectors, w_reduce, pieces
        )
        got = flip(send, 1)
        output = unshift(place, length, shifted)
        chip = mine + after(got, output)
        early = swap_plane(chip)
        grad_one, dctx, dwo, small = back_to_context(
            place,
            residual,
            grad_two,
            slope,
            ctx,
            all_expand,
            all_reduce,
            all_output,
            after(vectors, chip),
        )
        total = sum_groups(jnp.sum(after(early, grad_one), axis=0))
        copies = jnp.broadcast_to(total[None], (4,) + total.shape)
        early = swap_plane(copies)

        dqkv, mine, send = attend_back_own(
            length, place, qkv, ctx, aug, dctx, after(kf, copies), inputs, dwo, small, small_one
        )
        got = flip(send, 1)
        dqkv = attend_back(length, peers, 1, 1, place, qkv, ctx, aug, dctx, kf, dqkv)
        parts = partial_sums(mine, got, dqkv)
        rest = exchange(parts)
        dqkv = attend_back(
            length, peers, 2, peers - 2, place, qkv, ctx, aug, dctx, after(kf, parts), dqkv
        )
        total = total_of(parts[0], rest, dqkv)
        early = after(early, total)
        second = [total] + exchange([None] + [total] * 3)
        grad_tokens = input_grads(place, length, after(grad_one, total), dqkv, weights)
        second = finish(second, grad_tokens)
        dwe, dwr = spread(place, early, flip(early, 1), [width // GROUP, hidden // GROUP])
        dq, dk, dv, dwo, small_two = spread_late(place, second, heads)
        sums = lambda i: small_two[3 : 3 + heads, i * HD : (i + 1) * HD].reshape(heads * HD)
        shape = (row_count, length, width)
        return (
            output.reshape(shape),
            grad_tokens.reshape(shape),
            dq.T,
            sums(0),
            dk.T,
            dv.T,
            sums(2),
            dwo,
            small_two[0],
            small_two[1],
            small_two[2],
            dwe,
            small_two[11],
            dwr,
            small_two[8],
            small_two[9],
            small_two[10],
        )

    rows, split = P("dp", None, None), P(None, "mp")
    return jax.shard_map(
        local,
        mesh=mesh,
        in_specs=(
            rows,
            P("dp", None),
            split,
            P("mp"),
            split,
            split,
            P("mp"),
            P("mp", None),
            P(),
            P(),
            P(),
            split,
            P("mp"),
            P("mp", None),
            P(),
            P(),
            P(),
            rows,
        ),
        out_specs=(
            rows,
            rows,
            split,
            P("mp"),
            split,
            split,
            P("mp"),
            P("mp", None),
            P(),
            P(),
            P(),
            split,
            P("mp"),
            P("mp", None),
            P(),
            P(),
            P(),
        ),
        check_vma=False,
    )
```

```python
import jax
import jax.numpy as jnp
from jax import lax
from jax.experimental import pallas as pl
from jax.experimental.pallas import tpu as pltpu
from jax.sharding import PartitionSpec as P

HD = 64
GROUP = 8
EXTRA = 16
MASK = -float(2**30)
EPS = 1e-12
F32 = jnp.float32
BF16 = jnp.bfloat16
LIMIT = 60 << 20


def dot(left, right, left_dim, right_dim):
    return lax.dot_general(
        left, right, (((left_dim,), (right_dim,)), ((), ())), preferred_element_type=F32
    )


def params():
    return pltpu.CompilerParams(vmem_limit_bytes=LIMIT)


def cost(flops, moved):
    return pl.CostEstimate(flops=int(flops), bytes_accessed=int(moved), transcendentals=0)


def whole(shape):
    zeros = (0,) * len(shape)
    return pl.BlockSpec(shape, lambda *_: zeros, pipeline_mode=pl.Buffered(1))


def split3(row):
    high = row.astype(BF16).astype(F32)
    rest = row - high
    mid = rest.astype(BF16).astype(F32)
    return high, mid, rest - mid


def rows_of(height, first, parts, width):
    place = lax.broadcasted_iota(jnp.int32, (height, width), 0)
    out = jnp.zeros((height, width), F32)
    for i, part in enumerate(parts):
        out = jnp.where(place == first + i, part, out)
    return out


def put(out_ref, start, values, step):
    rows = pl.ds(pl.multiple_of(start, step), values.shape[0])
    out_ref[rows, :] = values.astype(out_ref.dtype)


def peer_shard(place_ref, shards, k):
    return lax.rem(place_ref[GROUP] + shards - k, shards)


def own_block(*shape):
    return pl.BlockSpec(shape, lambda i, p: (p[GROUP],) + (0,) * (len(shape) - 2) + (i,))


def peer_block(peers, first, *shape):
    middle = (0,) * (len(shape) - 2)
    return pl.BlockSpec(
        shape, lambda k, i, p: (lax.rem(p[GROUP] + peers - first - k, peers),) + middle + (i,)
    )


ANY = pl.BlockSpec(memory_space=pl.ANY)


def shift_matrix(amount, length, forward):
    row = lax.broadcasted_iota(jnp.int32, (length, length), 0)
    column = lax.broadcasted_iota(jnp.int32, (length, length), 1)
    apart = column - row if forward else row - column
    return jnp.where((apart == amount) | (apart == amount - length), 1.0, 0.0).astype(BF16)


def shift_kernel(place_ref, first_ref, second_ref, first_out, second_out):
    length = first_ref.shape[0]
    amount = place_ref[GROUP + 1 + pl.program_id(0)]
    matrix = shift_matrix(amount, length, True)
    first_out[...] = dot(matrix, first_ref[...], 1, 0).astype(BF16)
    second_out[...] = dot(matrix, second_ref[...], 1, 0).astype(BF16)


def shift(place, length, first, second):
    tokens, width = first.shape
    by_row = lambda: pl.BlockSpec((length, width), lambda i, *_: (i, 0))
    return pl.pallas_call(
        shift_kernel,
        grid_spec=pltpu.PrefetchScalarGridSpec(
            num_scalar_prefetch=1,
            grid=(tokens // length,),
            in_specs=[by_row(), by_row()],
            out_specs=[by_row(), by_row()],
        ),
        out_shape=[jax.ShapeDtypeStruct((tokens, width), BF16)] * 2,
        compiler_params=params(),
        cost_estimate=cost(4 * tokens * length * width, 12e6),
        name="shift",
    )(place, first, second)


def unshift_kernel(place_ref, in_ref, out_ref):
    length = in_ref.shape[0]
    matrix = shift_matrix(place_ref[GROUP + 1 + pl.program_id(0)], length, False)
    out_ref[...] = dot(matrix, in_ref[...], 1, 0).astype(BF16)


def unshift(place, length, shifted):
    tokens, width = shifted.shape
    by_row = lambda: pl.BlockSpec((length, width), lambda i, *_: (i, 0))
    return pl.pallas_call(
        unshift_kernel,
        grid_spec=pltpu.PrefetchScalarGridSpec(
            num_scalar_prefetch=1,
            grid=(tokens // length,),
            in_specs=[by_row()],
            out_specs=by_row(),
        ),
        out_shape=jax.ShapeDtypeStruct((tokens, width), BF16),
        compiler_params=params(),
        cost_estimate=cost(2 * tokens * length * width, 6e6),
        name="unshift",
    )(place, shifted)


def tiles(heads, block):
    return [(h, slice(i * block, (i + 1) * block)) for h in range(heads) for i in range(2)]


def attend_rows(x_ref, bias_ref, qf_ref, kf_ref, w_scr, qkv_ref, ctx_ref, aug_ref):
    heads = ctx_ref.shape[0]
    length = x_ref.shape[0]
    block = length // 2
    span = 3 * HD
    proj = dot(w_scr[...], x_ref[...], 1, 1)
    scale = HD ** (-0.5)
    for h in range(heads):
        part = proj[h * span : (h + 1) * span] + bias_ref[h]
        qkv_ref[h, :HD, :] = (part[:HD] * scale).astype(BF16)
        qkv_ref[h, HD:, :] = part[HD:].astype(BF16)
    ones_rows = rows_of(EXTRA, 0, (jnp.ones((1, block), F32),), block).astype(BF16)
    items = tiles(heads, block)
    scores = []
    for h, at in items:
        queries = jnp.concatenate([qkv_ref[h, :HD, at], qf_ref[:, at]], axis=0)
        keys = jnp.concatenate([qkv_ref[h, HD : 2 * HD, at], kf_ref[:, at]], axis=0)
        scores.append(dot(keys, queries, 0, 0))
    highest = [jnp.max(part, axis=0, keepdims=True) for part in scores]
    weight = [jnp.exp(part - top).astype(BF16) for part, top in zip(scores, highest)]
    context = []
    for (h, at), part in zip(items, weight):
        values = jnp.concatenate([qkv_ref[h, 2 * HD :, at], ones_rows], axis=0)
        context.append(dot(values, part, 1, 0))
    for (h, at), part, top in zip(items, context, highest):
        total = part[HD : HD + 1]
        ctx_ref[h, :, at] = (part[:HD] * (1.0 / total)).astype(BF16)
        log_total = top + jnp.log(total)
        extra = rows_of(EXTRA, 4, split3(-log_total), block)
        aug_ref[h, :, at] = (extra + qf_ref[:, at].astype(F32)).astype(BF16)


def attend_own_kernel(place_ref, x_ref, bias_ref, qf_ref, kf_ref, own_ref, *refs):
    w_ref, wo_ref, qkv_ref, ctx_ref, aug_ref = refs
    height = w_ref.shape[0]

    @pl.when(pl.program_id(0) == 0)
    def _():
        w_ref[...] = own_ref[:height, :]
        wo_ref[...] = own_ref[height:, :]

    attend_rows(x_ref, bias_ref, qf_ref, kf_ref, w_ref, qkv_ref, ctx_ref, aug_ref)


def attend_own(length, peers, place, inputs, bias, qf, kf, own):
    heads = own.shape[0] // (4 * HD)
    tokens, width = inputs.shape
    every = peers * heads
    shapes = [(every * 3 * HD, width), (every * HD, width)]
    shapes += [(every, n, tokens) for n in (3 * HD, HD, EXTRA)]
    by_row = pl.BlockSpec((EXTRA, length), lambda i, *_: (0, i))
    return pl.pallas_call(
        attend_own_kernel,
        grid_spec=pltpu.PrefetchScalarGridSpec(
            num_scalar_prefetch=1,
            grid=(tokens // length,),
            in_specs=[
                pl.BlockSpec((length, width), lambda i, *_: (i, 0)),
                whole(bias.shape),
                by_row,
                by_row,
                whole(own.shape),
            ],
            out_specs=[
                pl.BlockSpec((heads * 3 * HD, width), lambda i, p: (p[GROUP], 0)),
                pl.BlockSpec((heads * HD, width), lambda i, p: (p[GROUP], 0)),
                *[own_block(heads, n, length) for n in (3 * HD, HD, EXTRA)],
            ],
        ),
        out_shape=[jax.ShapeDtypeStruct(shape, BF16) for shape in shapes],
        compiler_params=params(),
        cost_estimate=cost(heads * tokens * (6 * HD * width + 16 * 64 * length), 12e6),
        name="attend_own",
    )(place, inputs, bias, qf, kf, own)


def attend_peers_kernel(spots, place_ref, x_ref, bias_ref, qf_ref, kf_ref, *refs):
    count = len(spots)
    parts = refs[:count]
    w_ref, wo_ref, qkv_ref, ctx_ref, aug_ref, w_scr = refs[count + 5 :]
    height = w_ref.shape[0]

    @pl.when(pl.program_id(1) == 0)
    def _():
        size = w_scr.shape[0] // GROUP
        for ref, (index, offset) in zip(parts, spots):
            put(w_scr, place_ref[index] * size + offset, ref[0], 16)
        w_ref[...] = w_scr[:height, :]
        wo_ref[...] = w_scr[height:, :]

    attend_rows(x_ref, bias_ref.at[0], qf_ref, kf_ref, w_ref, qkv_ref, ctx_ref, aug_ref)


def attend_peers(length, peers, place, inputs, bias, qf, kf, pieces, arrays):
    heads = arrays[2].shape[0] // peers
    tokens, width = inputs.shape
    spots = [(index, offset) for _, index, offset in pieces]
    parts = [array for array, _, _ in pieces]
    by_row = pl.BlockSpec((EXTRA, length), lambda k, i, *_: (0, i))
    return pl.pallas_call(
        lambda *refs: attend_peers_kernel(spots, *refs),
        grid_spec=pltpu.PrefetchScalarGridSpec(
            num_scalar_prefetch=1,
            grid=(peers - 1, tokens // length),
            in_specs=[
                pl.BlockSpec((length, width), lambda k, i, *_: (i, 0)),
                pl.BlockSpec((1,) + bias.shape[1:], lambda k, i, *_: (k, 0, 0, 0)),
                by_row,
                by_row,
                *[
                    pl.BlockSpec((1,) + a.shape[1:], lambda k, i, *_: (k, 0, 0)) for a in parts
                ],
                *[ANY] * 5,
            ],
            out_specs=[
                *[
                    pl.BlockSpec(
                        (heads * n, width),
                        lambda k, i, p: (lax.rem(p[GROUP] + peers - 1 - k, peers), 0),
                    )
                    for n in (3 * HD, HD)
                ],
                *[peer_block(peers, 1, heads, n, length) for n in (3 * HD, HD, EXTRA)],
            ],
            scratch_shapes=[pltpu.VMEM((heads * 4 * HD, width), BF16)],
        ),
        out_shape=[jax.ShapeDtypeStruct(a.shape, a.dtype) for a in arrays],
        input_output_aliases={5 + len(parts) + i: i for i in range(5)},
        compiler_params=params(),
        cost_estimate=cost(
            (peers - 1) * heads * tokens * (6 * HD * width + 16 * 64 * length), 30e6
        ),
        name="attend_peers",
    )(place, inputs, bias, qf, kf, *parts, *arrays)


def attend_back_rows(qkv_ref, ctx_ref, aug_ref, grad_ref, kf_ref, out_ref):
    heads, _, length = ctx_ref.shape
    block = length // 2
    scale = HD ** (-0.5)
    one = jnp.ones((1, block), F32)
    ones_rows = rows_of(EXTRA, 0, (one, one, one), block).astype(BF16)
    items = tiles(heads, block)
    scores, spreads = [], []
    for h, at in items:
        scores.append(
            dot(
                jnp.concatenate([qkv_ref[h, HD : 2 * HD, at], kf_ref[:, at]], axis=0),
                jnp.concatenate([qkv_ref[h, :HD, at], aug_ref[h, :, at]], axis=0),
                0,
                0,
            )
        )
    for h, at in items:
        grad = grad_ref[h, :, at]
        inner = jnp.sum(grad.astype(F32) * ctx_ref[h, :, at].astype(F32), axis=0, keepdims=True)
        grad_extra = rows_of(EXTRA, 0, split3(-inner), block).astype(BF16)
        spreads.append(
            dot(
                jnp.concatenate([qkv_ref[h, 2 * HD :, at], ones_rows], axis=0),
                jnp.concatenate([grad, grad_extra], axis=0),
                0,
                0,
            )
        )
    probs = [jnp.exp(part) for part in scores]
    slopes = [(part * spread).astype(BF16) for part, spread in zip(probs, spreads)]
    probs = [part.astype(BF16) for part in probs]
    for (h, at), part in zip(items, probs):
        out_ref[h, 2 * HD :, at] = dot(grad_ref[h, :, at], part, 1, 1).astype(BF16)
    for (h, at), part in zip(items, slopes):
        out_ref[h, HD : 2 * HD, at] = dot(qkv_ref[h, :HD, at], part, 1, 1).astype(BF16)
    for (h, at), part in zip(items, slopes):
        grad = dot(qkv_ref[h, HD : 2 * HD, at], part, 1, 0)
        out_ref[h, :HD, at] = (grad * scale).astype(BF16)


def attend_back_own_kernel(place_ref, qkv_ref, ctx_ref, aug_ref, grad_ref, kf_ref, *refs):
    x_ref, dwo_ref, small_ref, early_ref, out_ref, mine_ref, send_ref, grad_scr, sum_scr = refs
    heads = ctx_ref.shape[0]
    height = heads * HD
    step = pl.program_id(0)

    @pl.when(step == 0)
    def _():
        grad_scr[...] = jnp.zeros_like(grad_scr)
        sum_scr[...] = jnp.zeros_like(sum_scr)

    attend_back_rows(qkv_ref, ctx_ref, aug_ref, grad_ref, kf_ref, out_ref)
    ones = jnp.ones((8, x_ref.shape[0]), BF16)
    row = lax.broadcasted_iota(jnp.int32, (8, 3 * HD), 0)
    sums = jnp.zeros((8, 3 * HD), F32)
    for h in range(heads):
        grad = dot(out_ref[h], x_ref[...], 1, 0)
        for i in range(3):
            grad_scr[i * height + h * HD : i * height + (h + 1) * HD, :] += grad[
                i * HD : (i + 1) * HD
            ]
        sums = jnp.where(row == 3 + h, dot(ones, out_ref[h], 1, 1), sums)
    sum_scr[:, : 3 * HD] += sums

    @pl.when(step == pl.num_programs(0) - 1)
    def _():
        size, size_two = 3 * height // GROUP, height // GROUP
        top = size + size_two
        for rel in range(4):
            for source, ref in enumerate((mine_ref, send_ref)):
                owner = place_ref[2 * rel + source]
                ref[rel, :size, :] = grad_scr[pl.ds(pl.multiple_of(owner * size, 8), size), :]
                start = pl.multiple_of(owner * size_two, 8)
                ref[rel, size:top, :] = dwo_ref[pl.ds(start, size_two), :]
                ref[rel, top : top + 8, :] = jnp.where(
                    owner == 0, small_ref[...] + sum_scr[...], 0.0
                )
                ref[rel, top + 8 :, :] = jnp.where(owner == 0, early_ref[...], 0.0)


def attend_back_own(length, place, qkv, ctx, aug, grad, kf, inputs, dwo, small, early):
    height, width = dwo.shape
    heads = height // HD
    tokens = inputs.shape[0]
    share = 4 * height // GROUP + 16
    return pl.pallas_call(
        attend_back_own_kernel,
        grid_spec=pltpu.PrefetchScalarGridSpec(
            num_scalar_prefetch=1,
            grid=(tokens // length,),
            in_specs=[
                own_block(heads, 3 * HD, length),
                own_block(heads, HD, length),
                own_block(heads, EXTRA, length),
                own_block(heads, HD, length),
                pl.BlockSpec((EXTRA, length), lambda i, *_: (0, i)),
                pl.BlockSpec((length, width), lambda i, *_: (i, 0)),
                whole(dwo.shape),
                whole(small.shape),
                whole(early.shape),
            ],
            out_specs=[
                own_block(heads, 3 * HD, length),
                whole((4, share, width)),
                whole((4, share, width)),
            ],
            scratch_shapes=[pltpu.VMEM((3 * height, width), F32), pltpu.VMEM((8, width), F32)],
        ),
        out_shape=[jax.ShapeDtypeStruct(qkv.shape, BF16)]
        + [jax.ShapeDtypeStruct((4, share, width), F32)] * 2,
        compiler_params=params(),
        cost_estimate=cost(heads * tokens * (20 * 64 * length + 6 * HD * width), 12e6),
        name="attend_back_own",
    )(place, qkv, ctx, aug, grad, kf, inputs, dwo, small, early)


def attend_back_kernel(place_ref, qkv_ref, ctx_ref, aug_ref, grad_ref, kf_ref, old_ref, out_ref):
    attend_back_rows(qkv_ref, ctx_ref, aug_ref, grad_ref, kf_ref, out_ref)


def attend_back(length, peers, first, count, place, qkv, ctx, aug, grad, kf, out):
    every, _, tokens = qkv.shape
    heads = every // peers
    by_peer = lambda n: peer_block(peers, first, heads, n, length)
    return pl.pallas_call(
        attend_back_kernel,
        grid_spec=pltpu.PrefetchScalarGridSpec(
            num_scalar_prefetch=1,
            grid=(count, tokens // length),
            in_specs=[
                by_peer(3 * HD),
                by_peer(HD),
                by_peer(EXTRA),
                by_peer(HD),
                pl.BlockSpec((EXTRA, length), lambda k, i, *_: (0, i)),
                ANY,
            ],
            out_specs=by_peer(3 * HD),
        ),
        out_shape=jax.ShapeDtypeStruct(out.shape, BF16),
        input_output_aliases={6: 0},
        compiler_params=params(),
        cost_estimate=cost(count * heads * tokens * 20 * 64 * length, 12e6),
        name="attend_back",
    )(place, qkv, ctx, aug, grad, kf, out)


def norm_forward(hidden):
    center = hidden - jnp.mean(hidden, axis=-1, keepdims=True)
    inverse = lax.rsqrt(jnp.mean(center * center, axis=-1, keepdims=True) + EPS)
    return center * inverse, inverse


def norm_backward(grad, gain, norm, inverse):
    scaled = grad * gain
    first = jnp.mean(scaled, axis=-1, keepdims=True)
    second = jnp.mean(scaled * norm, axis=-1, keepdims=True)
    return (scaled - first - norm * second) * inverse


def column_sum(values):
    return jnp.sum(values, axis=0, keepdims=True)


def flat(values):
    return values.reshape(-1, values.shape[-1])


def attended_kernel(x_ref, ctx_ref, wo_ref, vec_ref, sum_ref, low_ref):
    b_output, gain_one, shift_one = vec_ref[0:1], vec_ref[1:2], vec_ref[2:3]
    half = x_ref.shape[0] // 2
    halves = [slice(0, half), slice(half, 2 * half)]
    attended = [dot(flat(ctx_ref[:, :, at]), wo_ref[...], 0, 0) for at in halves]
    for at, part in zip(halves, attended):
        residual = x_ref[at, :].astype(F32) + (part + b_output)
        sum_ref[at, :] = residual
        norm_one, _ = norm_forward(residual)
        low_ref[at, :] = (norm_one * gain_one + shift_one).astype(BF16)


def add_attended(inputs, ctx, w_output, vectors):
    tokens, width = inputs.shape
    every = ctx.shape[0]
    block = 512
    by_token = lambda: pl.BlockSpec((block, width), lambda i: (i, 0))
    return pl.pallas_call(
        attended_kernel,
        grid=(tokens // block,),
        in_specs=[
            by_token(),
            pl.BlockSpec((every, HD, block), lambda i: (0, 0, i)),
            whole(w_output.shape),
            whole(vectors.shape),
        ],
        out_specs=[by_token(), by_token()],
        out_shape=[
            jax.ShapeDtypeStruct((tokens, width), F32),
            jax.ShapeDtypeStruct((tokens, width), BF16),
        ],
        compiler_params=params(),
        cost_estimate=cost(2 * tokens * width * every * HD, 17e6),
        name="add_attended",
    )(inputs, ctx, w_output, vectors)


def fill(place_ref, own_ref, parts, spots, out_ref):
    shards, height, _ = out_ref.shape
    out_ref[place_ref[GROUP]] = own_ref[...]
    for k in range(1, shards):
        shard = peer_shard(place_ref, shards, k)
        for ref, (index, offset) in zip(parts, spots):
            start = place_ref[index] * (height // GROUP) + offset
            put(out_ref.at[shard], start, ref[k - 1], 16)


def expand_kernel(spots, place_ref, low_ref, bias_ref, own_ref, *refs):
    parts, (act_ref, slope_ref, full_ref, we_ref, sem) = refs[: len(spots)], refs[len(spots) :]
    shards = we_ref.shape[0]
    kept = pltpu.make_async_copy(we_ref, full_ref, sem)

    @pl.when(pl.program_id(0) == 0)
    def _():
        fill(place_ref, own_ref, parts, spots, we_ref)
        kept.start()

    @pl.when(pl.program_id(0) == pl.num_programs(0) - 1)
    def _():
        kept.wait()

    half = low_ref.shape[0] // 2
    halves = [slice(0, half), slice(half, 2 * half)]
    items = [(s, at) for s in range(shards) for at in halves]
    ahead = dot(low_ref[halves[0], :], we_ref[0], 1, 0)
    for n, (s, at) in enumerate(items):
        hidden = ahead + bias_ref[peer_shard(place_ref, shards, s), 1:2]
        if n + 1 < len(items):
            s_next, at_next = items[n + 1]
            ahead = dot(low_ref[at_next, :], we_ref[s_next], 1, 0)
        square = hidden * hidden
        bent = jnp.tanh(hidden * (0.7978845608028654 + 0.035677408136300125 * square))
        gate = 0.5 + 0.5 * bent
        active = hidden * gate
        act_ref[s, at, :] = active.astype(BF16)
        slope = gate + (active * (1.0 - gate)) * (1.5957691216057308 + 0.21406444881780075 * square)
        slope_ref[s, at, :] = slope.astype(BF16)


def expand(place, low, biases, own, pieces, shards):
    tokens, width = low.shape
    hidden = own.shape[1]
    block = 512
    spots = [(index, offset) for _, index, offset in pieces]
    parts = [array for array, _, _ in pieces]
    full = (shards, width, hidden)
    by_shard = lambda: pl.BlockSpec((shards, block, hidden), lambda i, *_: (0, i, 0))
    return pl.pallas_call(
        lambda *refs: expand_kernel(spots, *refs),
        grid_spec=pltpu.PrefetchScalarGridSpec(
            num_scalar_prefetch=1,
            grid=(tokens // block,),
            in_specs=[
                pl.BlockSpec((block, width), lambda i, *_: (i, 0)),
                whole(biases.shape),
                whole(own.shape),
                *[whole(a.shape) for a in parts],
            ],
            out_specs=[by_shard(), by_shard(), ANY],
            scratch_shapes=[pltpu.VMEM(full, BF16), pltpu.SemaphoreType.DMA],
        ),
        out_shape=[
            jax.ShapeDtypeStruct((shards, tokens, hidden), BF16),
            jax.ShapeDtypeStruct((shards, tokens, hidden), BF16),
            jax.ShapeDtypeStruct(full, BF16),
        ],
        compiler_params=params(),
        cost_estimate=cost(2 * tokens * width * shards * hidden, 40e6),
        name="expand",
    )(place, low, biases, own, *parts)


def reduce_kernel(spots, place_ref, sum_ref, cot_ref, act_ref, slope_ref, vec_ref, *refs):
    own_ref, refs = refs[0], refs[1:]
    piece_refs, refs = refs[: len(spots)], refs[len(spots) :]
    out_ref, g2_ref, full_ref, mine_ref, send_ref, small_scr = refs[:6]
    dwe_scr, dwr_scr, wr_ref, sems = refs[6:]
    kept = pltpu.make_async_copy(wr_ref, full_ref, sems.at[0])
    step = pl.program_id(0)
    shards = act_ref.shape[0]
    me = place_ref[GROUP]

    @pl.when(step == 0)
    def _():
        fill(place_ref, own_ref, piece_refs, spots, wr_ref)
        kept.start()
        for scr in (dwe_scr, dwr_scr, small_scr):
            scr[...] = jnp.zeros_like(scr)

    gain_one, shift_one = vec_ref[1:2], vec_ref[2:3]
    b_reduce, gain_two, shift_two = vec_ref[3:4], vec_ref[4:5], vec_ref[5:6]
    half = sum_ref.shape[0] // 2
    halves = [slice(0, half), slice(half, 2 * half)]
    mixed = []
    for at in halves:
        part = dot(act_ref[0, at, :], wr_ref[0], 1, 0)
        for s in range(1, shards):
            part = part + dot(act_ref[s, at, :], wr_ref[s], 1, 0)
        mixed.append(part)
    small = [jnp.zeros((1, sum_ref.shape[1]), F32)] * 4
    low, normed_low, active = [], [], []
    for at, part in zip(halves, mixed):
        norm_one, _ = norm_forward(sum_ref[at, :])
        normed = norm_one * gain_one + shift_one
        normed_low.append(normed.astype(BF16))
        norm_two, inverse_two = norm_forward(normed + (part + b_reduce))
        out_ref[at, :] = (norm_two * gain_two + shift_two).astype(BF16)
        cot = cot_ref[at, :].astype(F32)
        grad_two = norm_backward(cot, gain_two, norm_two, inverse_two)
        g2_ref[at, :] = grad_two
        low.append(grad_two.astype(BF16))
        active.append(dot(low[-1], own_ref[...], 1, 1))
        small[0] = small[0] + column_sum(grad_two)
        small[1] = small[1] + column_sum(cot * norm_two)
        small[2] = small[2] + column_sum(cot)
    dwr_scr[...] += dot(act_ref[me], jnp.concatenate(low, axis=0), 0, 0)
    own = []
    for at, part in zip(halves, active):
        own.append((part * slope_ref[0, at, :].astype(F32)).astype(BF16))
        small[3] = small[3] + column_sum(own[-1].astype(F32))
    dwe_scr[...] += dot(
        jnp.concatenate(normed_low, axis=0), jnp.concatenate(own, axis=0), 0, 0
    )
    for n, part in enumerate(small):
        small_scr[n : n + 1] += part

    @pl.when(step == pl.num_programs(0) - 1)
    def _():
        copies = [kept]
        for plane in range(4):
            for ref, core in ((send_ref, place_ref[1]), (mine_ref, place_ref[0])):
                owner = 2 * plane + lax.rem(core, 2)
                top = 0
                for scr in (dwe_scr, dwr_scr):
                    size = scr.shape[0] // GROUP
                    start = pl.multiple_of(owner * size, 8)
                    copy = pltpu.make_async_copy(
                        scr.at[pl.ds(start, size), :],
                        ref.at[plane, top : top + size, :],
                        sems.at[len(copies)],
                    )
                    copy.start()
                    copies.append(copy)
                    top += size
        for copy in copies:
            copy.wait()


def reduce(place, residual, cot, act, slope, vectors, own, pieces):
    tokens, width = residual.shape
    shards, _, hidden = act.shape
    block = 512
    share = (width + hidden) // GROUP
    spots = [(index, offset) for _, index, offset in pieces]
    arrays = [array for array, _, _ in pieces]
    by_token = lambda: pl.BlockSpec((block, width), lambda i, *_: (i, 0))
    return pl.pallas_call(
        lambda *refs: reduce_kernel(spots, *refs),
        grid_spec=pltpu.PrefetchScalarGridSpec(
            num_scalar_prefetch=1,
            grid=(tokens // block,),
            in_specs=[
                by_token(),
                by_token(),
                pl.BlockSpec((shards, block, hidden), lambda i, *_: (0, i, 0)),
                pl.BlockSpec((1, block, hidden), lambda i, p: (p[GROUP], i, 0)),
                whole(vectors.shape),
                whole(own.shape),
                *[whole(a.shape) for a in arrays],
            ],
            out_specs=[
                by_token(),
                by_token(),
                ANY,
                ANY,
                ANY,
                whole((8, width)),
            ],
            scratch_shapes=[
                pltpu.VMEM((width, hidden), F32),
                pltpu.VMEM((hidden, width), F32),
                pltpu.VMEM((shards, hidden, width), BF16),
                pltpu.SemaphoreType.DMA((17,)),
            ],
        ),
        out_shape=[
            jax.ShapeDtypeStruct((tokens, width), BF16),
            jax.ShapeDtypeStruct((tokens, width), F32),
            jax.ShapeDtypeStruct((shards, hidden, width), BF16),
            jax.ShapeDtypeStruct((4, share, width), F32),
            jax.ShapeDtypeStruct((4, share, width), F32),
            jax.ShapeDtypeStruct((8, width), F32),
        ],
        compiler_params=params(),
        cost_estimate=cost(tokens * width * hidden * (2 * shards + 6), 40e6),
        name="reduce",
    )(place, residual, cot, act, slope, vectors, own, *arrays)


def return_kernel(place_ref, sum_ref, g2_ref, slope_ref, ctx_ref, we_ref, wr_ref, w_ref, *refs):
    vec_ref, g1_ref, dctx_ref, dwo_ref, small_ref = refs
    shards = we_ref.shape[0]

    @pl.when(pl.program_id(0) == 0)
    def _():
        dwo_ref[...] = jnp.zeros_like(dwo_ref)
        small_ref[...] = jnp.zeros_like(small_ref)

    half = sum_ref.shape[0] // 2
    halves = [slice(0, half), slice(half, 2 * half)]
    gain_one = vec_ref[1:2]
    low = [g2_ref[at, :].astype(BF16) for at in halves]
    items = [(s, i) for s in range(shards) for i in range(2)]
    total = [g2_ref[at, :] for at in halves]
    ahead = dot(low[0], wr_ref[0], 1, 1)
    for n, (s, i) in enumerate(items):
        grad_active = ahead
        if n + 1 < len(items):
            s_next, i_next = items[n + 1]
            ahead = dot(low[i_next], wr_ref[s_next], 1, 1)
        grad_hidden = (grad_active * slope_ref[s, halves[i], :].astype(F32)).astype(BF16)
        total[i] = total[i] + dot(grad_hidden, we_ref[s], 1, 1)
    small = [jnp.zeros((1, sum_ref.shape[1]), F32)] * 3
    one = []
    for at, grad_normed in zip(halves, total):
        norm_one, inverse_one = norm_forward(sum_ref[at, :])
        grad_one = norm_backward(grad_normed, gain_one, norm_one, inverse_one)
        g1_ref[at, :] = grad_one
        one.append(grad_one.astype(BF16))
        small[0] = small[0] + column_sum(grad_one)
        small[1] = small[1] + column_sum(grad_normed * norm_one)
        small[2] = small[2] + column_sum(grad_normed)
    one = jnp.concatenate(one, axis=0)
    dctx = dot(w_ref[...], one, 1, 1)
    dwo_ref[...] += dot(flat(ctx_ref[...]), one, 1, 0)
    dctx_ref[...] = dctx.astype(BF16).reshape(dctx_ref.shape)
    for n, part in enumerate(small):
        small_ref[n : n + 1] += part


def back_to_context(place, residual, grad_two, slope, ctx, w_expand, w_reduce, weights, vectors):
    tokens, width = residual.shape
    shards, _, hidden = w_expand.shape
    every = ctx.shape[0]
    heads = every // shards
    block = 512
    by_token = lambda: pl.BlockSpec((block, width), lambda i, *_: (i, 0))
    return pl.pallas_call(
        return_kernel,
        grid_spec=pltpu.PrefetchScalarGridSpec(
            num_scalar_prefetch=1,
            grid=(tokens // block,),
            in_specs=[
                by_token(),
                by_token(),
                pl.BlockSpec((shards, block, hidden), lambda i, *_: (0, i, 0)),
                own_block(heads, HD, block),
                whole(w_expand.shape),
                whole(w_reduce.shape),
                whole(weights.shape),
                whole(vectors.shape),
            ],
            out_specs=[
                by_token(),
                pl.BlockSpec((every, HD, block), lambda i, *_: (0, 0, i)),
                whole((heads * HD, width)),
                whole((8, width)),
            ],
        ),
        out_shape=[
            jax.ShapeDtypeStruct((tokens, width), F32),
            jax.ShapeDtypeStruct(ctx.shape, BF16),
            jax.ShapeDtypeStruct((heads * HD, width), F32),
            jax.ShapeDtypeStruct((8, width), F32),
        ],
        compiler_params=params(),
        cost_estimate=cost(tokens * width * (4 * shards * hidden + 2 * every * HD), 40e6),
        name="back_to_context",
    )(place, residual, grad_two, slope, ctx, w_expand, w_reduce, weights, vectors)


def spread_kernel(spots, place_ref, *refs):
    parts, outs = refs[: len(spots)], refs[len(spots) :]
    for ref, (index, offset) in zip(parts, spots):
        start = 0
        for i, out_ref in enumerate(outs):
            size = out_ref.shape[0] // GROUP
            if offset <= i * size < offset + ref.shape[1]:
                put(out_ref, place_ref[index] * size, ref[0, start : start + size, :], 8)
                start += size


def spread(place, pieces, sizes):
    spots = [(index, offset) for _, index, offset in pieces]
    parts = [array for array, _, _ in pieces]
    width = parts[0].shape[2]
    shapes = [(GROUP * size, width) for size in sizes]
    return pl.pallas_call(
        lambda *refs: spread_kernel(spots, *refs),
        grid_spec=pltpu.PrefetchScalarGridSpec(
            num_scalar_prefetch=1,
            grid=(1,),
            in_specs=[whole(a.shape) for a in parts],
            out_specs=[whole(s) for s in shapes],
        ),
        out_shape=[jax.ShapeDtypeStruct(s, F32) for s in shapes],
        compiler_params=params(),
        cost_estimate=cost(0, 10e6),
        name="spread",
    )(place, *parts)


def spread_late_kernel(heads, place_ref, *refs):
    parts = refs[:GROUP]
    dq_ref, dk_ref, dv_ref, dwo_ref, small_ref, grad_scr = refs[GROUP:]
    height = heads * HD
    size, size_two = 3 * height // GROUP, height // GROUP
    top = size + size_two
    for i, ref in enumerate(parts):
        owner = place_ref[i]
        put(grad_scr, owner * size, ref[:size, :], 8)
        put(dwo_ref, owner * size_two, ref[size:top, :], 8)

        @pl.when(owner == 0)
        def _():
            small_ref[...] = ref[top:, :]

    for i, out_ref in enumerate((dq_ref, dk_ref, dv_ref)):
        out_ref[...] = grad_scr[i * height : (i + 1) * height, :]


def spread_late(place, parts, heads):
    share, width = parts[0].shape
    height = heads * HD
    shapes = [(height, width)] * 4 + [(16, width)]
    return pl.pallas_call(
        lambda *refs: spread_late_kernel(heads, *refs),
        grid_spec=pltpu.PrefetchScalarGridSpec(
            num_scalar_prefetch=1,
            grid=(1,),
            in_specs=[whole(a.shape) for a in parts],
            out_specs=[whole(s) for s in shapes],
            scratch_shapes=[pltpu.VMEM((3 * height, width), F32)],
        ),
        out_shape=[jax.ShapeDtypeStruct(s, F32) for s in shapes],
        compiler_params=params(),
        cost_estimate=cost(0, 8 * parts[0].size * 8),
        name="spread_late",
    )(place, *parts)


def input_grads_kernel(place_ref, g1_ref, grad_ref, w_ref, out_ref):
    amount = place_ref[GROUP + 1 + pl.program_id(0)]
    matrix = shift_matrix(amount, g1_ref.shape[0], False)
    total = g1_ref[...] + dot(flat(grad_ref[...]), w_ref[...], 0, 0)
    out_ref[...] = dot(matrix, total.astype(BF16), 1, 0).astype(BF16)


def input_grads(place, length, grad_one, grads, weights):
    tokens, width = grad_one.shape
    every = grads.shape[0]
    by_row = lambda: pl.BlockSpec((length, width), lambda i, *_: (i, 0))
    return pl.pallas_call(
        input_grads_kernel,
        grid_spec=pltpu.PrefetchScalarGridSpec(
            num_scalar_prefetch=1,
            grid=(tokens // length,),
            in_specs=[
                by_row(),
                pl.BlockSpec((every, 3 * HD, length), lambda i, *_: (0, 0, i)),
                whole(weights.shape),
            ],
            out_specs=by_row(),
        ),
        out_shape=jax.ShapeDtypeStruct((tokens, width), BF16),
        compiler_params=params(),
        cost_estimate=cost(2 * tokens * width * (every * 3 * HD + length), 20e6),
        name="input_grads",
    )(place, grad_one, grads, weights)


def after(values, *others):
    return lax.optimization_barrier((values, others))[0]


def solution(mesh):
    peers = mesh.shape["mp"]
    lanes = mesh.shape["dp"]
    rotations = [[(i, (i + k) % peers) for i in range(peers)] for k in range(1, peers)]

    def flip(values, bits):
        return lax.ppermute(values, "dp", [(i, i ^ bits) for i in range(lanes)])

    def from_peers(piece):
        return jnp.stack([lax.ppermute(piece, "mp", perm) for perm in rotations])

    def swapped(piece, *ready):
        copies = jnp.broadcast_to(piece[None], (peers,) + piece.shape)
        got = lax.all_to_all(after(copies, *ready), "mp", 0, 0, tiled=True)
        me = lax.axis_index("mp")
        return jnp.concatenate(
            [
                lax.dynamic_slice_in_dim(got, lax.rem(me + peers - k, peers), 1, 0)
                for k in range(1, peers)
            ]
        )

    def both(near):
        return flip(near, 2), flip(near, 4)

    def corner(by_x, by_y, cut):
        return flip(by_y[:, :cut], 2), flip(by_x[:, cut:], 4)

    def listed(near, by_x, by_y, first, second, cut):
        places = ((near, 0, 0), (by_x, 1, 0), (by_y, 2, 0), (first, 3, 0), (second, 3, cut))
        return with_core(places)

    def with_core(places):
        out = []
        for array, rel, offset in places:
            out.append((array, 2 * rel, offset))
            out.append((flip(array, 1), 2 * rel + 1, offset))
        return out

    planes = [[g + c + i for i in (0, 2, 4, 6)] for g in range(0, lanes, GROUP) for c in (0, 1)]

    def swap_plane(values):
        return lax.all_to_all(values, "dp", 0, 0, tiled=True, axis_index_groups=planes)

    def sum_groups(total):
        step = GROUP
        while step < lanes:
            total = total + flip(total, step)
            step *= 2
        return total

    def partial_sums(mine, got, *ready):
        got = after(got, *ready)
        return [mine[rel] + got[rel] for rel in range(4)]

    def exchange(parts):
        return [flip(parts[rel], 2 * rel) for rel in (1, 2, 3)]

    def total_of(first, rest, *ready):
        rest = after(rest, *ready)
        return sum_groups(first + rest[0] + rest[1] + rest[2])

    def finish(arrays, *ready):
        out = []
        for array in after(arrays, *ready):
            out += [array, flip(array, 1)]
        return out

    def local(
        tokens,
        doc_lengths,
        w_query,
        b_query,
        w_key,
        w_value,
        b_value,
        w_output,
        b_output,
        gain_attn,
        shift_attn,
        w_expand,
        b_expand,
        w_reduce,
        b_reduce,
        gain_ffn,
        shift_ffn,
        cotangent,
    ):
        row_count, length, width = tokens.shape
        heads = w_query.shape[1] // HD
        hidden = w_expand.shape[1]
        count = row_count * length
        inside = lax.axis_index("dp") % GROUP
        me = lax.axis_index("mp")
        ends = jnp.cumsum(doc_lengths, axis=-1)
        longest = jnp.max(doc_lengths, axis=-1, keepdims=True)
        offset = jnp.max(jnp.where(doc_lengths == longest, ends - doc_lengths, 0), axis=-1)
        place = jnp.stack([inside ^ i for i in range(GROUP)] + [me])
        place = jnp.concatenate([place, offset]).astype(jnp.int32)

        by_head = lambda w: w.T.reshape(heads, HD, width)
        own_heads = jnp.concatenate([by_head(w_query), by_head(w_key), by_head(w_value)], axis=1)
        own_heads = jnp.concatenate([own_heads.reshape(3 * heads * HD, width), w_output])
        blank = jnp.zeros((width - 2 * heads * HD,), BF16)
        own_bias = jnp.stack(
            [jnp.concatenate([b_query, b_value, blank]), b_expand]
            + [jnp.zeros((width,), BF16)] * 6
        ).astype(F32)

        def piece_of(array, bits=0):
            size = array.shape[0] // GROUP
            return lax.dynamic_slice_in_dim(array, (inside ^ bits) * size, size, 0).astype(F32)

        piece = piece_of(own_heads)
        near = from_peers(jnp.concatenate([piece, own_bias]))

        def columns(rows):
            parts = rows[:, 0, : 2 * heads * HD].reshape(-1, 2, heads, HD)
            blank = jnp.zeros((rows.shape[0], heads, HD), F32)
            return jnp.concatenate([parts[:, 0], blank, parts[:, 1]], axis=-1)[..., None]

        position = (jnp.arange(length, dtype=jnp.int32)[None] + offset[:, None]) % length
        segment = jnp.sum((position[:, :, None] >= ends[:, None, :]).astype(jnp.int32), axis=-1)
        segment = segment.reshape(1, count)
        docs = doc_lengths.shape[1]
        label = jnp.arange(EXTRA, dtype=jnp.int32)[:, None]
        is_doc = label < docs
        qf = jnp.where(is_doc & (segment == label), 1.0, 0.0).astype(BF16)
        kf = jnp.where(
            is_doc,
            jnp.where(segment == label, 0.0, MASK),
            jnp.where(label < docs + 3, 1.0, 0.0),
        ).astype(BF16)
        inputs, cot = shift(
            place, length, tokens.reshape(count, width), cotangent.reshape(count, width)
        )
        own = attend_own(
            length, peers, place, inputs, columns(own_bias[None])[0], qf, kf, own_heads
        )

        near = after(near, own)
        biases = near[:, -own_bias.shape[0] :]
        peer_columns = columns(biases)
        biases = jnp.concatenate([own_bias[None], biases])
        near = near[:, : -own_bias.shape[0]]
        cut = piece.shape[0] // 2
        near_expand = swapped(piece_of(w_expand), near)
        sides = both(near)
        corners = corner(*sides, cut)
        pieces = listed(near, *sides, *corners, cut)
        near_reduce = swapped(piece_of(w_reduce), near_expand)
        sides_expand = both(after(near_expand, corners))
        weights, all_output, qkv, ctx, aug = attend_peers(
            length, peers, place, inputs, after(peer_columns, near_expand), qf, kf, pieces, own
        )

        sides_expand = after(sides_expand, ctx)
        cut = width // GROUP // 2
        corners = corner(*sides_expand, cut)
        vectors = jnp.stack(
            [b_output, gain_attn, shift_attn, b_reduce, gain_ffn, shift_ffn]
            + [jnp.zeros((width,), BF16)] * 2
        ).astype(F32)
        residual, low = add_attended(inputs, ctx, all_output, after(vectors, sides_expand))
        near_reduce, corners = after((near_reduce, corners), low)
        pieces = listed(near_expand, *sides_expand, *corners, cut)
        sides_reduce = both(near_reduce)
        diagonal = swapped(piece_of(w_reduce, 6), near_reduce)
        act, slope, all_expand = expand(
            place, low, after(biases, near_reduce), w_expand, pieces, peers
        )
        far_reduce = after((*sides_reduce, diagonal), act)
        pieces = with_core([(array, rel, 0) for rel, array in enumerate([near_reduce, *far_reduce])])
        shifted, grad_two, all_reduce, mine, send, small_one = reduce(
            place, residual, cot, act, slope, vectors, w_reduce, pieces
        )
        got = flip(send, 1)
        output = unshift(place, length, shifted)
        chip = mine + after(got, output)
        early = swap_plane(chip)
        grad_one, dctx, dwo, small = back_to_context(
            place,
            residual,
            grad_two,
            slope,
            ctx,
            all_expand,
            all_reduce,
            all_output,
            after(vectors, chip),
        )
        cut = width // GROUP
        early = sum_groups(jnp.sum(after(early, grad_one), axis=0))[None]
        sides = both(early)
        dqkv, mine, send = attend_back_own(
            length, place, qkv, ctx, aug, dctx, after(kf, early), inputs, dwo, small, small_one
        )
        got = flip(after(send, sides), 1)
        dqkv = attend_back(
            length, peers, 1, 1, place, qkv, ctx, aug, dctx, after(kf, sides), dqkv
        )
        corners = corner(*sides, cut)
        beside = [flip(array, 1) for array in (early, *sides)]
        parts = partial_sums(mine, got, dqkv)
        rest = exchange(parts)
        corners, beside, kept = after((corners, beside, kf), parts)
        dqkv = attend_back(length, peers, 2, peers - 2, place, qkv, ctx, aug, dctx, kept, dqkv)
        total = total_of(parts[0], rest, dqkv)
        second = [total] + exchange([None] + [total] * 3)
        beside += [flip(array, 1) for array in corners]
        pieces = []
        spots = ((0, 0), (2, 0), (4, 0), (6, 0), (6, cut))
        for near, far, (index, top) in zip((early, *sides, *corners), beside, spots):
            pieces += [(near, index, top), (far, index + 1, top)]
        grad_one = after(grad_one, total, beside)
        grad_tokens = input_grads(place, length, grad_one, dqkv, weights)
        second = finish(second, grad_tokens)
        dwe, dwr = spread(place, pieces, [width // GROUP, hidden // GROUP])
        dq, dk, dv, dwo, small_two = spread_late(place, second, heads)
        sums = lambda i: small_two[3 : 3 + heads, i * HD : (i + 1) * HD].reshape(heads * HD)
        shape = (row_count, length, width)
        return (
            output.reshape(shape),
            grad_tokens.reshape(shape),
            dq.T,
            sums(0),
            dk.T,
            dv.T,
            sums(2),
            dwo,
            small_two[0],
            small_two[1],
            small_two[2],
            dwe,
            small_two[11],
            dwr,
            small_two[8],
            small_two[9],
            small_two[10],
        )

    rows, split = P("dp", None, None), P(None, "mp")
    return jax.shard_map(
        local,
        mesh=mesh,
        in_specs=(
            rows,
            P("dp", None),
            split,
            P("mp"),
            split,
            split,
            P("mp"),
            P("mp", None),
            P(),
            P(),
            P(),
            split,
            P("mp"),
            P("mp", None),
            P(),
            P(),
            P(),
            rows,
        ),
        out_specs=(
            rows,
            rows,
            split,
            P("mp"),
            split,
            split,
            P("mp"),
            P("mp", None),
            P(),
            P(),
            P(),
            split,
            P("mp"),
            P("mp", None),
            P(),
            P(),
            P(),
        ),
        check_vma=False,
    )
```

```python
import jax
import jax.numpy as jnp
from jax import lax
from jax.experimental import pallas as pl
from jax.experimental.pallas import tpu as pltpu
from jax.sharding import PartitionSpec as P

HD = 64
GROUP = 8
EXTRA = 16
MASK = -float(2**30)
EPS = 1e-12
F32 = jnp.float32
BF16 = jnp.bfloat16
LIMIT = 60 << 20


def dot(left, right, left_dim, right_dim):
    return lax.dot_general(
        left, right, (((left_dim,), (right_dim,)), ((), ())), preferred_element_type=F32
    )


def params():
    return pltpu.CompilerParams(vmem_limit_bytes=LIMIT)


def cost(flops, moved):
    return pl.CostEstimate(flops=int(flops), bytes_accessed=int(moved), transcendentals=0)


def whole(shape):
    zeros = (0,) * len(shape)
    return pl.BlockSpec(shape, lambda *_: zeros, pipeline_mode=pl.Buffered(1))


def split3(row):
    high = row.astype(BF16).astype(F32)
    rest = row - high
    mid = rest.astype(BF16).astype(F32)
    return high, mid, rest - mid


def rows_of(height, first, parts, width):
    place = lax.broadcasted_iota(jnp.int32, (height, width), 0)
    out = jnp.zeros((height, width), F32)
    for i, part in enumerate(parts):
        out = jnp.where(place == first + i, part, out)
    return out


def put(out_ref, start, values, step):
    rows = pl.ds(pl.multiple_of(start, step), values.shape[0])
    out_ref[rows, :] = values.astype(out_ref.dtype)


def peer_shard(place_ref, shards, k):
    return lax.rem(place_ref[GROUP] + shards - k, shards)


def own_block(*shape):
    return pl.BlockSpec(shape, lambda i, p: (p[GROUP],) + (0,) * (len(shape) - 2) + (i,))


def peer_block(peers, first, *shape):
    middle = (0,) * (len(shape) - 2)
    return pl.BlockSpec(
        shape, lambda k, i, p: (lax.rem(p[GROUP] + peers - first - k, peers),) + middle + (i,)
    )


ANY = pl.BlockSpec(memory_space=pl.ANY)


def shift_matrix(amount, length, forward):
    row = lax.broadcasted_iota(jnp.int32, (length, length), 0)
    column = lax.broadcasted_iota(jnp.int32, (length, length), 1)
    apart = column - row if forward else row - column
    return jnp.where((apart == amount) | (apart == amount - length), 1.0, 0.0).astype(BF16)


def shift_kernel(place_ref, first_ref, second_ref, first_out, second_out):
    length = first_ref.shape[0]
    amount = place_ref[GROUP + 1 + pl.program_id(0)]
    matrix = shift_matrix(amount, length, True)
    first_out[...] = dot(matrix, first_ref[...], 1, 0).astype(BF16)
    second_out[...] = dot(matrix, second_ref[...], 1, 0).astype(BF16)


def shift(place, length, first, second):
    tokens, width = first.shape
    by_row = lambda: pl.BlockSpec((length, width), lambda i, *_: (i, 0))
    return pl.pallas_call(
        shift_kernel,
        grid_spec=pltpu.PrefetchScalarGridSpec(
            num_scalar_prefetch=1,
            grid=(tokens // length,),
            in_specs=[by_row(), by_row()],
            out_specs=[by_row(), by_row()],
        ),
        out_shape=[jax.ShapeDtypeStruct((tokens, width), BF16)] * 2,
        compiler_params=params(),
        cost_estimate=cost(4 * tokens * length * width, 12e6),
        name="shift",
    )(place, first, second)


def unshift_kernel(place_ref, in_ref, out_ref):
    length = in_ref.shape[0]
    matrix = shift_matrix(place_ref[GROUP + 1 + pl.program_id(0)], length, False)
    out_ref[...] = dot(matrix, in_ref[...], 1, 0).astype(BF16)


def unshift(place, length, shifted):
    tokens, width = shifted.shape
    by_row = lambda: pl.BlockSpec((length, width), lambda i, *_: (i, 0))
    return pl.pallas_call(
        unshift_kernel,
        grid_spec=pltpu.PrefetchScalarGridSpec(
            num_scalar_prefetch=1,
            grid=(tokens // length,),
            in_specs=[by_row()],
            out_specs=by_row(),
        ),
        out_shape=jax.ShapeDtypeStruct((tokens, width), BF16),
        compiler_params=params(),
        cost_estimate=cost(2 * tokens * length * width, 6e6),
        name="unshift",
    )(place, shifted)


def tiles(heads, block):
    return [(h, slice(i * block, (i + 1) * block)) for h in range(heads) for i in range(2)]


def attend_rows(x_ref, bias_ref, qf_ref, kf_ref, w_scr, qkv_ref, ctx_ref, aug_ref):
    heads = ctx_ref.shape[0]
    length = x_ref.shape[0]
    block = length // 2
    span = 3 * HD
    proj = dot(w_scr[...], x_ref[...], 1, 1)
    scale = HD ** (-0.5)
    column = bias_ref[...].T[:, 0:1]
    for h in range(heads):
        part = proj[h * span : (h + 1) * span]
        queries = part[:HD] + column[h * HD : (h + 1) * HD]
        values = part[2 * HD :] + column[(heads + h) * HD : (heads + h + 1) * HD]
        qkv_ref[h, :HD, :] = (queries * scale).astype(BF16)
        qkv_ref[h, HD : 2 * HD, :] = part[HD : 2 * HD].astype(BF16)
        qkv_ref[h, 2 * HD :, :] = values.astype(BF16)
    ones_rows = rows_of(EXTRA, 0, (jnp.ones((1, block), F32),), block).astype(BF16)
    items = tiles(heads, block)
    scores = []
    for h, at in items:
        queries = jnp.concatenate([qkv_ref[h, :HD, at], qf_ref[:, at]], axis=0)
        keys = jnp.concatenate([qkv_ref[h, HD : 2 * HD, at], kf_ref[:, at]], axis=0)
        scores.append(dot(keys, queries, 0, 0))
    highest = [jnp.max(part, axis=0, keepdims=True) for part in scores]
    weight = [jnp.exp(part - top).astype(BF16) for part, top in zip(scores, highest)]
    context = []
    for (h, at), part in zip(items, weight):
        values = jnp.concatenate([qkv_ref[h, 2 * HD :, at], ones_rows], axis=0)
        context.append(dot(values, part, 1, 0))
    for (h, at), part, top in zip(items, context, highest):
        total = part[HD : HD + 1]
        ctx_ref[h, :, at] = (part[:HD] * (1.0 / total)).astype(BF16)
        log_total = top + jnp.log(total)
        extra = rows_of(EXTRA, 4, split3(-log_total), block)
        aug_ref[h, :, at] = (extra + qf_ref[:, at].astype(F32)).astype(BF16)


def attend_own_kernel(place_ref, x_ref, bias_ref, qf_ref, kf_ref, own_ref, *refs):
    w_ref, wo_ref, qkv_ref, ctx_ref, aug_ref = refs
    height = w_ref.shape[0]

    @pl.when(pl.program_id(0) == 0)
    def _():
        w_ref[...] = own_ref[:height, :]
        wo_ref[...] = own_ref[height:, :]

    attend_rows(x_ref, bias_ref, qf_ref, kf_ref, w_ref, qkv_ref, ctx_ref, aug_ref)


def attend_own(length, peers, place, inputs, bias, qf, kf, own):
    heads = own.shape[0] // (4 * HD)
    tokens, width = inputs.shape
    every = peers * heads
    shapes = [(every * 3 * HD, width), (every * HD, width)]
    shapes += [(every, n, tokens) for n in (3 * HD, HD, EXTRA)]
    by_row = pl.BlockSpec((EXTRA, length), lambda i, *_: (0, i))
    return pl.pallas_call(
        attend_own_kernel,
        grid_spec=pltpu.PrefetchScalarGridSpec(
            num_scalar_prefetch=1,
            grid=(tokens // length,),
            in_specs=[
                pl.BlockSpec((length, width), lambda i, *_: (i, 0)),
                whole(bias.shape),
                by_row,
                by_row,
                whole(own.shape),
            ],
            out_specs=[
                pl.BlockSpec((heads * 3 * HD, width), lambda i, p: (p[GROUP], 0)),
                pl.BlockSpec((heads * HD, width), lambda i, p: (p[GROUP], 0)),
                *[own_block(heads, n, length) for n in (3 * HD, HD, EXTRA)],
            ],
        ),
        out_shape=[jax.ShapeDtypeStruct(shape, BF16) for shape in shapes],
        compiler_params=params(),
        cost_estimate=cost(heads * tokens * (6 * HD * width + 16 * 64 * length), 12e6),
        name="attend_own",
    )(place, inputs, bias, qf, kf, own)


def attend_peers_kernel(spots, place_ref, x_ref, bias_ref, qf_ref, kf_ref, *refs):
    count = len(spots)
    parts = refs[:count]
    w_ref, wo_ref, qkv_ref, ctx_ref, aug_ref, w_scr = refs[count + 5 :]
    height = w_ref.shape[0]

    @pl.when(pl.program_id(1) == 0)
    def _():
        size = w_scr.shape[0] // GROUP
        for ref, (index, offset) in zip(parts, spots):
            put(w_scr, place_ref[index] * size + offset, ref[0], 16)
        w_ref[...] = w_scr[:height, :]
        wo_ref[...] = w_scr[height:, :]

    attend_rows(x_ref, bias_ref.at[0], qf_ref, kf_ref, w_ref, qkv_ref, ctx_ref, aug_ref)


def attend_peers(length, peers, place, inputs, bias, qf, kf, pieces, arrays):
    heads = arrays[2].shape[0] // peers
    tokens, width = inputs.shape
    spots = [(index, offset) for _, index, offset in pieces]
    parts = [array for array, _, _ in pieces]
    by_row = pl.BlockSpec((EXTRA, length), lambda k, i, *_: (0, i))
    return pl.pallas_call(
        lambda *refs: attend_peers_kernel(spots, *refs),
        grid_spec=pltpu.PrefetchScalarGridSpec(
            num_scalar_prefetch=1,
            grid=(peers - 1, tokens // length),
            in_specs=[
                pl.BlockSpec((length, width), lambda k, i, *_: (i, 0)),
                pl.BlockSpec((1,) + bias.shape[1:], lambda k, i, *_: (k, 0, 0)),
                by_row,
                by_row,
                *[
                    pl.BlockSpec((1,) + a.shape[1:], lambda k, i, *_: (k, 0, 0)) for a in parts
                ],
                *[ANY] * 5,
            ],
            out_specs=[
                *[
                    pl.BlockSpec(
                        (heads * n, width),
                        lambda k, i, p: (lax.rem(p[GROUP] + peers - 1 - k, peers), 0),
                    )
                    for n in (3 * HD, HD)
                ],
                *[peer_block(peers, 1, heads, n, length) for n in (3 * HD, HD, EXTRA)],
            ],
            scratch_shapes=[pltpu.VMEM((heads * 4 * HD, width), BF16)],
        ),
        out_shape=[jax.ShapeDtypeStruct(a.shape, a.dtype) for a in arrays],
        input_output_aliases={5 + len(parts) + i: i for i in range(5)},
        compiler_params=params(),
        cost_estimate=cost(
            (peers - 1) * heads * tokens * (6 * HD * width + 16 * 64 * length), 30e6
        ),
        name="attend_peers",
    )(place, inputs, bias, qf, kf, *parts, *arrays)


def attend_back_rows(qkv_ref, ctx_ref, aug_ref, grad_ref, kf_ref, out_ref):
    heads, _, length = ctx_ref.shape
    block = length // 2
    scale = HD ** (-0.5)
    one = jnp.ones((1, block), F32)
    ones_rows = rows_of(EXTRA, 0, (one, one, one), block).astype(BF16)
    items = tiles(heads, block)
    scores, spreads = [], []
    for h, at in items:
        scores.append(
            dot(
                jnp.concatenate([qkv_ref[h, HD : 2 * HD, at], kf_ref[:, at]], axis=0),
                jnp.concatenate([qkv_ref[h, :HD, at], aug_ref[h, :, at]], axis=0),
                0,
                0,
            )
        )
    for h, at in items:
        grad = grad_ref[h, :, at]
        inner = jnp.sum(grad.astype(F32) * ctx_ref[h, :, at].astype(F32), axis=0, keepdims=True)
        grad_extra = rows_of(EXTRA, 0, split3(-inner), block).astype(BF16)
        spreads.append(
            dot(
                jnp.concatenate([qkv_ref[h, 2 * HD :, at], ones_rows], axis=0),
                jnp.concatenate([grad, grad_extra], axis=0),
                0,
                0,
            )
        )
    probs = [jnp.exp(part) for part in scores]
    slopes = [(part * spread).astype(BF16) for part, spread in zip(probs, spreads)]
    probs = [part.astype(BF16) for part in probs]
    for (h, at), part in zip(items, probs):
        out_ref[h, 2 * HD :, at] = dot(grad_ref[h, :, at], part, 1, 1).astype(BF16)
    for (h, at), part in zip(items, slopes):
        out_ref[h, HD : 2 * HD, at] = dot(qkv_ref[h, :HD, at], part, 1, 1).astype(BF16)
    for (h, at), part in zip(items, slopes):
        grad = dot(qkv_ref[h, HD : 2 * HD, at], part, 1, 0)
        out_ref[h, :HD, at] = (grad * scale).astype(BF16)


def attend_back_own_kernel(place_ref, qkv_ref, ctx_ref, aug_ref, grad_ref, kf_ref, *refs):
    x_ref, dwo_ref, small_ref, early_ref, out_ref, mine_ref, send_ref, grad_scr, sum_scr = refs
    heads = ctx_ref.shape[0]
    height = heads * HD
    step = pl.program_id(0)

    @pl.when(step == 0)
    def _():
        grad_scr[...] = jnp.zeros_like(grad_scr)
        sum_scr[...] = jnp.zeros_like(sum_scr)

    attend_back_rows(qkv_ref, ctx_ref, aug_ref, grad_ref, kf_ref, out_ref)
    ones = jnp.ones((8, x_ref.shape[0]), BF16)
    row = lax.broadcasted_iota(jnp.int32, (8, 3 * HD), 0)
    sums = jnp.zeros((8, 3 * HD), F32)
    for h in range(heads):
        grad = dot(out_ref[h], x_ref[...], 1, 0)
        for i in range(3):
            grad_scr[i * height + h * HD : i * height + (h + 1) * HD, :] += grad[
                i * HD : (i + 1) * HD
            ]
        sums = jnp.where(row == 3 + h, dot(ones, out_ref[h], 1, 1), sums)
    sum_scr[:, : 3 * HD] += sums

    @pl.when(step == pl.num_programs(0) - 1)
    def _():
        size, size_two = 3 * height // GROUP, height // GROUP
        top = size + size_two
        for rel in range(4):
            for source, ref in enumerate((mine_ref, send_ref)):
                owner = place_ref[2 * rel + source]
                ref[rel, :size, :] = grad_scr[pl.ds(pl.multiple_of(owner * size, 8), size), :]
                start = pl.multiple_of(owner * size_two, 8)
                ref[rel, size:top, :] = dwo_ref[pl.ds(start, size_two), :]
                ref[rel, top : top + 8, :] = jnp.where(
                    owner == 0, small_ref[...] + sum_scr[...], 0.0
                )
                ref[rel, top + 8 :, :] = jnp.where(owner == 0, early_ref[...], 0.0)


def attend_back_own(length, place, qkv, ctx, aug, grad, kf, inputs, dwo, small, early):
    height, width = dwo.shape
    heads = height // HD
    tokens = inputs.shape[0]
    share = 4 * height // GROUP + 16
    return pl.pallas_call(
        attend_back_own_kernel,
        grid_spec=pltpu.PrefetchScalarGridSpec(
            num_scalar_prefetch=1,
            grid=(tokens // length,),
            in_specs=[
                own_block(heads, 3 * HD, length),
                own_block(heads, HD, length),
                own_block(heads, EXTRA, length),
                own_block(heads, HD, length),
                pl.BlockSpec((EXTRA, length), lambda i, *_: (0, i)),
                pl.BlockSpec((length, width), lambda i, *_: (i, 0)),
                whole(dwo.shape),
                whole(small.shape),
                whole(early.shape),
            ],
            out_specs=[
                own_block(heads, 3 * HD, length),
                whole((4, share, width)),
                whole((4, share, width)),
            ],
            scratch_shapes=[pltpu.VMEM((3 * height, width), F32), pltpu.VMEM((8, width), F32)],
        ),
        out_shape=[jax.ShapeDtypeStruct(qkv.shape, BF16)]
        + [jax.ShapeDtypeStruct((4, share, width), F32)] * 2,
        compiler_params=params(),
        cost_estimate=cost(heads * tokens * (20 * 64 * length + 6 * HD * width), 12e6),
        name="attend_back_own",
    )(place, qkv, ctx, aug, grad, kf, inputs, dwo, small, early)


def attend_back_kernel(place_ref, qkv_ref, ctx_ref, aug_ref, grad_ref, kf_ref, old_ref, out_ref):
    attend_back_rows(qkv_ref, ctx_ref, aug_ref, grad_ref, kf_ref, out_ref)


def attend_back(length, peers, first, count, place, qkv, ctx, aug, grad, kf, out):
    every, _, tokens = qkv.shape
    heads = every // peers
    by_peer = lambda n: peer_block(peers, first, heads, n, length)
    return pl.pallas_call(
        attend_back_kernel,
        grid_spec=pltpu.PrefetchScalarGridSpec(
            num_scalar_prefetch=1,
            grid=(count, tokens // length),
            in_specs=[
                by_peer(3 * HD),
                by_peer(HD),
                by_peer(EXTRA),
                by_peer(HD),
                pl.BlockSpec((EXTRA, length), lambda k, i, *_: (0, i)),
                ANY,
            ],
            out_specs=by_peer(3 * HD),
        ),
        out_shape=jax.ShapeDtypeStruct(out.shape, BF16),
        input_output_aliases={6: 0},
        compiler_params=params(),
        cost_estimate=cost(count * heads * tokens * 20 * 64 * length, 12e6),
        name="attend_back",
    )(place, qkv, ctx, aug, grad, kf, out)


def norm_forward(hidden):
    center = hidden - jnp.mean(hidden, axis=-1, keepdims=True)
    inverse = lax.rsqrt(jnp.mean(center * center, axis=-1, keepdims=True) + EPS)
    return center * inverse, inverse


def norm_backward(grad, gain, norm, inverse):
    scaled = grad * gain
    first = jnp.mean(scaled, axis=-1, keepdims=True)
    second = jnp.mean(scaled * norm, axis=-1, keepdims=True)
    return (scaled - first - norm * second) * inverse


def column_sum(values):
    return jnp.sum(values, axis=0, keepdims=True)


def flat(values):
    return values.reshape(-1, values.shape[-1])


def attended_kernel(x_ref, ctx_ref, wo_ref, vec_ref, sum_ref, low_ref):
    b_output, gain_one, shift_one = vec_ref[0:1], vec_ref[1:2], vec_ref[2:3]
    half = x_ref.shape[0] // 2
    halves = [slice(0, half), slice(half, 2 * half)]
    attended = [dot(flat(ctx_ref[:, :, at]), wo_ref[...], 0, 0) for at in halves]
    for at, part in zip(halves, attended):
        residual = x_ref[at, :].astype(F32) + (part + b_output)
        sum_ref[at, :] = residual
        norm_one, _ = norm_forward(residual)
        low_ref[at, :] = (norm_one * gain_one + shift_one).astype(BF16)


def add_attended(inputs, ctx, w_output, vectors):
    tokens, width = inputs.shape
    every = ctx.shape[0]
    block = 512
    by_token = lambda: pl.BlockSpec((block, width), lambda i: (i, 0))
    return pl.pallas_call(
        attended_kernel,
        grid=(tokens // block,),
        in_specs=[
            by_token(),
            pl.BlockSpec((every, HD, block), lambda i: (0, 0, i)),
            whole(w_output.shape),
            whole(vectors.shape),
        ],
        out_specs=[by_token(), by_token()],
        out_shape=[
            jax.ShapeDtypeStruct((tokens, width), F32),
            jax.ShapeDtypeStruct((tokens, width), BF16),
        ],
        compiler_params=params(),
        cost_estimate=cost(2 * tokens * width * every * HD, 17e6),
        name="add_attended",
    )(inputs, ctx, w_output, vectors)


def fill(place_ref, own_ref, parts, spots, out_ref):
    shards, height, _ = out_ref.shape
    out_ref[place_ref[GROUP]] = own_ref[...]
    for k in range(1, shards):
        shard = peer_shard(place_ref, shards, k)
        for ref, (index, offset) in zip(parts, spots):
            start = place_ref[index] * (height // GROUP) + offset
            put(out_ref.at[shard], start, ref[k - 1], 16)


def expand_kernel(spots, place_ref, low_ref, bias_ref, own_ref, *refs):
    parts, (act_ref, slope_ref, full_ref, we_ref, sem) = refs[: len(spots)], refs[len(spots) :]
    shards = we_ref.shape[0]
    kept = pltpu.make_async_copy(we_ref, full_ref, sem)

    @pl.when(pl.program_id(0) == 0)
    def _():
        fill(place_ref, own_ref, parts, spots, we_ref)
        kept.start()

    @pl.when(pl.program_id(0) == pl.num_programs(0) - 1)
    def _():
        kept.wait()

    half = low_ref.shape[0] // 2
    halves = [slice(0, half), slice(half, 2 * half)]
    def shard(s, carry):
        bias = bias_ref[peer_shard(place_ref, shards, s), 1:2]
        products = [dot(low_ref[at, :], we_ref[s], 1, 0) for at in halves]
        for at, product in zip(halves, products):
            hidden = product + bias
            square = hidden * hidden
            bent = jnp.tanh(hidden * (0.7978845608028654 + 0.035677408136300125 * square))
            gate = 0.5 + 0.5 * bent
            active = hidden * gate
            act_ref[s, at, :] = active.astype(BF16)
            slope = gate + (active * (1.0 - gate)) * (
                1.5957691216057308 + 0.21406444881780075 * square
            )
            slope_ref[s, at, :] = slope.astype(BF16)
        return carry

    lax.fori_loop(0, shards, shard, 0)


def expand(place, low, biases, own, pieces, shards):
    tokens, width = low.shape
    hidden = own.shape[1]
    block = 512
    spots = [(index, offset) for _, index, offset in pieces]
    parts = [array for array, _, _ in pieces]
    full = (shards, width, hidden)
    by_shard = lambda: pl.BlockSpec((shards, block, hidden), lambda i, *_: (0, i, 0))
    return pl.pallas_call(
        lambda *refs: expand_kernel(spots, *refs),
        grid_spec=pltpu.PrefetchScalarGridSpec(
            num_scalar_prefetch=1,
            grid=(tokens // block,),
            in_specs=[
                pl.BlockSpec((block, width), lambda i, *_: (i, 0)),
                whole(biases.shape),
                whole(own.shape),
                *[whole(a.shape) for a in parts],
            ],
            out_specs=[by_shard(), by_shard(), ANY],
            scratch_shapes=[pltpu.VMEM(full, BF16), pltpu.SemaphoreType.DMA],
        ),
        out_shape=[
            jax.ShapeDtypeStruct((shards, tokens, hidden), BF16),
            jax.ShapeDtypeStruct((shards, tokens, hidden), BF16),
            jax.ShapeDtypeStruct(full, BF16),
        ],
        compiler_params=params(),
        cost_estimate=cost(2 * tokens * width * shards * hidden, 40e6),
        name="expand",
    )(place, low, biases, own, *parts)


def reduce_kernel(spots, place_ref, sum_ref, cot_ref, act_ref, slope_ref, vec_ref, *refs):
    own_ref, refs = refs[0], refs[1:]
    piece_refs, refs = refs[: len(spots)], refs[len(spots) :]
    out_ref, g2_ref, full_ref, mine_ref, send_ref, small_scr = refs[:6]
    dwe_scr, dwr_scr, wr_ref, sems = refs[6:]
    kept = pltpu.make_async_copy(wr_ref, full_ref, sems.at[0])
    step = pl.program_id(0)
    shards = act_ref.shape[0]
    me = place_ref[GROUP]

    @pl.when(step == 0)
    def _():
        fill(place_ref, own_ref, piece_refs, spots, wr_ref)
        kept.start()
        for scr in (dwe_scr, dwr_scr, small_scr):
            scr[...] = jnp.zeros_like(scr)

    gain_one, shift_one = vec_ref[1:2], vec_ref[2:3]
    b_reduce, gain_two, shift_two = vec_ref[3:4], vec_ref[4:5], vec_ref[5:6]
    half = sum_ref.shape[0] // 2
    halves = [slice(0, half), slice(half, 2 * half)]
    mixed = []
    for at in halves:
        part = dot(act_ref[0, at, :], wr_ref[0], 1, 0)
        for s in range(1, shards):
            part = part + dot(act_ref[s, at, :], wr_ref[s], 1, 0)
        mixed.append(part)
    small = [jnp.zeros((1, sum_ref.shape[1]), F32)] * 4
    low, normed_low, active = [], [], []
    for at, part in zip(halves, mixed):
        norm_one, _ = norm_forward(sum_ref[at, :])
        normed = norm_one * gain_one + shift_one
        normed_low.append(normed.astype(BF16))
        norm_two, inverse_two = norm_forward(normed + (part + b_reduce))
        out_ref[at, :] = (norm_two * gain_two + shift_two).astype(BF16)
        cot = cot_ref[at, :].astype(F32)
        grad_two = norm_backward(cot, gain_two, norm_two, inverse_two)
        g2_ref[at, :] = grad_two
        low.append(grad_two.astype(BF16))
        active.append(dot(low[-1], own_ref[...], 1, 1))
        small[0] = small[0] + column_sum(grad_two)
        small[1] = small[1] + column_sum(cot * norm_two)
        small[2] = small[2] + column_sum(cot)
    dwr_scr[...] += dot(act_ref[me], jnp.concatenate(low, axis=0), 0, 0)
    own = []
    for at, part in zip(halves, active):
        own.append((part * slope_ref[0, at, :].astype(F32)).astype(BF16))
        small[3] = small[3] + column_sum(own[-1].astype(F32))
    dwe_scr[...] += dot(
        jnp.concatenate(normed_low, axis=0), jnp.concatenate(own, axis=0), 0, 0
    )
    for n, part in enumerate(small):
        small_scr[n : n + 1] += part

    @pl.when(step == pl.num_programs(0) - 1)
    def _():
        copies = [kept]
        for plane in range(4):
            for ref, core in ((send_ref, place_ref[1]), (mine_ref, place_ref[0])):
                owner = 2 * plane + lax.rem(core, 2)
                top = 0
                for scr in (dwe_scr, dwr_scr):
                    size = scr.shape[0] // GROUP
                    start = pl.multiple_of(owner * size, 8)
                    copy = pltpu.make_async_copy(
                        scr.at[pl.ds(start, size), :],
                        ref.at[plane, top : top + size, :],
                        sems.at[len(copies)],
                    )
                    copy.start()
                    copies.append(copy)
                    top += size
        for copy in copies:
            copy.wait()


def reduce(place, residual, cot, act, slope, vectors, own, pieces):
    tokens, width = residual.shape
    shards, _, hidden = act.shape
    block = 512
    share = (width + hidden) // GROUP
    spots = [(index, offset) for _, index, offset in pieces]
    arrays = [array for array, _, _ in pieces]
    by_token = lambda: pl.BlockSpec((block, width), lambda i, *_: (i, 0))
    return pl.pallas_call(
        lambda *refs: reduce_kernel(spots, *refs),
        grid_spec=pltpu.PrefetchScalarGridSpec(
            num_scalar_prefetch=1,
            grid=(tokens // block,),
            in_specs=[
                by_token(),
                by_token(),
                pl.BlockSpec((shards, block, hidden), lambda i, *_: (0, i, 0)),
                pl.BlockSpec((1, block, hidden), lambda i, p: (p[GROUP], i, 0)),
                whole(vectors.shape),
                whole(own.shape),
                *[whole(a.shape) for a in arrays],
            ],
            out_specs=[
                by_token(),
                by_token(),
                ANY,
                ANY,
                ANY,
                whole((8, width)),
            ],
            scratch_shapes=[
                pltpu.VMEM((width, hidden), F32),
                pltpu.VMEM((hidden, width), F32),
                pltpu.VMEM((shards, hidden, width), BF16),
                pltpu.SemaphoreType.DMA((17,)),
            ],
        ),
        out_shape=[
            jax.ShapeDtypeStruct((tokens, width), BF16),
            jax.ShapeDtypeStruct((tokens, width), F32),
            jax.ShapeDtypeStruct((shards, hidden, width), BF16),
            jax.ShapeDtypeStruct((4, share, width), F32),
            jax.ShapeDtypeStruct((4, share, width), F32),
            jax.ShapeDtypeStruct((8, width), F32),
        ],
        compiler_params=params(),
        cost_estimate=cost(tokens * width * hidden * (2 * shards + 6), 40e6),
        name="reduce",
    )(place, residual, cot, act, slope, vectors, own, *arrays)


def return_kernel(place_ref, sum_ref, g2_ref, slope_ref, ctx_ref, we_ref, wr_ref, w_ref, *refs):
    vec_ref, g1_ref, dctx_ref, dwo_ref, small_ref = refs
    shards = we_ref.shape[0]

    @pl.when(pl.program_id(0) == 0)
    def _():
        dwo_ref[...] = jnp.zeros_like(dwo_ref)
        small_ref[...] = jnp.zeros_like(small_ref)

    half = sum_ref.shape[0] // 2
    halves = [slice(0, half), slice(half, 2 * half)]
    gain_one = vec_ref[1:2]
    low = [g2_ref[at, :].astype(BF16) for at in halves]
    items = [(s, i) for s in range(shards) for i in range(2)]
    total = [g2_ref[at, :] for at in halves]
    ahead = dot(low[0], wr_ref[0], 1, 1)
    for n, (s, i) in enumerate(items):
        grad_active = ahead
        if n + 1 < len(items):
            s_next, i_next = items[n + 1]
            ahead = dot(low[i_next], wr_ref[s_next], 1, 1)
        grad_hidden = (grad_active * slope_ref[s, halves[i], :].astype(F32)).astype(BF16)
        total[i] = total[i] + dot(grad_hidden, we_ref[s], 1, 1)
    small = [jnp.zeros((1, sum_ref.shape[1]), F32)] * 3
    one = []
    for at, grad_normed in zip(halves, total):
        norm_one, inverse_one = norm_forward(sum_ref[at, :])
        grad_one = norm_backward(grad_normed, gain_one, norm_one, inverse_one)
        g1_ref[at, :] = grad_one
        one.append(grad_one.astype(BF16))
        small[0] = small[0] + column_sum(grad_one)
        small[1] = small[1] + column_sum(grad_normed * norm_one)
        small[2] = small[2] + column_sum(grad_normed)
    one = jnp.concatenate(one, axis=0)
    dctx = dot(w_ref[...], one, 1, 1)
    dwo_ref[...] += dot(flat(ctx_ref[...]), one, 1, 0)
    dctx_ref[...] = dctx.astype(BF16).reshape(dctx_ref.shape)
    for n, part in enumerate(small):
        small_ref[n : n + 1] += part


def back_to_context(place, residual, grad_two, slope, ctx, w_expand, w_reduce, weights, vectors):
    tokens, width = residual.shape
    shards, _, hidden = w_expand.shape
    every = ctx.shape[0]
    heads = every // shards
    block = 512
    by_token = lambda: pl.BlockSpec((block, width), lambda i, *_: (i, 0))
    return pl.pallas_call(
        return_kernel,
        grid_spec=pltpu.PrefetchScalarGridSpec(
            num_scalar_prefetch=1,
            grid=(tokens // block,),
            in_specs=[
                by_token(),
                by_token(),
                pl.BlockSpec((shards, block, hidden), lambda i, *_: (0, i, 0)),
                own_block(heads, HD, block),
                whole(w_expand.shape),
                whole(w_reduce.shape),
                whole(weights.shape),
                whole(vectors.shape),
            ],
            out_specs=[
                by_token(),
                pl.BlockSpec((every, HD, block), lambda i, *_: (0, 0, i)),
                whole((heads * HD, width)),
                whole((8, width)),
            ],
        ),
        out_shape=[
            jax.ShapeDtypeStruct((tokens, width), F32),
            jax.ShapeDtypeStruct(ctx.shape, BF16),
            jax.ShapeDtypeStruct((heads * HD, width), F32),
            jax.ShapeDtypeStruct((8, width), F32),
        ],
        compiler_params=params(),
        cost_estimate=cost(tokens * width * (4 * shards * hidden + 2 * every * HD), 40e6),
        name="back_to_context",
    )(place, residual, grad_two, slope, ctx, w_expand, w_reduce, weights, vectors)


def spread_kernel(spots, place_ref, *refs):
    parts, outs = refs[: len(spots)], refs[len(spots) :]
    for ref, (index, offset) in zip(parts, spots):
        start = 0
        for i, out_ref in enumerate(outs):
            size = out_ref.shape[0] // GROUP
            if offset <= i * size < offset + ref.shape[1]:
                put(out_ref, place_ref[index] * size, ref[0, start : start + size, :], 8)
                start += size


def spread(place, pieces, sizes):
    spots = [(index, offset) for _, index, offset in pieces]
    parts = [array for array, _, _ in pieces]
    width = parts[0].shape[2]
    shapes = [(GROUP * size, width) for size in sizes]
    return pl.pallas_call(
        lambda *refs: spread_kernel(spots, *refs),
        grid_spec=pltpu.PrefetchScalarGridSpec(
            num_scalar_prefetch=1,
            grid=(1,),
            in_specs=[whole(a.shape) for a in parts],
            out_specs=[whole(s) for s in shapes],
        ),
        out_shape=[jax.ShapeDtypeStruct(s, F32) for s in shapes],
        compiler_params=params(),
        cost_estimate=cost(0, 10e6),
        name="spread",
    )(place, *parts)


def spread_late_kernel(heads, place_ref, *refs):
    parts = refs[:GROUP]
    dq_ref, dk_ref, dv_ref, dwo_ref, small_ref, grad_scr = refs[GROUP:]
    height = heads * HD
    size, size_two = 3 * height // GROUP, height // GROUP
    top = size + size_two
    for i, ref in enumerate(parts):
        owner = place_ref[i]
        put(grad_scr, owner * size, ref[:size, :], 8)
        put(dwo_ref, owner * size_two, ref[size:top, :], 8)

        @pl.when(owner == 0)
        def _():
            small_ref[...] = ref[top:, :]

    for i, out_ref in enumerate((dq_ref, dk_ref, dv_ref)):
        out_ref[...] = grad_scr[i * height : (i + 1) * height, :]


def spread_late(place, parts, heads):
    share, width = parts[0].shape
    height = heads * HD
    shapes = [(height, width)] * 4 + [(16, width)]
    return pl.pallas_call(
        lambda *refs: spread_late_kernel(heads, *refs),
        grid_spec=pltpu.PrefetchScalarGridSpec(
            num_scalar_prefetch=1,
            grid=(1,),
            in_specs=[whole(a.shape) for a in parts],
            out_specs=[whole(s) for s in shapes],
            scratch_shapes=[pltpu.VMEM((3 * height, width), F32)],
        ),
        out_shape=[jax.ShapeDtypeStruct(s, F32) for s in shapes],
        compiler_params=params(),
        cost_estimate=cost(0, 8 * parts[0].size * 8),
        name="spread_late",
    )(place, *parts)


def input_grads_kernel(place_ref, g1_ref, grad_ref, w_ref, out_ref):
    amount = place_ref[GROUP + 1 + pl.program_id(0)]
    matrix = shift_matrix(amount, g1_ref.shape[0], False)
    total = g1_ref[...] + dot(flat(grad_ref[...]), w_ref[...], 0, 0)
    out_ref[...] = dot(matrix, total.astype(BF16), 1, 0).astype(BF16)


def input_grads(place, length, grad_one, grads, weights):
    tokens, width = grad_one.shape
    every = grads.shape[0]
    by_row = lambda: pl.BlockSpec((length, width), lambda i, *_: (i, 0))
    return pl.pallas_call(
        input_grads_kernel,
        grid_spec=pltpu.PrefetchScalarGridSpec(
            num_scalar_prefetch=1,
            grid=(tokens // length,),
            in_specs=[
                by_row(),
                pl.BlockSpec((every, 3 * HD, length), lambda i, *_: (0, 0, i)),
                whole(weights.shape),
            ],
            out_specs=by_row(),
        ),
        out_shape=jax.ShapeDtypeStruct((tokens, width), BF16),
        compiler_params=params(),
        cost_estimate=cost(2 * tokens * width * (every * 3 * HD + length), 20e6),
        name="input_grads",
    )(place, grad_one, grads, weights)


def after(values, *others):
    return lax.optimization_barrier((values, others))[0]


def solution(mesh):
    peers = mesh.shape["mp"]
    lanes = mesh.shape["dp"]
    rotations = [[(i, (i + k) % peers) for i in range(peers)] for k in range(1, peers)]

    def flip(values, bits):
        return lax.ppermute(values, "dp", [(i, i ^ bits) for i in range(lanes)])

    def from_peers(piece):
        return jnp.stack([lax.ppermute(piece, "mp", perm) for perm in rotations])

    def swapped(piece, *ready):
        copies = jnp.broadcast_to(piece[None], (peers,) + piece.shape)
        got = lax.all_to_all(after(copies, *ready), "mp", 0, 0, tiled=True)
        me = lax.axis_index("mp")
        return jnp.concatenate(
            [
                lax.dynamic_slice_in_dim(got, lax.rem(me + peers - k, peers), 1, 0)
                for k in range(1, peers)
            ]
        )

    def both(near):
        return flip(near, 2), flip(near, 4)

    def corner(by_x, by_y, cut):
        return flip(by_y[:, :cut], 2), flip(by_x[:, cut:], 4)

    def listed(near, by_x, by_y, first, second, cut):
        places = ((near, 0, 0), (by_x, 1, 0), (by_y, 2, 0), (first, 3, 0), (second, 3, cut))
        return with_core(places)

    def with_core(places):
        out = []
        for array, rel, offset in places:
            out.append((array, 2 * rel, offset))
            out.append((flip(array, 1), 2 * rel + 1, offset))
        return out

    planes = [[g + c + i for i in (0, 2, 4, 6)] for g in range(0, lanes, GROUP) for c in (0, 1)]

    def swap_plane(values):
        return lax.all_to_all(values, "dp", 0, 0, tiled=True, axis_index_groups=planes)

    def sum_groups(total):
        step = GROUP
        while step < lanes:
            total = total + flip(total, step)
            step *= 2
        return total

    def partial_sums(mine, got, *ready):
        got = after(got, *ready)
        return [mine[rel] + got[rel] for rel in range(4)]

    def exchange(parts):
        return [flip(parts[rel], 2 * rel) for rel in (1, 2, 3)]

    def total_of(first, rest, *ready):
        rest = after(rest, *ready)
        return sum_groups(first + rest[0] + rest[1] + rest[2])

    def finish(arrays, *ready):
        out = []
        for array in after(arrays, *ready):
            out += [array, flip(array, 1)]
        return out

    def local(
        tokens,
        doc_lengths,
        w_query,
        b_query,
        w_key,
        w_value,
        b_value,
        w_output,
        b_output,
        gain_attn,
        shift_attn,
        w_expand,
        b_expand,
        w_reduce,
        b_reduce,
        gain_ffn,
        shift_ffn,
        cotangent,
    ):
        row_count, length, width = tokens.shape
        heads = w_query.shape[1] // HD
        hidden = w_expand.shape[1]
        count = row_count * length
        inside = lax.axis_index("dp") % GROUP
        me = lax.axis_index("mp")
        ends = jnp.cumsum(doc_lengths, axis=-1)
        longest = jnp.max(doc_lengths, axis=-1, keepdims=True)
        offset = jnp.max(jnp.where(doc_lengths == longest, ends - doc_lengths, 0), axis=-1)
        place = jnp.stack([inside ^ i for i in range(GROUP)] + [me])
        place = jnp.concatenate([place, offset]).astype(jnp.int32)

        by_head = lambda w: w.T.reshape(heads, HD, width)
        own_heads = jnp.concatenate([by_head(w_query), by_head(w_key), by_head(w_value)], axis=1)
        own_heads = jnp.concatenate([own_heads.reshape(3 * heads * HD, width), w_output])
        blank = jnp.zeros((width - 2 * heads * HD,), BF16)
        own_bias = jnp.stack(
            [jnp.concatenate([b_query, b_value, blank]), b_expand]
            + [jnp.zeros((width,), BF16)] * 6
        ).astype(F32)

        def piece_of(array, bits=0):
            size = array.shape[0] // GROUP
            return lax.dynamic_slice_in_dim(array, (inside ^ bits) * size, size, 0).astype(F32)

        piece = piece_of(own_heads)
        near = from_peers(jnp.concatenate([piece, own_bias]))

        position = (jnp.arange(length, dtype=jnp.int32)[None] + offset[:, None]) % length
        segment = jnp.sum((position[:, :, None] >= ends[:, None, :]).astype(jnp.int32), axis=-1)
        segment = segment.reshape(1, count)
        docs = doc_lengths.shape[1]
        label = jnp.arange(EXTRA, dtype=jnp.int32)[:, None]
        is_doc = label < docs
        qf = jnp.where(is_doc & (segment == label), 1.0, 0.0).astype(BF16)
        kf = jnp.where(
            is_doc,
            jnp.where(segment == label, 0.0, MASK),
            jnp.where(label < docs + 3, 1.0, 0.0),
        ).astype(BF16)
        inputs, cot = shift(
            place, length, tokens.reshape(count, width), cotangent.reshape(count, width)
        )
        own = attend_own(
            length, peers, place, inputs, own_bias, qf, kf, own_heads
        )

        near = after(near, own)
        biases = near[:, -own_bias.shape[0] :]
        all_biases = jnp.concatenate([own_bias[None], biases])
        near = near[:, : -own_bias.shape[0]]
        cut = piece.shape[0] // 2
        near_expand = swapped(piece_of(w_expand), near)
        sides = both(near)
        corners = corner(*sides, cut)
        pieces = listed(near, *sides, *corners, cut)
        near_reduce = swapped(piece_of(w_reduce), near_expand)
        sides_expand = both(after(near_expand, corners))
        weights, all_output, qkv, ctx, aug = attend_peers(
            length, peers, place, inputs, after(biases, near_expand), qf, kf, pieces, own
        )

        sides_expand = after(sides_expand, ctx)
        cut = width // GROUP // 2
        corners = corner(*sides_expand, cut)
        vectors = jnp.stack(
            [b_output, gain_attn, shift_attn, b_reduce, gain_ffn, shift_ffn]
            + [jnp.zeros((width,), BF16)] * 2
        ).astype(F32)
        residual, low = add_attended(inputs, ctx, all_output, after(vectors, sides_expand))
        near_reduce, corners = after((near_reduce, corners), low)
        pieces = listed(near_expand, *sides_expand, *corners, cut)
        sides_reduce = both(near_reduce)
        diagonal = swapped(piece_of(w_reduce, 6), near_reduce)
        act, slope, all_expand = expand(
            place, low, after(all_biases, near_reduce), w_expand, pieces, peers
        )
        far_reduce = after((*sides_reduce, diagonal), act)
        pieces = with_core([(array, rel, 0) for rel, array in enumerate([near_reduce, *far_reduce])])
        shifted, grad_two, all_reduce, mine, send, small_one = reduce(
            place, residual, cot, act, slope, vectors, w_reduce, pieces
        )
        got = flip(send, 1)
        output = unshift(place, length, shifted)
        chip = mine + after(got, output)
        early = swap_plane(chip)
        grad_one, dctx, dwo, small = back_to_context(
            place,
            residual,
            grad_two,
            slope,
            ctx,
            all_expand,
            all_reduce,
            all_output,
            after(vectors, chip),
        )
        cut = width // GROUP
        early = sum_groups(jnp.sum(after(early, grad_one), axis=0))[None]
        sides = both(early)
        dqkv, mine, send = attend_back_own(
            length, place, qkv, ctx, aug, dctx, after(kf, early), inputs, dwo, small, small_one
        )
        got = flip(after(send, sides), 1)
        dqkv = attend_back(
            length, peers, 1, 1, place, qkv, ctx, aug, dctx, after(kf, sides), dqkv
        )
        corners = corner(*sides, cut)
        beside = [flip(array, 1) for array in (early, *sides)]
        parts = partial_sums(mine, got, dqkv)
        rest = exchange(parts)
        corners, beside, kept = after((corners, beside, kf), parts)
        dqkv = attend_back(length, peers, 2, peers - 2, place, qkv, ctx, aug, dctx, kept, dqkv)
        total = total_of(parts[0], rest, dqkv)
        second = [total] + exchange([None] + [total] * 3)
        beside += [flip(array, 1) for array in corners]
        pieces = []
        spots = ((0, 0), (2, 0), (4, 0), (6, 0), (6, cut))
        for near, far, (index, top) in zip((early, *sides, *corners), beside, spots):
            pieces += [(near, index, top), (far, index + 1, top)]
        grad_one = after(grad_one, total, beside)
        grad_tokens = input_grads(place, length, grad_one, dqkv, weights)
        second = finish(second, grad_tokens)
        dwe, dwr = spread(place, pieces, [width // GROUP, hidden // GROUP])
        dq, dk, dv, dwo, small_two = spread_late(place, second, heads)
        sums = lambda i: small_two[3 : 3 + heads, i * HD : (i + 1) * HD].reshape(heads * HD)
        shape = (row_count, length, width)
        return (
            output.reshape(shape),
            grad_tokens.reshape(shape),
            dq.T,
            sums(0),
            dk.T,
            dv.T,
            sums(2),
            dwo,
            small_two[0],
            small_two[1],
            small_two[2],
            dwe,
            small_two[11],
            dwr,
            small_two[8],
            small_two[9],
            small_two[10],
        )

    rows, split = P("dp", None, None), P(None, "mp")
    return jax.shard_map(
        local,
        mesh=mesh,
        in_specs=(
            rows,
            P("dp", None),
            split,
            P("mp"),
            split,
            split,
            P("mp"),
            P("mp", None),
            P(),
            P(),
            P(),
            split,
            P("mp"),
            P("mp", None),
            P(),
            P(),
            P(),
            rows,
        ),
        out_specs=(
            rows,
            rows,
            split,
            P("mp"),
            split,
            split,
            P("mp"),
            P("mp", None),
            P(),
            P(),
            P(),
            split,
            P("mp"),
            P("mp", None),
            P(),
            P(),
            P(),
        ),
        check_vma=False,
    )
```

```python
import jax
import jax.numpy as jnp
from jax import lax
from jax.experimental import pallas as pl
from jax.experimental.pallas import tpu as pltpu
from jax.sharding import PartitionSpec as P

HD = 64
GROUP = 8
EXTRA = 16
MASK = -float(2**30)
EPS = 1e-12
F32 = jnp.float32
BF16 = jnp.bfloat16
LIMIT = 60 << 20


def dot(left, right, left_dim, right_dim):
    return lax.dot_general(
        left, right, (((left_dim,), (right_dim,)), ((), ())), preferred_element_type=F32
    )


def params():
    return pltpu.CompilerParams(vmem_limit_bytes=LIMIT)


def cost(flops, moved):
    return pl.CostEstimate(flops=int(flops), bytes_accessed=int(moved), transcendentals=0)


def whole(shape):
    zeros = (0,) * len(shape)
    return pl.BlockSpec(shape, lambda *_: zeros, pipeline_mode=pl.Buffered(1))


def split3(row):
    high = row.astype(BF16).astype(F32)
    rest = row - high
    mid = rest.astype(BF16).astype(F32)
    return high, mid, rest - mid


def rows_of(height, first, parts, width):
    place = lax.broadcasted_iota(jnp.int32, (height, width), 0)
    out = jnp.zeros((height, width), F32)
    for i, part in enumerate(parts):
        out = jnp.where(place == first + i, part, out)
    return out


def put(out_ref, start, values, step):
    rows = pl.ds(pl.multiple_of(start, step), values.shape[0])
    out_ref[rows, :] = values.astype(out_ref.dtype)


def peer_shard(place_ref, shards, k):
    return lax.rem(place_ref[GROUP] + shards - k, shards)


def own_block(*shape):
    return pl.BlockSpec(shape, lambda i, p: (p[GROUP],) + (0,) * (len(shape) - 2) + (i,))


def peer_block(peers, first, *shape):
    middle = (0,) * (len(shape) - 2)
    return pl.BlockSpec(
        shape, lambda k, i, p: (lax.rem(p[GROUP] + peers - first - k, peers),) + middle + (i,)
    )


ANY = pl.BlockSpec(memory_space=pl.ANY)


def shift_matrix(amount, length, forward):
    row = lax.broadcasted_iota(jnp.int32, (length, length), 0)
    column = lax.broadcasted_iota(jnp.int32, (length, length), 1)
    apart = column - row if forward else row - column
    return jnp.where((apart == amount) | (apart == amount - length), 1.0, 0.0).astype(BF16)


def shift_kernel(place_ref, first_ref, second_ref, first_out, second_out):
    length = first_ref.shape[0]
    amount = place_ref[GROUP + 1 + pl.program_id(0)]
    matrix = shift_matrix(amount, length, True)
    first_out[...] = dot(matrix, first_ref[...], 1, 0).astype(BF16)
    second_out[...] = dot(matrix, second_ref[...], 1, 0).astype(BF16)


def shift(place, length, first, second):
    tokens, width = first.shape
    by_row = lambda: pl.BlockSpec((length, width), lambda i, *_: (i, 0))
    return pl.pallas_call(
        shift_kernel,
        grid_spec=pltpu.PrefetchScalarGridSpec(
            num_scalar_prefetch=1,
            grid=(tokens // length,),
            in_specs=[by_row(), by_row()],
            out_specs=[by_row(), by_row()],
        ),
        out_shape=[jax.ShapeDtypeStruct((tokens, width), BF16)] * 2,
        compiler_params=params(),
        cost_estimate=cost(4 * tokens * length * width, 12e6),
        name="shift",
    )(place, first, second)


def unshift_kernel(place_ref, in_ref, out_ref):
    length = in_ref.shape[0]
    matrix = shift_matrix(place_ref[GROUP + 1 + pl.program_id(0)], length, False)
    out_ref[...] = dot(matrix, in_ref[...], 1, 0).astype(BF16)


def unshift(place, length, shifted):
    tokens, width = shifted.shape
    by_row = lambda: pl.BlockSpec((length, width), lambda i, *_: (i, 0))
    return pl.pallas_call(
        unshift_kernel,
        grid_spec=pltpu.PrefetchScalarGridSpec(
            num_scalar_prefetch=1,
            grid=(tokens // length,),
            in_specs=[by_row()],
            out_specs=by_row(),
        ),
        out_shape=jax.ShapeDtypeStruct((tokens, width), BF16),
        compiler_params=params(),
        cost_estimate=cost(2 * tokens * length * width, 6e6),
        name="unshift",
    )(place, shifted)


def tiles(heads, block):
    return [(h, slice(i * block, (i + 1) * block)) for h in range(heads) for i in range(2)]


def attend_rows(x_ref, bias_ref, qf_ref, kf_ref, w_scr, qkv_ref, ctx_ref, aug_ref):
    heads = ctx_ref.shape[0]
    length = x_ref.shape[0]
    block = length // 2
    span = 3 * HD
    proj = dot(w_scr[...], x_ref[...], 1, 1)
    scale = HD ** (-0.5)
    column = bias_ref[...].T[:, 0:1]
    for h in range(heads):
        part = proj[h * span : (h + 1) * span]
        queries = part[:HD] + column[h * HD : (h + 1) * HD]
        values = part[2 * HD :] + column[(heads + h) * HD : (heads + h + 1) * HD]
        qkv_ref[h, :HD, :] = (queries * scale).astype(BF16)
        qkv_ref[h, HD : 2 * HD, :] = part[HD : 2 * HD].astype(BF16)
        qkv_ref[h, 2 * HD :, :] = values.astype(BF16)
    ones_rows = rows_of(EXTRA, 0, (jnp.ones((1, block), F32),), block).astype(BF16)
    items = tiles(heads, block)
    scores = []
    for h, at in items:
        queries = jnp.concatenate([qkv_ref[h, :HD, at], qf_ref[:, at]], axis=0)
        keys = jnp.concatenate([qkv_ref[h, HD : 2 * HD, at], kf_ref[:, at]], axis=0)
        scores.append(dot(keys, queries, 0, 0))
    highest = [jnp.max(part, axis=0, keepdims=True) for part in scores]
    weight = [jnp.exp(part - top).astype(BF16) for part, top in zip(scores, highest)]
    context = []
    for (h, at), part in zip(items, weight):
        values = jnp.concatenate([qkv_ref[h, 2 * HD :, at], ones_rows], axis=0)
        context.append(dot(values, part, 1, 0))
    for (h, at), part, top in zip(items, context, highest):
        total = part[HD : HD + 1]
        ctx_ref[h, :, at] = (part[:HD] * (1.0 / total)).astype(BF16)
        log_total = top + jnp.log(total)
        extra = rows_of(EXTRA, 4, split3(-log_total), block)
        aug_ref[h, :, at] = (extra + qf_ref[:, at].astype(F32)).astype(BF16)


def attend_own_kernel(place_ref, x_ref, bias_ref, qf_ref, kf_ref, own_ref, *refs):
    w_ref, qkv_ref, ctx_ref, aug_ref = refs

    @pl.when(pl.program_id(0) == 0)
    def _():
        w_ref[...] = own_ref[...]

    attend_rows(x_ref, bias_ref, qf_ref, kf_ref, w_ref, qkv_ref, ctx_ref, aug_ref)


def attend_own(length, peers, place, inputs, bias, qf, kf, own):
    heads = own.shape[0] // (3 * HD)
    tokens, width = inputs.shape
    every = peers * heads
    shapes = [(every * 3 * HD, width)] + [(every, n, tokens) for n in (3 * HD, HD, EXTRA)]
    by_row = pl.BlockSpec((EXTRA, length), lambda i, *_: (0, i))
    return pl.pallas_call(
        attend_own_kernel,
        grid_spec=pltpu.PrefetchScalarGridSpec(
            num_scalar_prefetch=1,
            grid=(tokens // length,),
            in_specs=[
                pl.BlockSpec((length, width), lambda i, *_: (i, 0)),
                whole(bias.shape),
                by_row,
                by_row,
                whole(own.shape),
            ],
            out_specs=[
                pl.BlockSpec((heads * 3 * HD, width), lambda i, p: (p[GROUP], 0)),
                *[own_block(heads, n, length) for n in (3 * HD, HD, EXTRA)],
            ],
        ),
        out_shape=[jax.ShapeDtypeStruct(shape, BF16) for shape in shapes],
        compiler_params=params(),
        cost_estimate=cost(heads * tokens * (6 * HD * width + 16 * 64 * length), 12e6),
        name="attend_own",
    )(place, inputs, bias, qf, kf, own)


def attend_peers_kernel(spots, place_ref, x_ref, bias_ref, qf_ref, kf_ref, *refs):
    count = len(spots)
    parts = refs[:count]
    w_ref, qkv_ref, ctx_ref, aug_ref, wide_scr = refs[count + 4 :]

    @pl.when(pl.program_id(1) == 0)
    def _():
        size = w_ref.shape[0] // GROUP
        for ref, (index, offset) in zip(parts, spots):
            put(wide_scr, place_ref[index] * size + offset, ref[0], 8)
        w_ref[...] = wide_scr[...].astype(BF16)

    attend_rows(x_ref, bias_ref.at[0], qf_ref, kf_ref, w_ref, qkv_ref, ctx_ref, aug_ref)


def attend_peers(length, peers, place, inputs, bias, qf, kf, pieces, arrays):
    heads = arrays[1].shape[0] // peers
    tokens, width = inputs.shape
    spots = [(index, offset) for _, index, offset in pieces]
    parts = [array for array, _, _ in pieces]
    by_row = pl.BlockSpec((EXTRA, length), lambda k, i, *_: (0, i))
    return pl.pallas_call(
        lambda *refs: attend_peers_kernel(spots, *refs),
        grid_spec=pltpu.PrefetchScalarGridSpec(
            num_scalar_prefetch=1,
            grid=(peers - 1, tokens // length),
            in_specs=[
                pl.BlockSpec((length, width), lambda k, i, *_: (i, 0)),
                pl.BlockSpec((1,) + bias.shape[1:], lambda k, i, *_: (k, 0, 0)),
                by_row,
                by_row,
                *[
                    pl.BlockSpec((1,) + a.shape[1:], lambda k, i, *_: (k, 0, 0)) for a in parts
                ],
                *[ANY] * 4,
            ],
            out_specs=[
                pl.BlockSpec(
                    (heads * 3 * HD, width),
                    lambda k, i, p: (lax.rem(p[GROUP] + peers - 1 - k, peers), 0),
                ),
                *[peer_block(peers, 1, heads, n, length) for n in (3 * HD, HD, EXTRA)],
            ],
            scratch_shapes=[pltpu.VMEM((heads * 3 * HD, width), F32)],
        ),
        out_shape=[jax.ShapeDtypeStruct(a.shape, a.dtype) for a in arrays],
        input_output_aliases={5 + len(parts) + i: i for i in range(4)},
        compiler_params=params(),
        cost_estimate=cost(
            (peers - 1) * heads * tokens * (6 * HD * width + 16 * 64 * length), 30e6
        ),
        name="attend_peers",
    )(place, inputs, bias, qf, kf, *parts, *arrays)


def attend_back_rows(qkv_ref, ctx_ref, aug_ref, grad_ref, kf_ref, out_ref):
    heads, _, length = ctx_ref.shape
    block = length // 2
    scale = HD ** (-0.5)
    one = jnp.ones((1, block), F32)
    ones_rows = rows_of(EXTRA, 0, (one, one, one), block).astype(BF16)
    items = tiles(heads, block)
    scores, spreads = [], []
    for h, at in items:
        scores.append(
            dot(
                jnp.concatenate([qkv_ref[h, HD : 2 * HD, at], kf_ref[:, at]], axis=0),
                jnp.concatenate([qkv_ref[h, :HD, at], aug_ref[h, :, at]], axis=0),
                0,
                0,
            )
        )
    for h, at in items:
        grad = grad_ref[h, :, at]
        inner = jnp.sum(grad.astype(F32) * ctx_ref[h, :, at].astype(F32), axis=0, keepdims=True)
        grad_extra = rows_of(EXTRA, 0, split3(-inner), block).astype(BF16)
        spreads.append(
            dot(
                jnp.concatenate([qkv_ref[h, 2 * HD :, at], ones_rows], axis=0),
                jnp.concatenate([grad, grad_extra], axis=0),
                0,
                0,
            )
        )
    probs = [jnp.exp(part) for part in scores]
    slopes = [(part * spread).astype(BF16) for part, spread in zip(probs, spreads)]
    probs = [part.astype(BF16) for part in probs]
    for (h, at), part in zip(items, probs):
        out_ref[h, 2 * HD :, at] = dot(grad_ref[h, :, at], part, 1, 1).astype(BF16)
    for (h, at), part in zip(items, slopes):
        out_ref[h, HD : 2 * HD, at] = dot(qkv_ref[h, :HD, at], part, 1, 1).astype(BF16)
    for (h, at), part in zip(items, slopes):
        grad = dot(qkv_ref[h, HD : 2 * HD, at], part, 1, 0)
        out_ref[h, :HD, at] = (grad * scale).astype(BF16)


def attend_back_own_kernel(place_ref, qkv_ref, ctx_ref, aug_ref, grad_ref, kf_ref, *refs):
    x_ref, dwo_ref, small_ref, early_ref, out_ref, mine_ref, send_ref, grad_scr, sum_scr = refs
    heads = ctx_ref.shape[0]
    height = heads * HD
    step = pl.program_id(0)

    @pl.when(step == 0)
    def _():
        grad_scr[...] = jnp.zeros_like(grad_scr)
        sum_scr[...] = jnp.zeros_like(sum_scr)

    attend_back_rows(qkv_ref, ctx_ref, aug_ref, grad_ref, kf_ref, out_ref)
    ones = jnp.ones((8, x_ref.shape[0]), BF16)
    row = lax.broadcasted_iota(jnp.int32, (8, 3 * HD), 0)
    sums = jnp.zeros((8, 3 * HD), F32)
    for h in range(heads):
        grad = dot(out_ref[h], x_ref[...], 1, 0)
        for i in range(3):
            grad_scr[i * height + h * HD : i * height + (h + 1) * HD, :] += grad[
                i * HD : (i + 1) * HD
            ]
        sums = jnp.where(row == 3 + h, dot(ones, out_ref[h], 1, 1), sums)
    sum_scr[:, : 3 * HD] += sums

    @pl.when(step == pl.num_programs(0) - 1)
    def _():
        size, size_two = 3 * height // GROUP, height // GROUP
        top = size + size_two
        for rel in range(4):
            for source, ref in enumerate((mine_ref, send_ref)):
                owner = place_ref[2 * rel + source]
                ref[rel, :size, :] = grad_scr[pl.ds(pl.multiple_of(owner * size, 8), size), :]
                start = pl.multiple_of(owner * size_two, 8)
                ref[rel, size:top, :] = dwo_ref[pl.ds(start, size_two), :]
                ref[rel, top : top + 8, :] = jnp.where(
                    owner == 0, small_ref[...] + sum_scr[...], 0.0
                )
                ref[rel, top + 8 :, :] = jnp.where(owner == 0, early_ref[...], 0.0)


def attend_back_own(length, place, qkv, ctx, aug, grad, kf, inputs, dwo, small, early):
    height, width = dwo.shape
    heads = height // HD
    tokens = inputs.shape[0]
    share = 4 * height // GROUP + 16
    return pl.pallas_call(
        attend_back_own_kernel,
        grid_spec=pltpu.PrefetchScalarGridSpec(
            num_scalar_prefetch=1,
            grid=(tokens // length,),
            in_specs=[
                own_block(heads, 3 * HD, length),
                own_block(heads, HD, length),
                own_block(heads, EXTRA, length),
                own_block(heads, HD, length),
                pl.BlockSpec((EXTRA, length), lambda i, *_: (0, i)),
                pl.BlockSpec((length, width), lambda i, *_: (i, 0)),
                whole(dwo.shape),
                whole(small.shape),
                whole(early.shape),
            ],
            out_specs=[
                own_block(heads, 3 * HD, length),
                whole((4, share, width)),
                whole((4, share, width)),
            ],
            scratch_shapes=[pltpu.VMEM((3 * height, width), F32), pltpu.VMEM((8, width), F32)],
        ),
        out_shape=[jax.ShapeDtypeStruct(qkv.shape, BF16)]
        + [jax.ShapeDtypeStruct((4, share, width), F32)] * 2,
        compiler_params=params(),
        cost_estimate=cost(heads * tokens * (20 * 64 * length + 6 * HD * width), 12e6),
        name="attend_back_own",
    )(place, qkv, ctx, aug, grad, kf, inputs, dwo, small, early)


def attend_back_kernel(place_ref, qkv_ref, ctx_ref, aug_ref, grad_ref, kf_ref, old_ref, out_ref):
    attend_back_rows(qkv_ref, ctx_ref, aug_ref, grad_ref, kf_ref, out_ref)


def attend_back(length, peers, first, count, place, qkv, ctx, aug, grad, kf, out):
    every, _, tokens = qkv.shape
    heads = every // peers
    by_peer = lambda n: peer_block(peers, first, heads, n, length)
    return pl.pallas_call(
        attend_back_kernel,
        grid_spec=pltpu.PrefetchScalarGridSpec(
            num_scalar_prefetch=1,
            grid=(count, tokens // length),
            in_specs=[
                by_peer(3 * HD),
                by_peer(HD),
                by_peer(EXTRA),
                by_peer(HD),
                pl.BlockSpec((EXTRA, length), lambda k, i, *_: (0, i)),
                ANY,
            ],
            out_specs=by_peer(3 * HD),
        ),
        out_shape=jax.ShapeDtypeStruct(out.shape, BF16),
        input_output_aliases={6: 0},
        compiler_params=params(),
        cost_estimate=cost(count * heads * tokens * 20 * 64 * length, 12e6),
        name="attend_back",
    )(place, qkv, ctx, aug, grad, kf, out)


def norm_forward(hidden):
    center = hidden - jnp.mean(hidden, axis=-1, keepdims=True)
    inverse = lax.rsqrt(jnp.mean(center * center, axis=-1, keepdims=True) + EPS)
    return center * inverse, inverse


def norm_backward(grad, gain, norm, inverse):
    scaled = grad * gain
    first = jnp.mean(scaled, axis=-1, keepdims=True)
    second = jnp.mean(scaled * norm, axis=-1, keepdims=True)
    return (scaled - first - norm * second) * inverse


def column_sum(values):
    return jnp.sum(values, axis=0, keepdims=True)


def flat(values):
    return values.reshape(-1, values.shape[-1])


def fill(place_ref, own_ref, parts, spots, out_ref):
    shards, height, _ = out_ref.shape
    out_ref[place_ref[GROUP]] = own_ref[...]
    for k in range(1, shards):
        shard = peer_shard(place_ref, shards, k)
        for ref, (index, offset) in zip(parts, spots):
            start = place_ref[index] * (height // GROUP) + offset
            put(out_ref.at[shard], start, ref[k - 1], 16)


def expand_kernel(spots, place_ref, x_ref, ctx_ref, bias_ref, vec_ref, own_ref, own_wo_ref, *refs):
    parts, refs = refs[: len(spots)], refs[len(spots) :]
    sum_ref, act_ref, slope_ref, full_ref, wo_ref, we_ref, wide_scr, low_scr, sem = refs
    shards, width, _ = we_ref.shape
    size, size_two = width // GROUP, wo_ref.shape[0] // (shards * GROUP)
    kept = pltpu.make_async_copy(we_ref, full_ref, sem)

    @pl.when(pl.program_id(0) == 0)
    def _():
        me = place_ref[GROUP]
        we_ref[me] = own_ref[...]
        put(wide_scr, me * size_two * GROUP, own_wo_ref[...], 8)
        for k in range(1, shards):
            shard = peer_shard(place_ref, shards, k)
            for ref, (index, offset) in zip(parts, spots):
                part = ref[k - 1]
                count = min(part.shape[0], size - offset)
                put(we_ref.at[shard], place_ref[index] * size + offset, part[:count], 16)
                if count < part.shape[0]:
                    start = (shard * GROUP + place_ref[index]) * size_two
                    put(wide_scr, start, part[count:], 8)
        wo_ref[...] = wide_scr[...].astype(BF16)
        kept.start()

    @pl.when(pl.program_id(0) == pl.num_programs(0) - 1)
    def _():
        kept.wait()

    b_output, gain_one, shift_one = vec_ref[0:1], vec_ref[1:2], vec_ref[2:3]
    half = x_ref.shape[0] // 2
    halves = [slice(0, half), slice(half, 2 * half)]
    attended = [dot(flat(ctx_ref[:, :, at]), wo_ref[...], 0, 0) for at in halves]
    for at, part in zip(halves, attended):
        residual = x_ref[at, :].astype(F32) + (part + b_output)
        sum_ref[at, :] = residual
        norm_one, _ = norm_forward(residual)
        low_scr[at, :] = (norm_one * gain_one + shift_one).astype(BF16)

    def shard_step(s, carry):
        bias = bias_ref[peer_shard(place_ref, shards, s), 1:2]
        products = [dot(low_scr[at, :], we_ref[s], 1, 0) for at in halves]
        for at, product in zip(halves, products):
            hidden = product + bias
            square = hidden * hidden
            bent = jnp.tanh(hidden * (0.7978845608028654 + 0.035677408136300125 * square))
            gate = 0.5 + 0.5 * bent
            active = hidden * gate
            act_ref[s, at, :] = active.astype(BF16)
            slope = gate + (active * (1.0 - gate)) * (
                1.5957691216057308 + 0.21406444881780075 * square
            )
            slope_ref[s, at, :] = slope.astype(BF16)
        return carry

    lax.fori_loop(0, shards, shard_step, 0)


def expand(place, inputs, ctx, biases, vectors, own, own_wo, pieces, shards):
    tokens, width = inputs.shape
    hidden = own.shape[1]
    every = ctx.shape[0]
    block = 512
    spots = [(index, offset) for _, index, offset in pieces]
    parts = [array for array, _, _ in pieces]
    full = (shards, width, hidden)
    by_token = lambda: pl.BlockSpec((block, width), lambda i, *_: (i, 0))
    by_shard = lambda: pl.BlockSpec((shards, block, hidden), lambda i, *_: (0, i, 0))
    return pl.pallas_call(
        lambda *refs: expand_kernel(spots, *refs),
        grid_spec=pltpu.PrefetchScalarGridSpec(
            num_scalar_prefetch=1,
            grid=(tokens // block,),
            in_specs=[
                by_token(),
                pl.BlockSpec((every, HD, block), lambda i, *_: (0, 0, i)),
                whole(biases.shape),
                whole(vectors.shape),
                whole(own.shape),
                whole(own_wo.shape),
                *[whole(a.shape) for a in parts],
            ],
            out_specs=[by_token(), by_shard(), by_shard(), ANY, whole((every * HD, width))],
            scratch_shapes=[
                pltpu.VMEM(full, BF16),
                pltpu.VMEM((every * HD, width), F32),
                pltpu.VMEM((block, width), BF16),
                pltpu.SemaphoreType.DMA,
            ],
        ),
        out_shape=[
            jax.ShapeDtypeStruct((tokens, width), F32),
            jax.ShapeDtypeStruct((shards, tokens, hidden), BF16),
            jax.ShapeDtypeStruct((shards, tokens, hidden), BF16),
            jax.ShapeDtypeStruct(full, BF16),
            jax.ShapeDtypeStruct((every * HD, width), BF16),
        ],
        compiler_params=params(),
        cost_estimate=cost(2 * tokens * width * (shards * hidden + every * HD), 40e6),
        name="expand",
    )(place, inputs, ctx, biases, vectors, own, own_wo, *parts)


def reduce_kernel(spots, place_ref, sum_ref, cot_ref, act_ref, slope_ref, vec_ref, *refs):
    own_ref, refs = refs[0], refs[1:]
    piece_refs, refs = refs[: len(spots)], refs[len(spots) :]
    out_ref, g2_ref, full_ref, mine_ref, send_ref, small_scr = refs[:6]
    dwe_scr, dwr_scr, wr_ref, sems = refs[6:]
    kept = pltpu.make_async_copy(wr_ref, full_ref, sems.at[0])
    step = pl.program_id(0)
    shards = act_ref.shape[0]
    me = place_ref[GROUP]

    @pl.when(step == 0)
    def _():
        fill(place_ref, own_ref, piece_refs, spots, wr_ref)
        kept.start()
        for scr in (dwe_scr, dwr_scr, small_scr):
            scr[...] = jnp.zeros_like(scr)

    gain_one, shift_one = vec_ref[1:2], vec_ref[2:3]
    b_reduce, gain_two, shift_two = vec_ref[3:4], vec_ref[4:5], vec_ref[5:6]
    half = sum_ref.shape[0] // 2
    halves = [slice(0, half), slice(half, 2 * half)]
    quarter = half // 4
    width = sum_ref.shape[1]
    small = [jnp.zeros((1, width), F32)] * 4

    def norm_part(start, mixed):
        at = slice(start, start + quarter)
        norm_one, _ = norm_forward(sum_ref[at, :])
        normed = norm_one * gain_one + shift_one
        norm_two, inverse_two = norm_forward(normed + (mixed + b_reduce))
        out_ref[at, :] = (norm_two * gain_two + shift_two).astype(BF16)
        cot = cot_ref[at, :].astype(F32)
        grad_two = norm_backward(cot, gain_two, norm_two, inverse_two)
        g2_ref[at, :] = grad_two
        small[0] = small[0] + column_sum(grad_two)
        small[1] = small[1] + column_sum(cot * norm_two)
        small[2] = small[2] + column_sum(cot)
        return grad_two.astype(BF16), normed.astype(BF16)

    first, second = halves
    mixed = dot(act_ref[0, first, :], wr_ref[0], 1, 0)
    for s in range(1, shards):
        mixed = mixed + dot(act_ref[s, first, :], wr_ref[s], 1, 0)
    later = None
    parts = []
    for s in range(shards):
        product = dot(act_ref[s, second, :], wr_ref[s], 1, 0)
        later = product if later is None else later + product
        parts.append(norm_part(s * quarter, mixed[s * quarter : (s + 1) * quarter]))
    low_a = jnp.concatenate([part[0] for part in parts], axis=0)
    normed_a = jnp.concatenate([part[1] for part in parts], axis=0)
    active_a = dot(low_a, own_ref[...], 1, 1)
    parts = [norm_part(half + s * quarter, later[s * quarter : (s + 1) * quarter]) for s in (0, 1)]
    dwr_scr[...] += dot(act_ref[me, first, :], low_a, 0, 0)
    parts += [norm_part(half + s * quarter, later[s * quarter : (s + 1) * quarter]) for s in (2, 3)]
    own_a = (active_a * slope_ref[0, first, :].astype(F32)).astype(BF16)
    low_b = jnp.concatenate([part[0] for part in parts], axis=0)
    normed_b = jnp.concatenate([part[1] for part in parts], axis=0)
    active_b = dot(low_b, own_ref[...], 1, 1)
    small[3] = small[3] + column_sum(own_a.astype(F32))
    dwe_scr[...] += dot(normed_a, own_a, 0, 0)
    own_b = (active_b * slope_ref[0, second, :].astype(F32)).astype(BF16)
    dwr_scr[...] += dot(act_ref[me, second, :], low_b, 0, 0)
    small[3] = small[3] + column_sum(own_b.astype(F32))
    dwe_scr[...] += dot(normed_b, own_b, 0, 0)
    for n, part in enumerate(small):
        small_scr[n : n + 1] += part

    @pl.when(step == pl.num_programs(0) - 1)
    def _():
        copies = [kept]
        for plane in range(4):
            for ref, core in ((send_ref, place_ref[1]), (mine_ref, place_ref[0])):
                owner = 2 * plane + lax.rem(core, 2)
                top = 0
                for scr in (dwe_scr, dwr_scr):
                    size = scr.shape[0] // GROUP
                    start = pl.multiple_of(owner * size, 8)
                    copy = pltpu.make_async_copy(
                        scr.at[pl.ds(start, size), :],
                        ref.at[plane, top : top + size, :],
                        sems.at[len(copies)],
                    )
                    copy.start()
                    copies.append(copy)
                    top += size
        for copy in copies:
            copy.wait()


def reduce(place, residual, cot, act, slope, vectors, own, pieces):
    tokens, width = residual.shape
    shards, _, hidden = act.shape
    block = 512
    share = (width + hidden) // GROUP
    spots = [(index, offset) for _, index, offset in pieces]
    arrays = [array for array, _, _ in pieces]
    by_token = lambda: pl.BlockSpec((block, width), lambda i, *_: (i, 0))
    return pl.pallas_call(
        lambda *refs: reduce_kernel(spots, *refs),
        grid_spec=pltpu.PrefetchScalarGridSpec(
            num_scalar_prefetch=1,
            grid=(tokens // block,),
            in_specs=[
                by_token(),
                by_token(),
                pl.BlockSpec((shards, block, hidden), lambda i, *_: (0, i, 0)),
                pl.BlockSpec((1, block, hidden), lambda i, p: (p[GROUP], i, 0)),
                whole(vectors.shape),
                whole(own.shape),
                *[whole(a.shape) for a in arrays],
            ],
            out_specs=[
                by_token(),
                by_token(),
                ANY,
                ANY,
                ANY,
                whole((8, width)),
            ],
            scratch_shapes=[
                pltpu.VMEM((width, hidden), F32),
                pltpu.VMEM((hidden, width), F32),
                pltpu.VMEM((shards, hidden, width), BF16),
                pltpu.SemaphoreType.DMA((17,)),
            ],
        ),
        out_shape=[
            jax.ShapeDtypeStruct((tokens, width), BF16),
            jax.ShapeDtypeStruct((tokens, width), F32),
            jax.ShapeDtypeStruct((shards, hidden, width), BF16),
            jax.ShapeDtypeStruct((4, share, width), F32),
            jax.ShapeDtypeStruct((4, share, width), F32),
            jax.ShapeDtypeStruct((8, width), F32),
        ],
        compiler_params=params(),
        cost_estimate=cost(tokens * width * hidden * (2 * shards + 6), 40e6),
        name="reduce",
    )(place, residual, cot, act, slope, vectors, own, *arrays)


def return_kernel(place_ref, sum_ref, g2_ref, slope_ref, ctx_ref, we_ref, wr_ref, w_ref, *refs):
    vec_ref, g1_ref, dctx_ref, dwo_ref, small_ref = refs
    shards = we_ref.shape[0]

    @pl.when(pl.program_id(0) == 0)
    def _():
        dwo_ref[...] = jnp.zeros_like(dwo_ref)
        small_ref[...] = jnp.zeros_like(small_ref)

    half = sum_ref.shape[0] // 2
    halves = [slice(0, half), slice(half, 2 * half)]
    gain_one = vec_ref[1:2]
    low = [g2_ref[at, :].astype(BF16) for at in halves]
    items = [(s, i) for s in range(shards) for i in range(2)]
    total = [g2_ref[at, :] for at in halves]
    ahead = dot(low[0], wr_ref[0], 1, 1)
    for n, (s, i) in enumerate(items):
        grad_active = ahead
        if n + 1 < len(items):
            s_next, i_next = items[n + 1]
            ahead = dot(low[i_next], wr_ref[s_next], 1, 1)
        grad_hidden = (grad_active * slope_ref[s, halves[i], :].astype(F32)).astype(BF16)
        total[i] = total[i] + dot(grad_hidden, we_ref[s], 1, 1)
    small = [jnp.zeros((1, sum_ref.shape[1]), F32)] * 3
    one = []
    for at, grad_normed in zip(halves, total):
        norm_one, inverse_one = norm_forward(sum_ref[at, :])
        grad_one = norm_backward(grad_normed, gain_one, norm_one, inverse_one)
        g1_ref[at, :] = grad_one
        one.append(grad_one.astype(BF16))
        small[0] = small[0] + column_sum(grad_one)
        small[1] = small[1] + column_sum(grad_normed * norm_one)
        small[2] = small[2] + column_sum(grad_normed)
    one = jnp.concatenate(one, axis=0)
    dctx = dot(w_ref[...], one, 1, 1)
    dwo_ref[...] += dot(flat(ctx_ref[...]), one, 1, 0)
    dctx_ref[...] = dctx.astype(BF16).reshape(dctx_ref.shape)
    for n, part in enumerate(small):
        small_ref[n : n + 1] += part


def back_to_context(place, residual, grad_two, slope, ctx, w_expand, w_reduce, weights, vectors):
    tokens, width = residual.shape
    shards, _, hidden = w_expand.shape
    every = ctx.shape[0]
    heads = every // shards
    block = 512
    by_token = lambda: pl.BlockSpec((block, width), lambda i, *_: (i, 0))
    return pl.pallas_call(
        return_kernel,
        grid_spec=pltpu.PrefetchScalarGridSpec(
            num_scalar_prefetch=1,
            grid=(tokens // block,),
            in_specs=[
                by_token(),
                by_token(),
                pl.BlockSpec((shards, block, hidden), lambda i, *_: (0, i, 0)),
                own_block(heads, HD, block),
                whole(w_expand.shape),
                whole(w_reduce.shape),
                whole(weights.shape),
                whole(vectors.shape),
            ],
            out_specs=[
                by_token(),
                pl.BlockSpec((every, HD, block), lambda i, *_: (0, 0, i)),
                whole((heads * HD, width)),
                whole((8, width)),
            ],
        ),
        out_shape=[
            jax.ShapeDtypeStruct((tokens, width), F32),
            jax.ShapeDtypeStruct(ctx.shape, BF16),
            jax.ShapeDtypeStruct((heads * HD, width), F32),
            jax.ShapeDtypeStruct((8, width), F32),
        ],
        compiler_params=params(),
        cost_estimate=cost(tokens * width * (4 * shards * hidden + 2 * every * HD), 40e6),
        name="back_to_context",
    )(place, residual, grad_two, slope, ctx, w_expand, w_reduce, weights, vectors)


def spread_kernel(spots, place_ref, *refs):
    parts, outs = refs[: len(spots)], refs[len(spots) :]
    for ref, (index, offset) in zip(parts, spots):
        start = 0
        for i, out_ref in enumerate(outs):
            size = out_ref.shape[0] // GROUP
            if offset <= i * size < offset + ref.shape[1]:
                put(out_ref, place_ref[index] * size, ref[0, start : start + size, :], 8)
                start += size


def spread(place, pieces, sizes):
    spots = [(index, offset) for _, index, offset in pieces]
    parts = [array for array, _, _ in pieces]
    width = parts[0].shape[2]
    shapes = [(GROUP * size, width) for size in sizes]
    return pl.pallas_call(
        lambda *refs: spread_kernel(spots, *refs),
        grid_spec=pltpu.PrefetchScalarGridSpec(
            num_scalar_prefetch=1,
            grid=(1,),
            in_specs=[whole(a.shape) for a in parts],
            out_specs=[whole(s) for s in shapes],
        ),
        out_shape=[jax.ShapeDtypeStruct(s, F32) for s in shapes],
        compiler_params=params(),
        cost_estimate=cost(0, 10e6),
        name="spread",
    )(place, *parts)


def spread_late_kernel(heads, place_ref, *refs):
    parts = refs[:GROUP]
    dq_ref, dk_ref, dv_ref, dwo_ref, small_ref, grad_scr = refs[GROUP:]
    height = heads * HD
    size, size_two = 3 * height // GROUP, height // GROUP
    top = size + size_two
    for i, ref in enumerate(parts):
        owner = place_ref[i]
        put(grad_scr, owner * size, ref[:size, :], 8)
        put(dwo_ref, owner * size_two, ref[size:top, :], 8)

        @pl.when(owner == 0)
        def _():
            small_ref[...] = ref[top:, :]

    for i, out_ref in enumerate((dq_ref, dk_ref, dv_ref)):
        out_ref[...] = grad_scr[i * height : (i + 1) * height, :]


def spread_late(place, parts, heads):
    share, width = parts[0].shape
    height = heads * HD
    shapes = [(height, width)] * 4 + [(16, width)]
    return pl.pallas_call(
        lambda *refs: spread_late_kernel(heads, *refs),
        grid_spec=pltpu.PrefetchScalarGridSpec(
            num_scalar_prefetch=1,
            grid=(1,),
            in_specs=[whole(a.shape) for a in parts],
            out_specs=[whole(s) for s in shapes],
            scratch_shapes=[pltpu.VMEM((3 * height, width), F32)],
        ),
        out_shape=[jax.ShapeDtypeStruct(s, F32) for s in shapes],
        compiler_params=params(),
        cost_estimate=cost(0, 8 * parts[0].size * 8),
        name="spread_late",
    )(place, *parts)


def input_grads_kernel(place_ref, g1_ref, grad_ref, w_ref, out_ref):
    amount = place_ref[GROUP + 1 + pl.program_id(0)]
    matrix = shift_matrix(amount, g1_ref.shape[0], False)
    total = g1_ref[...] + dot(flat(grad_ref[...]), w_ref[...], 0, 0)
    out_ref[...] = dot(matrix, total.astype(BF16), 1, 0).astype(BF16)


def input_grads(place, length, grad_one, grads, weights):
    tokens, width = grad_one.shape
    every = grads.shape[0]
    by_row = lambda: pl.BlockSpec((length, width), lambda i, *_: (i, 0))
    return pl.pallas_call(
        input_grads_kernel,
        grid_spec=pltpu.PrefetchScalarGridSpec(
            num_scalar_prefetch=1,
            grid=(tokens // length,),
            in_specs=[
                by_row(),
                pl.BlockSpec((every, 3 * HD, length), lambda i, *_: (0, 0, i)),
                whole(weights.shape),
            ],
            out_specs=by_row(),
        ),
        out_shape=jax.ShapeDtypeStruct((tokens, width), BF16),
        compiler_params=params(),
        cost_estimate=cost(2 * tokens * width * (every * 3 * HD + length), 20e6),
        name="input_grads",
    )(place, grad_one, grads, weights)


def after(values, *others):
    return lax.optimization_barrier((values, others))[0]


def solution(mesh):
    peers = mesh.shape["mp"]
    lanes = mesh.shape["dp"]
    rotations = [[(i, (i + k) % peers) for i in range(peers)] for k in range(1, peers)]

    def flip(values, bits):
        return lax.ppermute(values, "dp", [(i, i ^ bits) for i in range(lanes)])

    def from_peers(piece):
        return jnp.stack([lax.ppermute(piece, "mp", perm) for perm in rotations])

    def swapped(piece, *ready):
        copies = jnp.broadcast_to(piece[None], (peers,) + piece.shape)
        got = lax.all_to_all(after(copies, *ready), "mp", 0, 0, tiled=True)
        me = lax.axis_index("mp")
        return jnp.concatenate(
            [
                lax.dynamic_slice_in_dim(got, lax.rem(me + peers - k, peers), 1, 0)
                for k in range(1, peers)
            ]
        )

    def both(near):
        return flip(near, 2), flip(near, 4)

    def corner(by_x, by_y, cut):
        return flip(by_y[:, :cut], 2), flip(by_x[:, cut:], 4)

    def listed(near, by_x, by_y, first, second, cut):
        places = ((near, 0, 0), (by_x, 1, 0), (by_y, 2, 0), (first, 3, 0), (second, 3, cut))
        return with_core(places)

    def with_core(places):
        out = []
        for array, rel, offset in places:
            out.append((array, 2 * rel, offset))
            out.append((flip(array, 1), 2 * rel + 1, offset))
        return out

    planes = [[g + c + i for i in (0, 2, 4, 6)] for g in range(0, lanes, GROUP) for c in (0, 1)]

    def swap_plane(values):
        return lax.all_to_all(values, "dp", 0, 0, tiled=True, axis_index_groups=planes)

    def sum_groups(total):
        step = GROUP
        while step < lanes:
            total = total + flip(total, step)
            step *= 2
        return total

    def partial_sums(mine, got, *ready):
        got = after(got, *ready)
        return [mine[rel] + got[rel] for rel in range(4)]

    def exchange(parts):
        return [flip(parts[rel], 2 * rel) for rel in (1, 2, 3)]

    def total_of(first, rest, *ready):
        rest = after(rest, *ready)
        return sum_groups(first + rest[0] + rest[1] + rest[2])

    def finish(arrays, *ready):
        out = []
        for array in after(arrays, *ready):
            out += [array, flip(array, 1)]
        return out

    def local(
        tokens,
        doc_lengths,
        w_query,
        b_query,
        w_key,
        w_value,
        b_value,
        w_output,
        b_output,
        gain_attn,
        shift_attn,
        w_expand,
        b_expand,
        w_reduce,
        b_reduce,
        gain_ffn,
        shift_ffn,
        cotangent,
    ):
        row_count, length, width = tokens.shape
        heads = w_query.shape[1] // HD
        hidden = w_expand.shape[1]
        count = row_count * length
        inside = lax.axis_index("dp") % GROUP
        me = lax.axis_index("mp")
        ends = jnp.cumsum(doc_lengths, axis=-1)
        longest = jnp.max(doc_lengths, axis=-1, keepdims=True)
        offset = jnp.max(jnp.where(doc_lengths == longest, ends - doc_lengths, 0), axis=-1)
        place = jnp.stack([inside ^ i for i in range(GROUP)] + [me])
        place = jnp.concatenate([place, offset]).astype(jnp.int32)

        by_head = lambda w: w.T.reshape(heads, HD, width)
        own_heads = jnp.concatenate([by_head(w_query), by_head(w_key), by_head(w_value)], axis=1)
        own_heads = own_heads.reshape(3 * heads * HD, width)
        blank = jnp.zeros((width - 2 * heads * HD,), BF16)
        own_bias = jnp.stack(
            [jnp.concatenate([b_query, b_value, blank]), b_expand]
            + [jnp.zeros((width,), BF16)] * 6
        ).astype(F32)

        def piece_of(array, bits=0):
            size = array.shape[0] // GROUP
            return lax.dynamic_slice_in_dim(array, (inside ^ bits) * size, size, 0).astype(F32)

        piece = piece_of(own_heads)
        near = from_peers(jnp.concatenate([piece, own_bias]))

        position = (jnp.arange(length, dtype=jnp.int32)[None] + offset[:, None]) % length
        segment = jnp.sum((position[:, :, None] >= ends[:, None, :]).astype(jnp.int32), axis=-1)
        segment = segment.reshape(1, count)
        docs = doc_lengths.shape[1]
        label = jnp.arange(EXTRA, dtype=jnp.int32)[:, None]
        is_doc = label < docs
        qf = jnp.where(is_doc & (segment == label), 1.0, 0.0).astype(BF16)
        kf = jnp.where(
            is_doc,
            jnp.where(segment == label, 0.0, MASK),
            jnp.where(label < docs + 3, 1.0, 0.0),
        ).astype(BF16)
        inputs, cot = shift(
            place, length, tokens.reshape(count, width), cotangent.reshape(count, width)
        )
        own = attend_own(
            length, peers, place, inputs, own_bias, qf, kf, own_heads
        )

        near = after(near, own)
        biases = near[:, -own_bias.shape[0] :]
        all_biases = jnp.concatenate([own_bias[None], biases])
        near = near[:, : -own_bias.shape[0]]
        cut = piece.shape[0] // 16 * 8
        share = jnp.concatenate([piece_of(w_expand), piece_of(w_output)])
        near_expand = swapped(share, near)
        sides = both(near)
        corners = corner(*sides, cut)
        pieces = listed(near, *sides, *corners, cut)
        sides_expand = both(after(near_expand, corners))
        near_reduce = swapped(piece_of(w_reduce), near_expand, [array for array, _, _ in pieces])
        weights, qkv, ctx, aug = attend_peers(
            length, peers, place, inputs, after(biases, near_expand), qf, kf, pieces, own
        )

        sides_expand = after(sides_expand, ctx)
        cut = share.shape[0] // 2 // 16 * 16 + 16
        corners = corner(*sides_expand, cut)
        vectors = jnp.stack(
            [b_output, gain_attn, shift_attn, b_reduce, gain_ffn, shift_ffn]
            + [jnp.zeros((width,), BF16)] * 2
        ).astype(F32)
        pieces = listed(near_expand, *sides_expand, *corners, cut)
        near_reduce = after(near_reduce, sides_expand)
        diagonal = swapped(piece_of(w_reduce, 6), near_reduce)
        sides_reduce = both(near_reduce)
        residual, act, slope, all_expand, all_output = expand(
            place,
            inputs,
            ctx,
            after(all_biases, near_reduce),
            vectors,
            w_expand,
            w_output,
            pieces,
            peers,
        )
        far_reduce = after((*sides_reduce, diagonal), act)
        pieces = with_core([(array, rel, 0) for rel, array in enumerate([near_reduce, *far_reduce])])
        shifted, grad_two, all_reduce, mine, send, small_one = reduce(
            place, residual, cot, act, slope, vectors, w_reduce, pieces
        )
        got = flip(send, 1)
        output = unshift(place, length, shifted)
        chip = mine + after(got, output)
        early = swap_plane(chip)
        grad_one, dctx, dwo, small = back_to_context(
            place,
            residual,
            grad_two,
            slope,
            ctx,
            all_expand,
            all_reduce,
            all_output,
            after(vectors, chip),
        )
        cut = width // GROUP
        early = sum_groups(jnp.sum(after(early, grad_one), axis=0))[None]
        sides = both(early)
        dqkv, mine, send = attend_back_own(
            length, place, qkv, ctx, aug, dctx, after(kf, early), inputs, dwo, small, small_one
        )
        got = flip(after(send, sides), 1)
        dqkv = attend_back(
            length, peers, 1, 1, place, qkv, ctx, aug, dctx, after(kf, sides), dqkv
        )
        corners = corner(*sides, cut)
        beside = [flip(array, 1) for array in (early, *sides)]
        parts = partial_sums(mine, got, dqkv)
        rest = exchange(parts)
        corners, beside, kept = after((corners, beside, kf), parts)
        dqkv = attend_back(length, peers, 2, peers - 2, place, qkv, ctx, aug, dctx, kept, dqkv)
        total = total_of(parts[0], rest, dqkv)
        second = [total] + exchange([None] + [total] * 3)
        beside += [flip(array, 1) for array in corners]
        pieces = []
        spots = ((0, 0), (2, 0), (4, 0), (6, 0), (6, cut))
        for near, far, (index, top) in zip((early, *sides, *corners), beside, spots):
            pieces += [(near, index, top), (far, index + 1, top)]
        grad_one = after(grad_one, total, beside)
        grad_tokens = input_grads(place, length, grad_one, dqkv, weights)
        second = finish(second, grad_tokens)
        dwe, dwr = spread(place, pieces, [width // GROUP, hidden // GROUP])
        dq, dk, dv, dwo, small_two = spread_late(place, second, heads)
        sums = lambda i: small_two[3 : 3 + heads, i * HD : (i + 1) * HD].reshape(heads * HD)
        shape = (row_count, length, width)
        return (
            output.reshape(shape),
            grad_tokens.reshape(shape),
            dq.T,
            sums(0),
            dk.T,
            dv.T,
            sums(2),
            dwo,
            small_two[0],
            small_two[1],
            small_two[2],
            dwe,
            small_two[11],
            dwr,
            small_two[8],
            small_two[9],
            small_two[10],
        )

    rows, split = P("dp", None, None), P(None, "mp")
    return jax.shard_map(
        local,
        mesh=mesh,
        in_specs=(
            rows,
            P("dp", None),
            split,
            P("mp"),
            split,
            split,
            P("mp"),
            P("mp", None),
            P(),
            P(),
            P(),
            split,
            P("mp"),
            P("mp", None),
            P(),
            P(),
            P(),
            rows,
        ),
        out_specs=(
            rows,
            rows,
            split,
            P("mp"),
            split,
            split,
            P("mp"),
            P("mp", None),
            P(),
            P(),
            P(),
            split,
            P("mp"),
            P("mp", None),
            P(),
            P(),
            P(),
        ),
        check_vma=False,
    )
```

```python
import jax
import jax.numpy as jnp
from jax import lax
from jax.experimental import pallas as pl
from jax.experimental.pallas import tpu as pltpu
from jax.sharding import PartitionSpec as P

HD = 64
GROUP = 8
EXTRA = 16
MASK = -float(2**30)
EPS = 1e-12
F32 = jnp.float32
BF16 = jnp.bfloat16
LIMIT = 60 << 20


def dot(left, right, left_dim, right_dim):
    return lax.dot_general(
        left, right, (((left_dim,), (right_dim,)), ((), ())), preferred_element_type=F32
    )


def params():
    return pltpu.CompilerParams(vmem_limit_bytes=LIMIT)


def cost(flops, moved):
    return pl.CostEstimate(flops=int(flops), bytes_accessed=int(moved), transcendentals=0)


def whole(shape):
    zeros = (0,) * len(shape)
    return pl.BlockSpec(shape, lambda *_: zeros, pipeline_mode=pl.Buffered(1))


def split3(row):
    high = row.astype(BF16).astype(F32)
    rest = row - high
    mid = rest.astype(BF16).astype(F32)
    return high, mid, rest - mid


def rows_of(height, first, parts, width):
    place = lax.broadcasted_iota(jnp.int32, (height, width), 0)
    out = jnp.zeros((height, width), F32)
    for i, part in enumerate(parts):
        out = jnp.where(place == first + i, part, out)
    return out


def put(out_ref, start, values, step):
    rows = pl.ds(pl.multiple_of(start, step), values.shape[0])
    out_ref[rows, :] = values.astype(out_ref.dtype)


def peer_shard(place_ref, shards, k):
    return lax.rem(place_ref[GROUP] + shards - k, shards)


def own_block(*shape):
    return pl.BlockSpec(shape, lambda i, p: (p[GROUP],) + (0,) * (len(shape) - 2) + (i,))


def peer_block(peers, first, *shape):
    middle = (0,) * (len(shape) - 2)
    return pl.BlockSpec(
        shape, lambda k, i, p: (lax.rem(p[GROUP] + peers - first - k, peers),) + middle + (i,)
    )


ANY = pl.BlockSpec(memory_space=pl.ANY)


def shift_matrix(amount, length, forward):
    row = lax.broadcasted_iota(jnp.int32, (length, length), 0)
    column = lax.broadcasted_iota(jnp.int32, (length, length), 1)
    apart = column - row if forward else row - column
    return jnp.where((apart == amount) | (apart == amount - length), 1.0, 0.0).astype(BF16)


def shift_kernel(place_ref, first_ref, second_ref, first_out, second_out):
    length = first_ref.shape[0]
    amount = place_ref[GROUP + 1 + pl.program_id(0)]
    matrix = shift_matrix(amount, length, True)
    first_out[...] = dot(matrix, first_ref[...], 1, 0).astype(BF16)
    second_out[...] = dot(matrix, second_ref[...], 1, 0).astype(BF16)


def shift(place, length, first, second):
    tokens, width = first.shape
    by_row = lambda: pl.BlockSpec((length, width), lambda i, *_: (i, 0))
    return pl.pallas_call(
        shift_kernel,
        grid_spec=pltpu.PrefetchScalarGridSpec(
            num_scalar_prefetch=1,
            grid=(tokens // length,),
            in_specs=[by_row(), by_row()],
            out_specs=[by_row(), by_row()],
        ),
        out_shape=[jax.ShapeDtypeStruct((tokens, width), BF16)] * 2,
        compiler_params=params(),
        cost_estimate=cost(4 * tokens * length * width, 12e6),
        name="shift",
    )(place, first, second)


def unshift_kernel(place_ref, in_ref, out_ref):
    length = in_ref.shape[0]
    matrix = shift_matrix(place_ref[GROUP + 1 + pl.program_id(0)], length, False)
    out_ref[...] = dot(matrix, in_ref[...], 1, 0).astype(BF16)


def unshift(place, length, shifted):
    tokens, width = shifted.shape
    by_row = lambda: pl.BlockSpec((length, width), lambda i, *_: (i, 0))
    return pl.pallas_call(
        unshift_kernel,
        grid_spec=pltpu.PrefetchScalarGridSpec(
            num_scalar_prefetch=1,
            grid=(tokens // length,),
            in_specs=[by_row()],
            out_specs=by_row(),
        ),
        out_shape=jax.ShapeDtypeStruct((tokens, width), BF16),
        compiler_params=params(),
        cost_estimate=cost(2 * tokens * length * width, 6e6),
        name="unshift",
    )(place, shifted)


def tiles(heads, block):
    return [(h, slice(i * block, (i + 1) * block)) for h in range(heads) for i in range(2)]


def attend_rows(x_ref, bias_ref, qf_ref, kf_ref, w_scr, qkv_ref, ctx_ref, aug_ref):
    heads = ctx_ref.shape[0]
    length = x_ref.shape[0]
    block = length // 2
    span = 3 * HD
    proj = dot(w_scr[...], x_ref[...], 1, 1)
    scale = HD ** (-0.5)
    column = bias_ref[...].T[:, 0:1]
    for h in range(heads):
        part = proj[h * span : (h + 1) * span]
        queries = part[:HD] + column[h * HD : (h + 1) * HD]
        values = part[2 * HD :] + column[(heads + h) * HD : (heads + h + 1) * HD]
        qkv_ref[h, :HD, :] = (queries * scale).astype(BF16)
        qkv_ref[h, HD : 2 * HD, :] = part[HD : 2 * HD].astype(BF16)
        qkv_ref[h, 2 * HD :, :] = values.astype(BF16)
    ones_rows = rows_of(EXTRA, 0, (jnp.ones((1, block), F32),), block).astype(BF16)
    items = tiles(heads, block)
    scores = []
    for h, at in items:
        queries = jnp.concatenate([qkv_ref[h, :HD, at], qf_ref[:, at]], axis=0)
        keys = jnp.concatenate([qkv_ref[h, HD : 2 * HD, at], kf_ref[:, at]], axis=0)
        scores.append(dot(keys, queries, 0, 0))
    highest = [jnp.max(part, axis=0, keepdims=True) for part in scores]
    weight = [jnp.exp(part - top).astype(BF16) for part, top in zip(scores, highest)]
    context = []
    for (h, at), part in zip(items, weight):
        values = jnp.concatenate([qkv_ref[h, 2 * HD :, at], ones_rows], axis=0)
        context.append(dot(values, part, 1, 0))
    for (h, at), part, top in zip(items, context, highest):
        total = part[HD : HD + 1]
        ctx_ref[h, :, at] = (part[:HD] * (1.0 / total)).astype(BF16)
        log_total = top + jnp.log(total)
        extra = rows_of(EXTRA, 4, split3(-log_total), block)
        aug_ref[h, :, at] = (extra + qf_ref[:, at].astype(F32)).astype(BF16)


def attend_own_kernel(place_ref, x_ref, bias_ref, qf_ref, kf_ref, own_ref, *refs):
    w_ref, qkv_ref, ctx_ref, aug_ref = refs

    @pl.when(pl.program_id(0) == 0)
    def _():
        w_ref[...] = own_ref[...]

    attend_rows(x_ref, bias_ref, qf_ref, kf_ref, w_ref, qkv_ref, ctx_ref, aug_ref)


def attend_own(length, peers, place, inputs, bias, qf, kf, own):
    heads = own.shape[0] // (3 * HD)
    tokens, width = inputs.shape
    every = peers * heads
    shapes = [(every * 3 * HD, width)] + [(every, n, tokens) for n in (3 * HD, HD, EXTRA)]
    by_row = pl.BlockSpec((EXTRA, length), lambda i, *_: (0, i))
    return pl.pallas_call(
        attend_own_kernel,
        grid_spec=pltpu.PrefetchScalarGridSpec(
            num_scalar_prefetch=1,
            grid=(tokens // length,),
            in_specs=[
                pl.BlockSpec((length, width), lambda i, *_: (i, 0)),
                whole(bias.shape),
                by_row,
                by_row,
                whole(own.shape),
            ],
            out_specs=[
                pl.BlockSpec((heads * 3 * HD, width), lambda i, p: (p[GROUP], 0)),
                *[own_block(heads, n, length) for n in (3 * HD, HD, EXTRA)],
            ],
        ),
        out_shape=[jax.ShapeDtypeStruct(shape, BF16) for shape in shapes],
        compiler_params=params(),
        cost_estimate=cost(heads * tokens * (6 * HD * width + 16 * 64 * length), 12e6),
        name="attend_own",
    )(place, inputs, bias, qf, kf, own)


def attend_peers_kernel(spots, place_ref, x_ref, bias_ref, qf_ref, kf_ref, *refs):
    count = len(spots)
    parts = refs[:count]
    w_ref, qkv_ref, ctx_ref, aug_ref, wide_scr = refs[count + 4 :]

    @pl.when(pl.program_id(1) == 0)
    def _():
        size = w_ref.shape[0] // GROUP
        for ref, (index, offset) in zip(parts, spots):
            put(wide_scr, place_ref[index] * size + offset, ref[0], 8)
        w_ref[...] = wide_scr[...].astype(BF16)

    attend_rows(x_ref, bias_ref.at[0], qf_ref, kf_ref, w_ref, qkv_ref, ctx_ref, aug_ref)


def attend_peers(length, peers, place, inputs, bias, qf, kf, pieces, arrays):
    heads = arrays[1].shape[0] // peers
    tokens, width = inputs.shape
    spots = [(index, offset) for _, index, offset in pieces]
    parts = [array for array, _, _ in pieces]
    by_row = pl.BlockSpec((EXTRA, length), lambda k, i, *_: (0, i))
    return pl.pallas_call(
        lambda *refs: attend_peers_kernel(spots, *refs),
        grid_spec=pltpu.PrefetchScalarGridSpec(
            num_scalar_prefetch=1,
            grid=(peers - 1, tokens // length),
            in_specs=[
                pl.BlockSpec((length, width), lambda k, i, *_: (i, 0)),
                pl.BlockSpec((1,) + bias.shape[1:], lambda k, i, *_: (k, 0, 0)),
                by_row,
                by_row,
                *[
                    pl.BlockSpec((1,) + a.shape[1:], lambda k, i, *_: (k, 0, 0)) for a in parts
                ],
                *[ANY] * 4,
            ],
            out_specs=[
                pl.BlockSpec(
                    (heads * 3 * HD, width),
                    lambda k, i, p: (lax.rem(p[GROUP] + peers - 1 - k, peers), 0),
                ),
                *[peer_block(peers, 1, heads, n, length) for n in (3 * HD, HD, EXTRA)],
            ],
            scratch_shapes=[pltpu.VMEM((heads * 3 * HD, width), F32)],
        ),
        out_shape=[jax.ShapeDtypeStruct(a.shape, a.dtype) for a in arrays],
        input_output_aliases={5 + len(parts) + i: i for i in range(4)},
        compiler_params=params(),
        cost_estimate=cost(
            (peers - 1) * heads * tokens * (6 * HD * width + 16 * 64 * length), 30e6
        ),
        name="attend_peers",
    )(place, inputs, bias, qf, kf, *parts, *arrays)


def attend_back_rows(qkv_ref, ctx_ref, aug_ref, grad_ref, kf_ref, out_ref):
    heads, _, length = ctx_ref.shape
    block = length // 2
    scale = HD ** (-0.5)
    one = jnp.ones((1, block), F32)
    ones_rows = rows_of(EXTRA, 0, (one, one, one), block).astype(BF16)
    items = tiles(heads, block)
    scores, spreads = [], []
    for h, at in items:
        scores.append(
            dot(
                jnp.concatenate([qkv_ref[h, HD : 2 * HD, at], kf_ref[:, at]], axis=0),
                jnp.concatenate([qkv_ref[h, :HD, at], aug_ref[h, :, at]], axis=0),
                0,
                0,
            )
        )
    for h, at in items:
        grad = grad_ref[h, :, at]
        inner = jnp.sum(grad.astype(F32) * ctx_ref[h, :, at].astype(F32), axis=0, keepdims=True)
        grad_extra = rows_of(EXTRA, 0, split3(-inner), block).astype(BF16)
        spreads.append(
            dot(
                jnp.concatenate([qkv_ref[h, 2 * HD :, at], ones_rows], axis=0),
                jnp.concatenate([grad, grad_extra], axis=0),
                0,
                0,
            )
        )
    probs = [jnp.exp(part) for part in scores]
    slopes = [(part * spread).astype(BF16) for part, spread in zip(probs, spreads)]
    probs = [part.astype(BF16) for part in probs]
    for (h, at), part in zip(items, probs):
        out_ref[h, 2 * HD :, at] = dot(grad_ref[h, :, at], part, 1, 1).astype(BF16)
    for (h, at), part in zip(items, slopes):
        out_ref[h, HD : 2 * HD, at] = dot(qkv_ref[h, :HD, at], part, 1, 1).astype(BF16)
    for (h, at), part in zip(items, slopes):
        grad = dot(qkv_ref[h, HD : 2 * HD, at], part, 1, 0)
        out_ref[h, :HD, at] = (grad * scale).astype(BF16)


def attend_back_own_kernel(place_ref, qkv_ref, ctx_ref, aug_ref, grad_ref, kf_ref, *refs):
    x_ref, dwo_ref, small_ref, early_ref, out_ref, mine_ref, send_ref, grad_scr, sum_scr = refs
    heads = ctx_ref.shape[0]
    height = heads * HD
    step = pl.program_id(0)

    @pl.when(step == 0)
    def _():
        grad_scr[...] = jnp.zeros_like(grad_scr)
        sum_scr[...] = jnp.zeros_like(sum_scr)

    attend_back_rows(qkv_ref, ctx_ref, aug_ref, grad_ref, kf_ref, out_ref)
    ones = jnp.ones((8, x_ref.shape[0]), BF16)
    row = lax.broadcasted_iota(jnp.int32, (8, 3 * HD), 0)
    sums = jnp.zeros((8, 3 * HD), F32)
    for h in range(heads):
        grad = dot(out_ref[h], x_ref[...], 1, 0)
        for i in range(3):
            grad_scr[i * height + h * HD : i * height + (h + 1) * HD, :] += grad[
                i * HD : (i + 1) * HD
            ]
        sums = jnp.where(row == 3 + h, dot(ones, out_ref[h], 1, 1), sums)
    sum_scr[:, : 3 * HD] += sums

    @pl.when(step == pl.num_programs(0) - 1)
    def _():
        size, size_two = 3 * height // GROUP, height // GROUP
        top = size + size_two
        for rel in range(4):
            for source, ref in enumerate((mine_ref, send_ref)):
                owner = place_ref[2 * rel + source]
                ref[rel, :size, :] = grad_scr[pl.ds(pl.multiple_of(owner * size, 8), size), :]
                start = pl.multiple_of(owner * size_two, 8)
                ref[rel, size:top, :] = dwo_ref[pl.ds(start, size_two), :]
                ref[rel, top : top + 8, :] = jnp.where(
                    owner == 0, small_ref[...] + sum_scr[...], 0.0
                )
                ref[rel, top + 8 :, :] = jnp.where(owner == 0, early_ref[...], 0.0)


def attend_back_own(length, place, qkv, ctx, aug, grad, kf, inputs, dwo, small, early):
    height, width = dwo.shape
    heads = height // HD
    tokens = inputs.shape[0]
    share = 4 * height // GROUP + 16
    return pl.pallas_call(
        attend_back_own_kernel,
        grid_spec=pltpu.PrefetchScalarGridSpec(
            num_scalar_prefetch=1,
            grid=(tokens // length,),
            in_specs=[
                own_block(heads, 3 * HD, length),
                own_block(heads, HD, length),
                own_block(heads, EXTRA, length),
                own_block(heads, HD, length),
                pl.BlockSpec((EXTRA, length), lambda i, *_: (0, i)),
                pl.BlockSpec((length, width), lambda i, *_: (i, 0)),
                whole(dwo.shape),
                whole(small.shape),
                whole(early.shape),
            ],
            out_specs=[
                own_block(heads, 3 * HD, length),
                whole((4, share, width)),
                whole((4, share, width)),
            ],
            scratch_shapes=[pltpu.VMEM((3 * height, width), F32), pltpu.VMEM((8, width), F32)],
        ),
        out_shape=[jax.ShapeDtypeStruct(qkv.shape, BF16)]
        + [jax.ShapeDtypeStruct((4, share, width), F32)] * 2,
        compiler_params=params(),
        cost_estimate=cost(heads * tokens * (20 * 64 * length + 6 * HD * width), 12e6),
        name="attend_back_own",
    )(place, qkv, ctx, aug, grad, kf, inputs, dwo, small, early)


def attend_back_kernel(place_ref, qkv_ref, ctx_ref, aug_ref, grad_ref, kf_ref, old_ref, out_ref):
    attend_back_rows(qkv_ref, ctx_ref, aug_ref, grad_ref, kf_ref, out_ref)


def attend_back(length, peers, first, count, place, qkv, ctx, aug, grad, kf, out):
    every, _, tokens = qkv.shape
    heads = every // peers
    by_peer = lambda n: peer_block(peers, first, heads, n, length)
    return pl.pallas_call(
        attend_back_kernel,
        grid_spec=pltpu.PrefetchScalarGridSpec(
            num_scalar_prefetch=1,
            grid=(count, tokens // length),
            in_specs=[
                by_peer(3 * HD),
                by_peer(HD),
                by_peer(EXTRA),
                by_peer(HD),
                pl.BlockSpec((EXTRA, length), lambda k, i, *_: (0, i)),
                ANY,
            ],
            out_specs=by_peer(3 * HD),
        ),
        out_shape=jax.ShapeDtypeStruct(out.shape, BF16),
        input_output_aliases={6: 0},
        compiler_params=params(),
        cost_estimate=cost(count * heads * tokens * 20 * 64 * length, 12e6),
        name="attend_back",
    )(place, qkv, ctx, aug, grad, kf, out)


def norm_forward(hidden):
    center = hidden - jnp.mean(hidden, axis=-1, keepdims=True)
    inverse = lax.rsqrt(jnp.mean(center * center, axis=-1, keepdims=True) + EPS)
    return center * inverse, inverse


def norm_backward(grad, gain, norm, inverse):
    scaled = grad * gain
    first = jnp.mean(scaled, axis=-1, keepdims=True)
    second = jnp.mean(scaled * norm, axis=-1, keepdims=True)
    return (scaled - first - norm * second) * inverse


def column_sum(values):
    return jnp.sum(values, axis=0, keepdims=True)


def flat(values):
    return values.reshape(-1, values.shape[-1])


def fill(place_ref, own_ref, parts, spots, out_ref):
    shards, height, _ = out_ref.shape
    out_ref[place_ref[GROUP]] = own_ref[...]
    for k in range(1, shards):
        shard = peer_shard(place_ref, shards, k)
        for ref, (index, offset) in zip(parts, spots):
            start = place_ref[index] * (height // GROUP) + offset
            put(out_ref.at[shard], start, ref[k - 1], 16)


def expand_kernel(spots, place_ref, x_ref, ctx_ref, bias_ref, vec_ref, own_ref, own_wo_ref, *refs):
    parts, refs = refs[: len(spots)], refs[len(spots) :]
    sum_ref, act_ref, slope_ref, full_ref, wo_ref, we_ref, wide_scr, low_scr, sem = refs
    shards, width, _ = we_ref.shape
    size, size_two = width // GROUP, wo_ref.shape[0] // (shards * GROUP)
    kept = pltpu.make_async_copy(we_ref, full_ref, sem)

    @pl.when(pl.program_id(0) == 0)
    def _():
        me = place_ref[GROUP]
        we_ref[me] = own_ref[...]
        put(wide_scr, me * size_two * GROUP, own_wo_ref[...], 8)
        for k in range(1, shards):
            shard = peer_shard(place_ref, shards, k)
            for ref, (index, offset) in zip(parts, spots):
                part = ref[k - 1]
                count = min(part.shape[0], size - offset)
                put(we_ref.at[shard], place_ref[index] * size + offset, part[:count], 16)
                if count < part.shape[0]:
                    start = (shard * GROUP + place_ref[index]) * size_two
                    put(wide_scr, start, part[count:], 8)
        wo_ref[...] = wide_scr[...].astype(BF16)
        kept.start()

    @pl.when(pl.program_id(0) == pl.num_programs(0) - 1)
    def _():
        kept.wait()

    b_output, gain_one, shift_one = vec_ref[0:1], vec_ref[1:2], vec_ref[2:3]
    half = x_ref.shape[0] // 2
    halves = [slice(0, half), slice(half, 2 * half)]
    attended = [dot(flat(ctx_ref[:, :, at]), wo_ref[...], 0, 0) for at in halves]
    for at, part in zip(halves, attended):
        residual = x_ref[at, :].astype(F32) + (part + b_output)
        sum_ref[at, :] = residual
        norm_one, _ = norm_forward(residual)
        low_scr[at, :] = (norm_one * gain_one + shift_one).astype(BF16)

    def shard_step(s, carry):
        bias = bias_ref[peer_shard(place_ref, shards, s), 1:2]
        products = [dot(low_scr[at, :], we_ref[s], 1, 0) for at in halves]
        for at, product in zip(halves, products):
            hidden = product + bias
            square = hidden * hidden
            bent = jnp.tanh(hidden * (0.7978845608028654 + 0.035677408136300125 * square))
            gate = 0.5 + 0.5 * bent
            active = hidden * gate
            act_ref[s, at, :] = active.astype(BF16)
            slope = gate + (active * (1.0 - gate)) * (
                1.5957691216057308 + 0.21406444881780075 * square
            )
            slope_ref[s, at, :] = slope.astype(BF16)
        return carry

    lax.fori_loop(0, shards, shard_step, 0, unroll=2)


def expand(place, inputs, ctx, biases, vectors, own, own_wo, pieces, shards):
    tokens, width = inputs.shape
    hidden = own.shape[1]
    every = ctx.shape[0]
    block = 512
    spots = [(index, offset) for _, index, offset in pieces]
    parts = [array for array, _, _ in pieces]
    full = (shards, width, hidden)
    by_token = lambda: pl.BlockSpec((block, width), lambda i, *_: (i, 0))
    by_shard = lambda: pl.BlockSpec((shards, block, hidden), lambda i, *_: (0, i, 0))
    return pl.pallas_call(
        lambda *refs: expand_kernel(spots, *refs),
        grid_spec=pltpu.PrefetchScalarGridSpec(
            num_scalar_prefetch=1,
            grid=(tokens // block,),
            in_specs=[
                by_token(),
                pl.BlockSpec((every, HD, block), lambda i, *_: (0, 0, i)),
                whole(biases.shape),
                whole(vectors.shape),
                whole(own.shape),
                whole(own_wo.shape),
                *[whole(a.shape) for a in parts],
            ],
            out_specs=[by_token(), by_shard(), by_shard(), ANY, whole((every * HD, width))],
            scratch_shapes=[
                pltpu.VMEM(full, BF16),
                pltpu.VMEM((every * HD, width), F32),
                pltpu.VMEM((block, width), BF16),
                pltpu.SemaphoreType.DMA,
            ],
        ),
        out_shape=[
            jax.ShapeDtypeStruct((tokens, width), F32),
            jax.ShapeDtypeStruct((shards, tokens, hidden), BF16),
            jax.ShapeDtypeStruct((shards, tokens, hidden), BF16),
            jax.ShapeDtypeStruct(full, BF16),
            jax.ShapeDtypeStruct((every * HD, width), BF16),
        ],
        compiler_params=params(),
        cost_estimate=cost(2 * tokens * width * (shards * hidden + every * HD), 40e6),
        name="expand",
    )(place, inputs, ctx, biases, vectors, own, own_wo, *parts)


def reduce_kernel(spots, place_ref, sum_ref, cot_ref, act_ref, slope_ref, vec_ref, *refs):
    own_ref, refs = refs[0], refs[1:]
    piece_refs, refs = refs[: len(spots)], refs[len(spots) :]
    out_ref, g2_ref, full_ref, mine_ref, send_ref, small_scr = refs[:6]
    dwe_scr, dwr_scr, wr_ref, sems = refs[6:]
    kept = pltpu.make_async_copy(wr_ref, full_ref, sems.at[0])
    step = pl.program_id(0)
    shards = act_ref.shape[0]
    me = place_ref[GROUP]

    @pl.when(step == 0)
    def _():
        fill(place_ref, own_ref, piece_refs, spots, wr_ref)
        kept.start()
        for scr in (dwe_scr, dwr_scr, small_scr):
            scr[...] = jnp.zeros_like(scr)

    gain_one, shift_one = vec_ref[1:2], vec_ref[2:3]
    b_reduce, gain_two, shift_two = vec_ref[3:4], vec_ref[4:5], vec_ref[5:6]
    half = sum_ref.shape[0] // 2
    halves = [slice(0, half), slice(half, 2 * half)]
    quarter = half // 4
    width = sum_ref.shape[1]
    small = [jnp.zeros((1, width), F32)] * 4

    def norm_part(start, mixed):
        at = slice(start, start + quarter)
        norm_one, _ = norm_forward(sum_ref[at, :])
        normed = norm_one * gain_one + shift_one
        norm_two, inverse_two = norm_forward(normed + (mixed + b_reduce))
        out_ref[at, :] = (norm_two * gain_two + shift_two).astype(BF16)
        cot = cot_ref[at, :].astype(F32)
        grad_two = norm_backward(cot, gain_two, norm_two, inverse_two)
        g2_ref[at, :] = grad_two
        small[0] = small[0] + column_sum(grad_two)
        small[1] = small[1] + column_sum(cot * norm_two)
        small[2] = small[2] + column_sum(cot)
        return grad_two.astype(BF16), normed.astype(BF16)

    first, second = halves
    mixed = dot(act_ref[0, first, :], wr_ref[0], 1, 0)
    for s in range(1, shards):
        mixed = mixed + dot(act_ref[s, first, :], wr_ref[s], 1, 0)
    later = None
    parts = []
    for s in range(shards):
        product = dot(act_ref[s, second, :], wr_ref[s], 1, 0)
        later = product if later is None else later + product
        parts.append(norm_part(s * quarter, mixed[s * quarter : (s + 1) * quarter]))
    low_a = jnp.concatenate([part[0] for part in parts], axis=0)
    normed_a = jnp.concatenate([part[1] for part in parts], axis=0)
    active_a = dot(low_a, own_ref[...], 1, 1)
    parts = [norm_part(half + s * quarter, later[s * quarter : (s + 1) * quarter]) for s in (0, 1)]
    dwr_scr[...] += dot(act_ref[me, first, :], low_a, 0, 0)
    parts += [norm_part(half + s * quarter, later[s * quarter : (s + 1) * quarter]) for s in (2, 3)]
    own_a = (active_a * slope_ref[0, first, :].astype(F32)).astype(BF16)
    low_b = jnp.concatenate([part[0] for part in parts], axis=0)
    normed_b = jnp.concatenate([part[1] for part in parts], axis=0)
    active_b = dot(low_b, own_ref[...], 1, 1)
    small[3] = small[3] + column_sum(own_a.astype(F32))
    dwe_scr[...] += dot(normed_a, own_a, 0, 0)
    own_b = (active_b * slope_ref[0, second, :].astype(F32)).astype(BF16)
    dwr_scr[...] += dot(act_ref[me, second, :], low_b, 0, 0)
    small[3] = small[3] + column_sum(own_b.astype(F32))
    dwe_scr[...] += dot(normed_b, own_b, 0, 0)
    for n, part in enumerate(small):
        small_scr[n : n + 1] += part

    @pl.when(step == pl.num_programs(0) - 1)
    def _():
        copies = [kept]
        for rel in range(4):
            for source, ref in ((1, send_ref), (0, mine_ref)):
                owner = place_ref[2 * rel + source]
                top = 0
                for scr in (dwe_scr, dwr_scr):
                    size = scr.shape[0] // GROUP
                    start = pl.multiple_of(owner * size, 8)
                    copy = pltpu.make_async_copy(
                        scr.at[pl.ds(start, size), :],
                        ref.at[rel, top : top + size, :],
                        sems.at[len(copies)],
                    )
                    copy.start()
                    copies.append(copy)
                    top += size
        for copy in copies:
            copy.wait()


def reduce(place, residual, cot, act, slope, vectors, own, pieces):
    tokens, width = residual.shape
    shards, _, hidden = act.shape
    block = 512
    share = (width + hidden) // GROUP
    spots = [(index, offset) for _, index, offset in pieces]
    arrays = [array for array, _, _ in pieces]
    by_token = lambda: pl.BlockSpec((block, width), lambda i, *_: (i, 0))
    return pl.pallas_call(
        lambda *refs: reduce_kernel(spots, *refs),
        grid_spec=pltpu.PrefetchScalarGridSpec(
            num_scalar_prefetch=1,
            grid=(tokens // block,),
            in_specs=[
                by_token(),
                by_token(),
                pl.BlockSpec((shards, block, hidden), lambda i, *_: (0, i, 0)),
                pl.BlockSpec((1, block, hidden), lambda i, p: (p[GROUP], i, 0)),
                whole(vectors.shape),
                whole(own.shape),
                *[whole(a.shape) for a in arrays],
            ],
            out_specs=[
                by_token(),
                by_token(),
                ANY,
                ANY,
                ANY,
                whole((8, width)),
            ],
            scratch_shapes=[
                pltpu.VMEM((width, hidden), F32),
                pltpu.VMEM((hidden, width), F32),
                pltpu.VMEM((shards, hidden, width), BF16),
                pltpu.SemaphoreType.DMA((17,)),
            ],
        ),
        out_shape=[
            jax.ShapeDtypeStruct((tokens, width), BF16),
            jax.ShapeDtypeStruct((tokens, width), F32),
            jax.ShapeDtypeStruct((shards, hidden, width), BF16),
            jax.ShapeDtypeStruct((4, share, width), F32),
            jax.ShapeDtypeStruct((4, share, width), F32),
            jax.ShapeDtypeStruct((8, width), F32),
        ],
        compiler_params=params(),
        cost_estimate=cost(tokens * width * hidden * (2 * shards + 6), 40e6),
        name="reduce",
    )(place, residual, cot, act, slope, vectors, own, *arrays)


def return_kernel(place_ref, sum_ref, g2_ref, slope_ref, ctx_ref, we_ref, wr_ref, w_ref, *refs):
    vec_ref, g1_ref, dctx_ref, dwo_ref, small_ref = refs
    shards = we_ref.shape[0]

    @pl.when(pl.program_id(0) == 0)
    def _():
        dwo_ref[...] = jnp.zeros_like(dwo_ref)
        small_ref[...] = jnp.zeros_like(small_ref)

    half = sum_ref.shape[0] // 2
    halves = [slice(0, half), slice(half, 2 * half)]
    gain_one = vec_ref[1:2]
    low = [g2_ref[at, :].astype(BF16) for at in halves]
    items = [(s, i) for s in range(shards) for i in range(2)]
    total = [g2_ref[at, :] for at in halves]
    ahead = dot(low[0], wr_ref[0], 1, 1)
    for n, (s, i) in enumerate(items):
        grad_active = ahead
        if n + 1 < len(items):
            s_next, i_next = items[n + 1]
            ahead = dot(low[i_next], wr_ref[s_next], 1, 1)
        grad_hidden = (grad_active * slope_ref[s, halves[i], :].astype(F32)).astype(BF16)
        total[i] = total[i] + dot(grad_hidden, we_ref[s], 1, 1)
    small = [jnp.zeros((1, sum_ref.shape[1]), F32)] * 3
    one = []
    for at, grad_normed in zip(halves, total):
        norm_one, inverse_one = norm_forward(sum_ref[at, :])
        grad_one = norm_backward(grad_normed, gain_one, norm_one, inverse_one)
        g1_ref[at, :] = grad_one
        one.append(grad_one.astype(BF16))
        small[0] = small[0] + column_sum(grad_one)
        small[1] = small[1] + column_sum(grad_normed * norm_one)
        small[2] = small[2] + column_sum(grad_normed)
    one = jnp.concatenate(one, axis=0)
    dctx = dot(w_ref[...], one, 1, 1)
    dwo_ref[...] += dot(flat(ctx_ref[...]), one, 1, 0)
    dctx_ref[...] = dctx.astype(BF16).reshape(dctx_ref.shape)
    for n, part in enumerate(small):
        small_ref[n : n + 1] += part


def back_to_context(place, residual, grad_two, slope, ctx, w_expand, w_reduce, weights, vectors):
    tokens, width = residual.shape
    shards, _, hidden = w_expand.shape
    every = ctx.shape[0]
    heads = every // shards
    block = 512
    by_token = lambda: pl.BlockSpec((block, width), lambda i, *_: (i, 0))
    return pl.pallas_call(
        return_kernel,
        grid_spec=pltpu.PrefetchScalarGridSpec(
            num_scalar_prefetch=1,
            grid=(tokens // block,),
            in_specs=[
                by_token(),
                by_token(),
                pl.BlockSpec((shards, block, hidden), lambda i, *_: (0, i, 0)),
                own_block(heads, HD, block),
                whole(w_expand.shape),
                whole(w_reduce.shape),
                whole(weights.shape),
                whole(vectors.shape),
            ],
            out_specs=[
                by_token(),
                pl.BlockSpec((every, HD, block), lambda i, *_: (0, 0, i)),
                whole((heads * HD, width)),
                whole((8, width)),
            ],
        ),
        out_shape=[
            jax.ShapeDtypeStruct((tokens, width), F32),
            jax.ShapeDtypeStruct(ctx.shape, BF16),
            jax.ShapeDtypeStruct((heads * HD, width), F32),
            jax.ShapeDtypeStruct((8, width), F32),
        ],
        compiler_params=params(),
        cost_estimate=cost(tokens * width * (4 * shards * hidden + 2 * every * HD), 40e6),
        name="back_to_context",
    )(place, residual, grad_two, slope, ctx, w_expand, w_reduce, weights, vectors)


def spread_kernel(spots, place_ref, *refs):
    parts, outs = refs[: len(spots)], refs[len(spots) :]
    for ref, (index, offset) in zip(parts, spots):
        start = 0
        for i, out_ref in enumerate(outs):
            size = out_ref.shape[0] // GROUP
            if offset <= i * size < offset + ref.shape[1]:
                put(out_ref, place_ref[index] * size, ref[0, start : start + size, :], 8)
                start += size


def spread(place, pieces, sizes):
    spots = [(index, offset) for _, index, offset in pieces]
    parts = [array for array, _, _ in pieces]
    width = parts[0].shape[2]
    shapes = [(GROUP * size, width) for size in sizes]
    return pl.pallas_call(
        lambda *refs: spread_kernel(spots, *refs),
        grid_spec=pltpu.PrefetchScalarGridSpec(
            num_scalar_prefetch=1,
            grid=(1,),
            in_specs=[whole(a.shape) for a in parts],
            out_specs=[whole(s) for s in shapes],
        ),
        out_shape=[jax.ShapeDtypeStruct(s, F32) for s in shapes],
        compiler_params=params(),
        cost_estimate=cost(0, 10e6),
        name="spread",
    )(place, *parts)


def spread_late_kernel(heads, place_ref, *refs):
    parts = refs[:GROUP]
    dq_ref, dk_ref, dv_ref, dwo_ref, small_ref, grad_scr = refs[GROUP:]
    height = heads * HD
    size, size_two = 3 * height // GROUP, height // GROUP
    top = size + size_two
    for i, ref in enumerate(parts):
        owner = place_ref[i]
        put(grad_scr, owner * size, ref[:size, :], 8)
        put(dwo_ref, owner * size_two, ref[size:top, :], 8)

        @pl.when(owner == 0)
        def _():
            small_ref[...] = ref[top:, :]

    for i, out_ref in enumerate((dq_ref, dk_ref, dv_ref)):
        out_ref[...] = grad_scr[i * height : (i + 1) * height, :]


def spread_late(place, parts, heads):
    share, width = parts[0].shape
    height = heads * HD
    shapes = [(height, width)] * 4 + [(16, width)]
    return pl.pallas_call(
        lambda *refs: spread_late_kernel(heads, *refs),
        grid_spec=pltpu.PrefetchScalarGridSpec(
            num_scalar_prefetch=1,
            grid=(1,),
            in_specs=[whole(a.shape) for a in parts],
            out_specs=[whole(s) for s in shapes],
            scratch_shapes=[pltpu.VMEM((3 * height, width), F32)],
        ),
        out_shape=[jax.ShapeDtypeStruct(s, F32) for s in shapes],
        compiler_params=params(),
        cost_estimate=cost(0, 8 * parts[0].size * 8),
        name="spread_late",
    )(place, *parts)


def input_grads_kernel(place_ref, g1_ref, grad_ref, w_ref, out_ref):
    amount = place_ref[GROUP + 1 + pl.program_id(0)]
    matrix = shift_matrix(amount, g1_ref.shape[0], False)
    total = g1_ref[...] + dot(flat(grad_ref[...]), w_ref[...], 0, 0)
    out_ref[...] = dot(matrix, total.astype(BF16), 1, 0).astype(BF16)


def input_grads(place, length, grad_one, grads, weights):
    tokens, width = grad_one.shape
    every = grads.shape[0]
    by_row = lambda: pl.BlockSpec((length, width), lambda i, *_: (i, 0))
    return pl.pallas_call(
        input_grads_kernel,
        grid_spec=pltpu.PrefetchScalarGridSpec(
            num_scalar_prefetch=1,
            grid=(tokens // length,),
            in_specs=[
                by_row(),
                pl.BlockSpec((every, 3 * HD, length), lambda i, *_: (0, 0, i)),
                whole(weights.shape),
            ],
            out_specs=by_row(),
        ),
        out_shape=jax.ShapeDtypeStruct((tokens, width), BF16),
        compiler_params=params(),
        cost_estimate=cost(2 * tokens * width * (every * 3 * HD + length), 20e6),
        name="input_grads",
    )(place, grad_one, grads, weights)


def after(values, *others):
    return lax.optimization_barrier((values, others))[0]


def solution(mesh):
    peers = mesh.shape["mp"]
    lanes = mesh.shape["dp"]
    rotations = [[(i, (i + k) % peers) for i in range(peers)] for k in range(1, peers)]

    def flip(values, bits):
        return lax.ppermute(values, "dp", [(i, i ^ bits) for i in range(lanes)])

    def from_peers(piece):
        return jnp.stack([lax.ppermute(piece, "mp", perm) for perm in rotations])

    def swapped(piece, *ready):
        copies = jnp.broadcast_to(piece[None], (peers,) + piece.shape)
        got = lax.all_to_all(after(copies, *ready), "mp", 0, 0, tiled=True)
        me = lax.axis_index("mp")
        return jnp.concatenate(
            [
                lax.dynamic_slice_in_dim(got, lax.rem(me + peers - k, peers), 1, 0)
                for k in range(1, peers)
            ]
        )

    def both(near):
        return flip(near, 2), flip(near, 4)

    def corner(by_x, by_y, cut):
        return flip(by_y[:, :cut], 2), flip(by_x[:, cut:], 4)

    def listed(near, by_x, by_y, first, second, cut):
        places = ((near, 0, 0), (by_x, 1, 0), (by_y, 2, 0), (first, 3, 0), (second, 3, cut))
        return with_core(places)

    def with_core(places):
        out = []
        for array, rel, offset in places:
            out.append((array, 2 * rel, offset))
            out.append((flip(array, 1), 2 * rel + 1, offset))
        return out

    def sum_groups(total):
        step = GROUP
        while step < lanes:
            total = total + flip(total, step)
            step *= 2
        return total

    def partial_sums(mine, got, *ready):
        got = after(got, *ready)
        return [mine[rel] + got[rel] for rel in range(4)]

    def exchange(parts):
        return [flip(parts[rel], 2 * rel) for rel in (1, 2, 3)]

    def total_of(first, rest, *ready):
        rest = after(rest, *ready)
        return sum_groups(first + rest[0] + rest[1] + rest[2])

    def finish(arrays, *ready):
        out = []
        for array in after(arrays, *ready):
            out += [array, flip(array, 1)]
        return out

    def local(
        tokens,
        doc_lengths,
        w_query,
        b_query,
        w_key,
        w_value,
        b_value,
        w_output,
        b_output,
        gain_attn,
        shift_attn,
        w_expand,
        b_expand,
        w_reduce,
        b_reduce,
        gain_ffn,
        shift_ffn,
        cotangent,
    ):
        row_count, length, width = tokens.shape
        heads = w_query.shape[1] // HD
        hidden = w_expand.shape[1]
        count = row_count * length
        inside = lax.axis_index("dp") % GROUP
        me = lax.axis_index("mp")
        ends = jnp.cumsum(doc_lengths, axis=-1)
        longest = jnp.max(doc_lengths, axis=-1, keepdims=True)
        offset = jnp.max(jnp.where(doc_lengths == longest, ends - doc_lengths, 0), axis=-1)
        place = jnp.stack([inside ^ i for i in range(GROUP)] + [me])
        place = jnp.concatenate([place, offset]).astype(jnp.int32)

        by_head = lambda w: w.T.reshape(heads, HD, width)
        own_heads = jnp.concatenate([by_head(w_query), by_head(w_key), by_head(w_value)], axis=1)
        own_heads = own_heads.reshape(3 * heads * HD, width)
        blank = jnp.zeros((width - 2 * heads * HD,), BF16)
        own_bias = jnp.stack(
            [jnp.concatenate([b_query, b_value, blank]), b_expand]
            + [jnp.zeros((width,), BF16)] * 6
        ).astype(F32)

        def piece_of(array, bits=0):
            size = array.shape[0] // GROUP
            return lax.dynamic_slice_in_dim(array, (inside ^ bits) * size, size, 0).astype(F32)

        piece = piece_of(own_heads)
        near = from_peers(jnp.concatenate([piece, own_bias]))

        position = (jnp.arange(length, dtype=jnp.int32)[None] + offset[:, None]) % length
        segment = jnp.sum((position[:, :, None] >= ends[:, None, :]).astype(jnp.int32), axis=-1)
        segment = segment.reshape(1, count)
        docs = doc_lengths.shape[1]
        label = jnp.arange(EXTRA, dtype=jnp.int32)[:, None]
        is_doc = label < docs
        qf = jnp.where(is_doc & (segment == label), 1.0, 0.0).astype(BF16)
        kf = jnp.where(
            is_doc,
            jnp.where(segment == label, 0.0, MASK),
            jnp.where(label < docs + 3, 1.0, 0.0),
        ).astype(BF16)
        inputs, cot = shift(
            place, length, tokens.reshape(count, width), cotangent.reshape(count, width)
        )
        own = attend_own(
            length, peers, place, inputs, own_bias, qf, kf, own_heads
        )

        near = after(near, own)
        biases = near[:, -own_bias.shape[0] :]
        all_biases = jnp.concatenate([own_bias[None], biases])
        near = near[:, : -own_bias.shape[0]]
        cut = piece.shape[0] // 16 * 8
        share = jnp.concatenate([piece_of(w_expand), piece_of(w_output)])
        near_expand = swapped(share, near)
        sides = both(near)
        corners = corner(*sides, cut)
        pieces = listed(near, *sides, *corners, cut)
        sides_expand = both(after(near_expand, corners))
        near_reduce = swapped(piece_of(w_reduce), near_expand, [array for array, _, _ in pieces])
        weights, qkv, ctx, aug = attend_peers(
            length, peers, place, inputs, after(biases, near_expand), qf, kf, pieces, own
        )

        sides_expand = after(sides_expand, ctx)
        cut = share.shape[0] // 2 // 16 * 16 + 16
        corners = corner(*sides_expand, cut)
        vectors = jnp.stack(
            [b_output, gain_attn, shift_attn, b_reduce, gain_ffn, shift_ffn]
            + [jnp.zeros((width,), BF16)] * 2
        ).astype(F32)
        pieces = listed(near_expand, *sides_expand, *corners, cut)
        near_reduce = after(near_reduce, sides_expand)
        diagonal = swapped(piece_of(w_reduce, 6), near_reduce)
        sides_reduce = both(near_reduce)
        residual, act, slope, all_expand, all_output = expand(
            place,
            inputs,
            ctx,
            after(all_biases, near_reduce),
            vectors,
            w_expand,
            w_output,
            pieces,
            peers,
        )
        far_reduce = after((*sides_reduce, diagonal), act)
        pieces = with_core([(array, rel, 0) for rel, array in enumerate([near_reduce, *far_reduce])])
        shifted, grad_two, all_reduce, mine, send, small_one = reduce(
            place, residual, cot, act, slope, vectors, w_reduce, pieces
        )
        got = flip(send, 1)
        output = unshift(place, length, shifted)
        chip = partial_sums(mine, got, output)
        early = exchange(chip)
        grad_one, dctx, dwo, small = back_to_context(
            place,
            residual,
            grad_two,
            slope,
            ctx,
            all_expand,
            all_reduce,
            all_output,
            after(vectors, chip),
        )
        early = total_of(chip[0], early, grad_one)[None]
        sides = both(early)
        dqkv, mine, send = attend_back_own(
            length, place, qkv, ctx, aug, dctx, after(kf, early), inputs, dwo, small, small_one
        )
        got = flip(after(send, sides), 1)
        dqkv = attend_back(
            length, peers, 1, 1, place, qkv, ctx, aug, dctx, after(kf, sides), dqkv
        )
        across = flip(after(early, sides), 6)
        beside = [flip(array, 1) for array in (early, *sides)]
        parts = partial_sums(mine, got, dqkv)
        rest = exchange(parts)
        across, beside, kept = after((across, beside, kf), parts)
        dqkv = attend_back(length, peers, 2, peers - 2, place, qkv, ctx, aug, dctx, kept, dqkv)
        total = total_of(parts[0], rest, dqkv)
        second = [total] + exchange([None] + [total] * 3)
        beside.append(flip(across, 1))
        pieces = []
        for rel, (near, far) in enumerate(zip((early, *sides, across), beside)):
            pieces += [(near, 2 * rel, 0), (far, 2 * rel + 1, 0)]
        grad_one = after(grad_one, total, beside)
        grad_tokens = input_grads(place, length, grad_one, dqkv, weights)
        second = finish(second, grad_tokens)
        dwe, dwr = spread(place, pieces, [width // GROUP, hidden // GROUP])
        dq, dk, dv, dwo, small_two = spread_late(place, second, heads)
        sums = lambda i: small_two[3 : 3 + heads, i * HD : (i + 1) * HD].reshape(heads * HD)
        shape = (row_count, length, width)
        return (
            output.reshape(shape),
            grad_tokens.reshape(shape),
            dq.T,
            sums(0),
            dk.T,
            dv.T,
            sums(2),
            dwo,
            small_two[0],
            small_two[1],
            small_two[2],
            dwe,
            small_two[11],
            dwr,
            small_two[8],
            small_two[9],
            small_two[10],
        )

    rows, split = P("dp", None, None), P(None, "mp")
    return jax.shard_map(
        local,
        mesh=mesh,
        in_specs=(
            rows,
            P("dp", None),
            split,
            P("mp"),
            split,
            split,
            P("mp"),
            P("mp", None),
            P(),
            P(),
            P(),
            split,
            P("mp"),
            P("mp", None),
            P(),
            P(),
            P(),
            rows,
        ),
        out_specs=(
            rows,
            rows,
            split,
            P("mp"),
            split,
            split,
            P("mp"),
            P("mp", None),
            P(),
            P(),
            P(),
            split,
            P("mp"),
            P("mp", None),
            P(),
            P(),
            P(),
        ),
        check_vma=False,
    )
```

```python
import jax
import jax.numpy as jnp
from jax import lax
from jax.experimental import pallas as pl
from jax.experimental.pallas import tpu as pltpu
from jax.sharding import PartitionSpec as P

HD = 64
GROUP = 8
EXTRA = 16
MASK = -float(2**30)
EPS = 1e-12
F32 = jnp.float32
BF16 = jnp.bfloat16
LIMIT = 60 << 20


def dot(left, right, left_dim, right_dim):
    return lax.dot_general(
        left, right, (((left_dim,), (right_dim,)), ((), ())), preferred_element_type=F32
    )


def params(limit=LIMIT):
    return pltpu.CompilerParams(vmem_limit_bytes=limit)


def cost(flops, moved):
    return pl.CostEstimate(flops=int(flops), bytes_accessed=int(moved), transcendentals=0)


def whole(shape):
    zeros = (0,) * len(shape)
    return pl.BlockSpec(shape, lambda *_: zeros, pipeline_mode=pl.Buffered(1))


def split3(row):
    high = row.astype(BF16).astype(F32)
    rest = row - high
    mid = rest.astype(BF16).astype(F32)
    return high, mid, rest - mid


def rows_of(height, first, parts, width):
    place = lax.broadcasted_iota(jnp.int32, (height, width), 0)
    out = jnp.zeros((height, width), F32)
    for i, part in enumerate(parts):
        out = jnp.where(place == first + i, part, out)
    return out


def put(out_ref, start, values, step):
    rows = pl.ds(pl.multiple_of(start, step), values.shape[0])
    out_ref[rows, :] = values.astype(out_ref.dtype)


def peer_shard(place_ref, shards, k):
    return lax.rem(place_ref[GROUP] + shards - k, shards)


def own_block(*shape):
    return pl.BlockSpec(shape, lambda i, p: (p[GROUP],) + (0,) * (len(shape) - 2) + (i,))


def peer_block(peers, first, *shape):
    middle = (0,) * (len(shape) - 2)
    return pl.BlockSpec(
        shape, lambda k, i, p: (lax.rem(p[GROUP] + peers - first - k, peers),) + middle + (i,)
    )


ANY = pl.BlockSpec(memory_space=pl.ANY)


def shift_matrix(amount, length, forward):
    row = lax.broadcasted_iota(jnp.int32, (length, length), 0)
    column = lax.broadcasted_iota(jnp.int32, (length, length), 1)
    apart = column - row if forward else row - column
    return jnp.where((apart == amount) | (apart == amount - length), 1.0, 0.0).astype(BF16)


def shift_kernel(place_ref, first_ref, second_ref, first_out, second_out):
    length = first_ref.shape[0]
    amount = place_ref[GROUP + 1 + pl.program_id(0)]
    matrix = shift_matrix(amount, length, True)
    first_out[...] = dot(matrix, first_ref[...], 1, 0).astype(BF16)
    second_out[...] = dot(matrix, second_ref[...], 1, 0).astype(BF16)


def shift(place, length, first, second):
    tokens, width = first.shape
    by_row = lambda: pl.BlockSpec((length, width), lambda i, *_: (i, 0))
    return pl.pallas_call(
        shift_kernel,
        grid_spec=pltpu.PrefetchScalarGridSpec(
            num_scalar_prefetch=1,
            grid=(tokens // length,),
            in_specs=[by_row(), by_row()],
            out_specs=[by_row(), by_row()],
        ),
        out_shape=[jax.ShapeDtypeStruct((tokens, width), BF16)] * 2,
        compiler_params=params(),
        cost_estimate=cost(4 * tokens * length * width, 12e6),
        name="shift",
    )(place, first, second)


def unshift_kernel(place_ref, in_ref, out_ref):
    length = in_ref.shape[0]
    matrix = shift_matrix(place_ref[GROUP + 1 + pl.program_id(0)], length, False)
    out_ref[...] = dot(matrix, in_ref[...], 1, 0).astype(BF16)


def unshift(place, length, shifted):
    tokens, width = shifted.shape
    by_row = lambda: pl.BlockSpec((length, width), lambda i, *_: (i, 0))
    return pl.pallas_call(
        unshift_kernel,
        grid_spec=pltpu.PrefetchScalarGridSpec(
            num_scalar_prefetch=1,
            grid=(tokens // length,),
            in_specs=[by_row()],
            out_specs=by_row(),
        ),
        out_shape=jax.ShapeDtypeStruct((tokens, width), BF16),
        compiler_params=params(),
        cost_estimate=cost(2 * tokens * length * width, 6e6),
        name="unshift",
    )(place, shifted)


def tiles(heads, block):
    return [(h, slice(i * block, (i + 1) * block)) for h in range(heads) for i in range(2)]


def attend_rows(x_ref, bias_ref, qf_ref, kf_ref, w_scr, qkv_ref, ctx_ref, aug_ref):
    heads = ctx_ref.shape[0]
    length = x_ref.shape[0]
    block = length // 2
    span = 3 * HD
    proj = dot(w_scr[...], x_ref[...], 1, 1)
    scale = HD ** (-0.5)
    column = bias_ref[...].T[:, 0:1]
    for h in range(heads):
        part = proj[h * span : (h + 1) * span]
        queries = part[:HD] + column[h * HD : (h + 1) * HD]
        values = part[2 * HD :] + column[(heads + h) * HD : (heads + h + 1) * HD]
        qkv_ref[h, :HD, :] = (queries * scale).astype(BF16)
        qkv_ref[h, HD : 2 * HD, :] = part[HD : 2 * HD].astype(BF16)
        qkv_ref[h, 2 * HD :, :] = values.astype(BF16)
    ones_rows = rows_of(EXTRA, 0, (jnp.ones((1, block), F32),), block).astype(BF16)
    items = tiles(heads, block)
    scores = []
    for h, at in items:
        queries = jnp.concatenate([qkv_ref[h, :HD, at], qf_ref[:, at]], axis=0)
        keys = jnp.concatenate([qkv_ref[h, HD : 2 * HD, at], kf_ref[:, at]], axis=0)
        scores.append(dot(keys, queries, 0, 0))
    highest = [jnp.max(part, axis=0, keepdims=True) for part in scores]
    weight = [jnp.exp(part - top).astype(BF16) for part, top in zip(scores, highest)]
    context = []
    for (h, at), part in zip(items, weight):
        values = jnp.concatenate([qkv_ref[h, 2 * HD :, at], ones_rows], axis=0)
        context.append(dot(values, part, 1, 0))
    for (h, at), part, top in zip(items, context, highest):
        total = part[HD : HD + 1]
        ctx_ref[h, :, at] = (part[:HD] * (1.0 / total)).astype(BF16)
        log_total = top + jnp.log(total)
        extra = rows_of(EXTRA, 4, split3(-log_total), block)
        aug_ref[h, :, at] = (extra + qf_ref[:, at].astype(F32)).astype(BF16)


def attend_own_kernel(place_ref, x_ref, bias_ref, qf_ref, kf_ref, own_ref, *refs):
    w_ref, qkv_ref, ctx_ref, aug_ref = refs

    @pl.when(pl.program_id(0) == 0)
    def _():
        w_ref[...] = own_ref[...]

    attend_rows(x_ref, bias_ref, qf_ref, kf_ref, w_ref, qkv_ref, ctx_ref, aug_ref)


def attend_own(length, peers, place, inputs, bias, qf, kf, own):
    heads = own.shape[0] // (3 * HD)
    tokens, width = inputs.shape
    every = peers * heads
    shapes = [(every * 3 * HD, width)] + [(every, n, tokens) for n in (3 * HD, HD, EXTRA)]
    by_row = pl.BlockSpec((EXTRA, length), lambda i, *_: (0, i))
    return pl.pallas_call(
        attend_own_kernel,
        grid_spec=pltpu.PrefetchScalarGridSpec(
            num_scalar_prefetch=1,
            grid=(tokens // length,),
            in_specs=[
                pl.BlockSpec((length, width), lambda i, *_: (i, 0)),
                whole(bias.shape),
                by_row,
                by_row,
                whole(own.shape),
            ],
            out_specs=[
                pl.BlockSpec((heads * 3 * HD, width), lambda i, p: (p[GROUP], 0)),
                *[own_block(heads, n, length) for n in (3 * HD, HD, EXTRA)],
            ],
        ),
        out_shape=[jax.ShapeDtypeStruct(shape, BF16) for shape in shapes],
        compiler_params=params(),
        cost_estimate=cost(heads * tokens * (6 * HD * width + 16 * 64 * length), 12e6),
        name="attend_own",
    )(place, inputs, bias, qf, kf, own)


def attend_peers_kernel(spots, place_ref, x_ref, bias_ref, qf_ref, kf_ref, *refs):
    count = len(spots)
    parts = refs[:count]
    w_ref, qkv_ref, ctx_ref, aug_ref, wide_scr = refs[count + 4 :]

    @pl.when(pl.program_id(1) == 0)
    def _():
        size = w_ref.shape[0] // GROUP
        for ref, (index, offset) in zip(parts, spots):
            put(wide_scr, place_ref[index] * size + offset, ref[0], 8)
        w_ref[...] = wide_scr[...].astype(BF16)

    attend_rows(x_ref, bias_ref.at[0], qf_ref, kf_ref, w_ref, qkv_ref, ctx_ref, aug_ref)


def attend_peers(length, peers, place, inputs, bias, qf, kf, pieces, arrays):
    heads = arrays[1].shape[0] // peers
    tokens, width = inputs.shape
    spots = [(index, offset) for _, index, offset in pieces]
    parts = [array for array, _, _ in pieces]
    by_row = pl.BlockSpec((EXTRA, length), lambda k, i, *_: (0, i))
    return pl.pallas_call(
        lambda *refs: attend_peers_kernel(spots, *refs),
        grid_spec=pltpu.PrefetchScalarGridSpec(
            num_scalar_prefetch=1,
            grid=(peers - 1, tokens // length),
            in_specs=[
                pl.BlockSpec((length, width), lambda k, i, *_: (i, 0)),
                pl.BlockSpec((1,) + bias.shape[1:], lambda k, i, *_: (k, 0, 0)),
                by_row,
                by_row,
                *[
                    pl.BlockSpec((1,) + a.shape[1:], lambda k, i, *_: (k, 0, 0)) for a in parts
                ],
                *[ANY] * 4,
            ],
            out_specs=[
                pl.BlockSpec(
                    (heads * 3 * HD, width),
                    lambda k, i, p: (lax.rem(p[GROUP] + peers - 1 - k, peers), 0),
                ),
                *[peer_block(peers, 1, heads, n, length) for n in (3 * HD, HD, EXTRA)],
            ],
            scratch_shapes=[pltpu.VMEM((heads * 3 * HD, width), F32)],
        ),
        out_shape=[jax.ShapeDtypeStruct(a.shape, a.dtype) for a in arrays],
        input_output_aliases={5 + len(parts) + i: i for i in range(4)},
        compiler_params=params(),
        cost_estimate=cost(
            (peers - 1) * heads * tokens * (6 * HD * width + 16 * 64 * length), 30e6
        ),
        name="attend_peers",
    )(place, inputs, bias, qf, kf, *parts, *arrays)


def attend_back_rows(qkv_ref, ctx_ref, aug_ref, grad_ref, kf_ref, out_ref):
    heads, _, length = ctx_ref.shape
    block = length // 2
    scale = HD ** (-0.5)
    one = jnp.ones((1, block), F32)
    ones_rows = rows_of(EXTRA, 0, (one, one, one), block).astype(BF16)
    items = tiles(heads, block)
    scores, spreads = [], []
    for h, at in items:
        scores.append(
            dot(
                jnp.concatenate([qkv_ref[h, HD : 2 * HD, at], kf_ref[:, at]], axis=0),
                jnp.concatenate([qkv_ref[h, :HD, at], aug_ref[h, :, at]], axis=0),
                0,
                0,
            )
        )
    for h, at in items:
        grad = grad_ref[h, :, at]
        inner = jnp.sum(grad.astype(F32) * ctx_ref[h, :, at].astype(F32), axis=0, keepdims=True)
        grad_extra = rows_of(EXTRA, 0, split3(-inner), block).astype(BF16)
        spreads.append(
            dot(
                jnp.concatenate([qkv_ref[h, 2 * HD :, at], ones_rows], axis=0),
                jnp.concatenate([grad, grad_extra], axis=0),
                0,
                0,
            )
        )
    probs = [jnp.exp(part) for part in scores]
    slopes = [(part * spread).astype(BF16) for part, spread in zip(probs, spreads)]
    probs = [part.astype(BF16) for part in probs]
    for (h, at), part in zip(items, probs):
        out_ref[h, 2 * HD :, at] = dot(grad_ref[h, :, at], part, 1, 1).astype(BF16)
    for (h, at), part in zip(items, slopes):
        out_ref[h, HD : 2 * HD, at] = dot(qkv_ref[h, :HD, at], part, 1, 1).astype(BF16)
    for (h, at), part in zip(items, slopes):
        grad = dot(qkv_ref[h, HD : 2 * HD, at], part, 1, 0)
        out_ref[h, :HD, at] = (grad * scale).astype(BF16)


def attend_back_own_kernel(place_ref, qkv_ref, ctx_ref, aug_ref, grad_ref, kf_ref, *refs):
    x_ref, dwo_ref, small_ref, early_ref, out_ref, mine_ref, send_ref, grad_scr, sum_scr = refs
    heads = ctx_ref.shape[0]
    height = heads * HD
    step = pl.program_id(0)

    @pl.when(step == 0)
    def _():
        grad_scr[...] = jnp.zeros_like(grad_scr)
        sum_scr[...] = jnp.zeros_like(sum_scr)

    attend_back_rows(qkv_ref, ctx_ref, aug_ref, grad_ref, kf_ref, out_ref)
    ones = jnp.ones((8, x_ref.shape[0]), BF16)
    row = lax.broadcasted_iota(jnp.int32, (8, 3 * HD), 0)
    sums = jnp.zeros((8, 3 * HD), F32)
    for h in range(heads):
        grad = dot(out_ref[h], x_ref[...], 1, 0)
        for i in range(3):
            grad_scr[i * height + h * HD : i * height + (h + 1) * HD, :] += grad[
                i * HD : (i + 1) * HD
            ]
        sums = jnp.where(row == 3 + h, dot(ones, out_ref[h], 1, 1), sums)
    sum_scr[:, : 3 * HD] += sums

    @pl.when(step == pl.num_programs(0) - 1)
    def _():
        size, size_two = 3 * height // GROUP, height // GROUP
        top = size + size_two
        for rel in range(4):
            for source, ref in enumerate((mine_ref, send_ref)):
                owner = place_ref[2 * rel + source]
                ref[rel, :size, :] = grad_scr[pl.ds(pl.multiple_of(owner * size, 8), size), :]
                start = pl.multiple_of(owner * size_two, 8)
                ref[rel, size:top, :] = dwo_ref[pl.ds(start, size_two), :]
                ref[rel, top : top + 8, :] = jnp.where(
                    owner == 0, small_ref[...] + sum_scr[...], 0.0
                )
                ref[rel, top + 8 :, :] = jnp.where(owner == 0, early_ref[...], 0.0)


def attend_back_own(length, place, qkv, ctx, aug, grad, kf, inputs, dwo, small, early):
    height, width = dwo.shape
    heads = height // HD
    tokens = inputs.shape[0]
    share = 4 * height // GROUP + 16
    return pl.pallas_call(
        attend_back_own_kernel,
        grid_spec=pltpu.PrefetchScalarGridSpec(
            num_scalar_prefetch=1,
            grid=(tokens // length,),
            in_specs=[
                own_block(heads, 3 * HD, length),
                own_block(heads, HD, length),
                own_block(heads, EXTRA, length),
                own_block(heads, HD, length),
                pl.BlockSpec((EXTRA, length), lambda i, *_: (0, i)),
                pl.BlockSpec((length, width), lambda i, *_: (i, 0)),
                whole(dwo.shape),
                whole(small.shape),
                whole(early.shape),
            ],
            out_specs=[
                own_block(heads, 3 * HD, length),
                whole((4, share, width)),
                whole((4, share, width)),
            ],
            scratch_shapes=[pltpu.VMEM((3 * height, width), F32), pltpu.VMEM((8, width), F32)],
        ),
        out_shape=[jax.ShapeDtypeStruct(qkv.shape, BF16)]
        + [jax.ShapeDtypeStruct((4, share, width), F32)] * 2,
        compiler_params=params(),
        cost_estimate=cost(heads * tokens * (20 * 64 * length + 6 * HD * width), 12e6),
        name="attend_back_own",
    )(place, qkv, ctx, aug, grad, kf, inputs, dwo, small, early)


def attend_back_kernel(place_ref, qkv_ref, ctx_ref, aug_ref, grad_ref, kf_ref, old_ref, out_ref):
    attend_back_rows(qkv_ref, ctx_ref, aug_ref, grad_ref, kf_ref, out_ref)


def attend_back(length, peers, first, count, place, qkv, ctx, aug, grad, kf, out):
    every, _, tokens = qkv.shape
    heads = every // peers
    by_peer = lambda n: peer_block(peers, first, heads, n, length)
    return pl.pallas_call(
        attend_back_kernel,
        grid_spec=pltpu.PrefetchScalarGridSpec(
            num_scalar_prefetch=1,
            grid=(count, tokens // length),
            in_specs=[
                by_peer(3 * HD),
                by_peer(HD),
                by_peer(EXTRA),
                by_peer(HD),
                pl.BlockSpec((EXTRA, length), lambda k, i, *_: (0, i)),
                ANY,
            ],
            out_specs=by_peer(3 * HD),
        ),
        out_shape=jax.ShapeDtypeStruct(out.shape, BF16),
        input_output_aliases={6: 0},
        compiler_params=params(),
        cost_estimate=cost(count * heads * tokens * 20 * 64 * length, 12e6),
        name="attend_back",
    )(place, qkv, ctx, aug, grad, kf, out)


def norm_forward(hidden):
    center = hidden - jnp.mean(hidden, axis=-1, keepdims=True)
    inverse = lax.rsqrt(jnp.mean(center * center, axis=-1, keepdims=True) + EPS)
    return center * inverse, inverse


def norm_backward(grad, gain, norm, inverse):
    scaled = grad * gain
    first = jnp.mean(scaled, axis=-1, keepdims=True)
    second = jnp.mean(scaled * norm, axis=-1, keepdims=True)
    return (scaled - first - norm * second) * inverse


def column_sum(values):
    return jnp.sum(values, axis=0, keepdims=True)


def flat(values):
    return values.reshape(-1, values.shape[-1])


def fill(place_ref, own_ref, parts, spots, out_ref):
    shards, height, _ = out_ref.shape
    out_ref[place_ref[GROUP]] = own_ref[...]
    for k in range(1, shards):
        shard = peer_shard(place_ref, shards, k)
        for ref, (index, offset) in zip(parts, spots):
            start = place_ref[index] * (height // GROUP) + offset
            put(out_ref.at[shard], start, ref[k - 1], 16)


def expand_kernel(spots, place_ref, x_ref, ctx_ref, bias_ref, vec_ref, own_ref, own_wo_ref, *refs):
    parts, refs = refs[: len(spots)], refs[len(spots) :]
    sum_ref, act_ref, slope_ref, full_ref, wo_ref, we_ref, wide_scr, low_scr, sem = refs
    shards, width, _ = we_ref.shape
    size, size_two = width // GROUP, wo_ref.shape[0] // (shards * GROUP)
    kept = pltpu.make_async_copy(we_ref, full_ref, sem)

    @pl.when(pl.program_id(0) == 0)
    def _():
        me = place_ref[GROUP]
        we_ref[me] = own_ref[...]
        put(wide_scr, me * size_two * GROUP, own_wo_ref[...], 8)
        for k in range(1, shards):
            shard = peer_shard(place_ref, shards, k)
            for ref, (index, offset) in zip(parts, spots):
                part = ref[k - 1]
                count = min(part.shape[0], size - offset)
                put(we_ref.at[shard], place_ref[index] * size + offset, part[:count], 16)
                if count < part.shape[0]:
                    start = (shard * GROUP + place_ref[index]) * size_two
                    put(wide_scr, start, part[count:], 8)
        wo_ref[...] = wide_scr[...].astype(BF16)
        kept.start()

    @pl.when(pl.program_id(0) == pl.num_programs(0) - 1)
    def _():
        kept.wait()

    b_output, gain_one, shift_one = vec_ref[0:1], vec_ref[1:2], vec_ref[2:3]
    half = x_ref.shape[0] // 2
    halves = [slice(0, half), slice(half, 2 * half)]
    attended = [dot(flat(ctx_ref[:, :, at]), wo_ref[...], 0, 0) for at in halves]
    for at, part in zip(halves, attended):
        residual = x_ref[at, :].astype(F32) + (part + b_output)
        sum_ref[at, :] = residual
        norm_one, _ = norm_forward(residual)
        low_scr[at, :] = (norm_one * gain_one + shift_one).astype(BF16)

    def shard_step(s, carry):
        bias = bias_ref[peer_shard(place_ref, shards, s), 1:2]
        products = [dot(low_scr[at, :], we_ref[s], 1, 0) for at in halves]
        for at, product in zip(halves, products):
            hidden = product + bias
            square = hidden * hidden
            bent = jnp.tanh(hidden * (0.7978845608028654 + 0.035677408136300125 * square))
            gate = 0.5 + 0.5 * bent
            active = hidden * gate
            act_ref[s, at, :] = active.astype(BF16)
            slope = gate + (active * (1.0 - gate)) * (
                1.5957691216057308 + 0.21406444881780075 * square
            )
            slope_ref[s, at, :] = slope.astype(BF16)
        return carry

    lax.fori_loop(0, shards, shard_step, 0, unroll=2)


def expand(place, inputs, ctx, biases, vectors, own, own_wo, pieces, shards):
    tokens, width = inputs.shape
    hidden = own.shape[1]
    every = ctx.shape[0]
    block = 512
    spots = [(index, offset) for _, index, offset in pieces]
    parts = [array for array, _, _ in pieces]
    full = (shards, width, hidden)
    by_token = lambda: pl.BlockSpec((block, width), lambda i, *_: (i, 0))
    by_shard = lambda: pl.BlockSpec((shards, block, hidden), lambda i, *_: (0, i, 0))
    return pl.pallas_call(
        lambda *refs: expand_kernel(spots, *refs),
        grid_spec=pltpu.PrefetchScalarGridSpec(
            num_scalar_prefetch=1,
            grid=(tokens // block,),
            in_specs=[
                by_token(),
                pl.BlockSpec((every, HD, block), lambda i, *_: (0, 0, i)),
                whole(biases.shape),
                whole(vectors.shape),
                whole(own.shape),
                whole(own_wo.shape),
                *[whole(a.shape) for a in parts],
            ],
            out_specs=[by_token(), by_shard(), by_shard(), ANY, whole((every * HD, width))],
            scratch_shapes=[
                pltpu.VMEM(full, BF16),
                pltpu.VMEM((every * HD, width), F32),
                pltpu.VMEM((block, width), BF16),
                pltpu.SemaphoreType.DMA,
            ],
        ),
        out_shape=[
            jax.ShapeDtypeStruct((tokens, width), F32),
            jax.ShapeDtypeStruct((shards, tokens, hidden), BF16),
            jax.ShapeDtypeStruct((shards, tokens, hidden), BF16),
            jax.ShapeDtypeStruct(full, BF16),
            jax.ShapeDtypeStruct((every * HD, width), BF16),
        ],
        compiler_params=params(),
        cost_estimate=cost(2 * tokens * width * (shards * hidden + every * HD), 40e6),
        name="expand",
    )(place, inputs, ctx, biases, vectors, own, own_wo, *parts)


def reduce_kernel(spots, place_ref, sum_ref, cot_ref, act_ref, slope_ref, vec_ref, *refs):
    own_ref, refs = refs[0], refs[1:]
    piece_refs, refs = refs[: len(spots)], refs[len(spots) :]
    out_ref, g2_ref, full_ref, mine_ref, send_ref, small_scr = refs[:6]
    dwe_scr, dwr_scr, wr_ref, sems = refs[6:]
    kept = pltpu.make_async_copy(wr_ref, full_ref, sems.at[0])
    step = pl.program_id(0)
    shards = act_ref.shape[0]
    me = place_ref[GROUP]

    @pl.when(step == 0)
    def _():
        fill(place_ref, own_ref, piece_refs, spots, wr_ref)
        kept.start()
        for scr in (dwe_scr, dwr_scr, small_scr):
            scr[...] = jnp.zeros_like(scr)

    gain_one, shift_one = vec_ref[1:2], vec_ref[2:3]
    b_reduce, gain_two, shift_two = vec_ref[3:4], vec_ref[4:5], vec_ref[5:6]
    half = sum_ref.shape[0] // 2
    halves = [slice(0, half), slice(half, 2 * half)]
    quarter = half // 4
    width = sum_ref.shape[1]
    small = [jnp.zeros((1, width), F32)] * 4

    def norm_part(start, mixed):
        at = slice(start, start + quarter)
        norm_one, _ = norm_forward(sum_ref[at, :])
        normed = norm_one * gain_one + shift_one
        norm_two, inverse_two = norm_forward(normed + (mixed + b_reduce))
        out_ref[at, :] = (norm_two * gain_two + shift_two).astype(BF16)
        cot = cot_ref[at, :].astype(F32)
        grad_two = norm_backward(cot, gain_two, norm_two, inverse_two)
        g2_ref[at, :] = grad_two
        small[0] = small[0] + column_sum(grad_two)
        small[1] = small[1] + column_sum(cot * norm_two)
        small[2] = small[2] + column_sum(cot)
        return grad_two.astype(BF16), normed.astype(BF16)

    first, second = halves
    mixed = dot(act_ref[0, first, :], wr_ref[0], 1, 0)
    for s in range(1, shards):
        mixed = mixed + dot(act_ref[s, first, :], wr_ref[s], 1, 0)
    later = None
    parts = []
    for s in range(shards):
        product = dot(act_ref[s, second, :], wr_ref[s], 1, 0)
        later = product if later is None else later + product
        parts.append(norm_part(s * quarter, mixed[s * quarter : (s + 1) * quarter]))
    low_a = jnp.concatenate([part[0] for part in parts], axis=0)
    normed_a = jnp.concatenate([part[1] for part in parts], axis=0)
    active_a = dot(low_a, own_ref[...], 1, 1)
    parts = [norm_part(half + s * quarter, later[s * quarter : (s + 1) * quarter]) for s in (0, 1)]
    dwr_scr[...] += dot(act_ref[me, first, :], low_a, 0, 0)
    parts += [norm_part(half + s * quarter, later[s * quarter : (s + 1) * quarter]) for s in (2, 3)]
    own_a = (active_a * slope_ref[0, first, :].astype(F32)).astype(BF16)
    low_b = jnp.concatenate([part[0] for part in parts], axis=0)
    normed_b = jnp.concatenate([part[1] for part in parts], axis=0)
    active_b = dot(low_b, own_ref[...], 1, 1)
    small[3] = small[3] + column_sum(own_a.astype(F32))
    dwe_scr[...] += dot(normed_a, own_a, 0, 0)
    own_b = (active_b * slope_ref[0, second, :].astype(F32)).astype(BF16)
    dwr_scr[...] += dot(act_ref[me, second, :], low_b, 0, 0)
    small[3] = small[3] + column_sum(own_b.astype(F32))
    dwe_scr[...] += dot(normed_b, own_b, 0, 0)
    for n, part in enumerate(small):
        small_scr[n : n + 1] += part

    @pl.when(step == pl.num_programs(0) - 1)
    def _():
        copies = [kept]
        for rel in range(4):
            for source, ref in ((1, send_ref), (0, mine_ref)):
                owner = place_ref[2 * rel + source]
                top = 0
                for scr in (dwe_scr, dwr_scr):
                    size = scr.shape[0] // GROUP
                    start = pl.multiple_of(owner * size, 8)
                    copy = pltpu.make_async_copy(
                        scr.at[pl.ds(start, size), :],
                        ref.at[rel, top : top + size, :],
                        sems.at[len(copies)],
                    )
                    copy.start()
                    copies.append(copy)
                    top += size
        for copy in copies:
            copy.wait()


def reduce(place, residual, cot, act, slope, vectors, own, pieces):
    tokens, width = residual.shape
    shards, _, hidden = act.shape
    block = 512
    share = (width + hidden) // GROUP
    spots = [(index, offset) for _, index, offset in pieces]
    arrays = [array for array, _, _ in pieces]
    by_token = lambda: pl.BlockSpec((block, width), lambda i, *_: (i, 0))
    return pl.pallas_call(
        lambda *refs: reduce_kernel(spots, *refs),
        grid_spec=pltpu.PrefetchScalarGridSpec(
            num_scalar_prefetch=1,
            grid=(tokens // block,),
            in_specs=[
                by_token(),
                by_token(),
                pl.BlockSpec((shards, block, hidden), lambda i, *_: (0, i, 0)),
                pl.BlockSpec((1, block, hidden), lambda i, p: (p[GROUP], i, 0)),
                whole(vectors.shape),
                whole(own.shape),
                *[whole(a.shape) for a in arrays],
            ],
            out_specs=[
                by_token(),
                by_token(),
                ANY,
                ANY,
                ANY,
                whole((8, width)),
            ],
            scratch_shapes=[
                pltpu.VMEM((width, hidden), F32),
                pltpu.VMEM((hidden, width), F32),
                pltpu.VMEM((shards, hidden, width), BF16),
                pltpu.SemaphoreType.DMA((17,)),
            ],
        ),
        out_shape=[
            jax.ShapeDtypeStruct((tokens, width), BF16),
            jax.ShapeDtypeStruct((tokens, width), F32),
            jax.ShapeDtypeStruct((shards, hidden, width), BF16),
            jax.ShapeDtypeStruct((4, share, width), F32),
            jax.ShapeDtypeStruct((4, share, width), F32),
            jax.ShapeDtypeStruct((8, width), F32),
        ],
        compiler_params=params(),
        cost_estimate=cost(tokens * width * hidden * (2 * shards + 6), 40e6),
        name="reduce",
    )(place, residual, cot, act, slope, vectors, own, *arrays)


def return_kernel(place_ref, sum_ref, g2_ref, slope_ref, ctx_ref, we_ref, wr_ref, w_ref, *refs):
    vec_ref, g1_ref, dctx_ref, dwo_ref, small_ref = refs
    shards = we_ref.shape[0]

    @pl.when(pl.program_id(0) == 0)
    def _():
        dwo_ref[...] = jnp.zeros_like(dwo_ref)
        small_ref[...] = jnp.zeros_like(small_ref)

    half = sum_ref.shape[0] // 2
    halves = [slice(0, half), slice(half, 2 * half)]
    gain_one = vec_ref[1:2]
    low = [g2_ref[at, :].astype(BF16) for at in halves]
    items = [(s, i) for s in range(shards) for i in range(2)]
    total = [g2_ref[at, :] for at in halves]
    ahead = dot(low[0], wr_ref[0], 1, 1)
    for n, (s, i) in enumerate(items):
        grad_active = ahead
        if n + 1 < len(items):
            s_next, i_next = items[n + 1]
            ahead = dot(low[i_next], wr_ref[s_next], 1, 1)
        grad_hidden = (grad_active * slope_ref[s, halves[i], :].astype(F32)).astype(BF16)
        total[i] = total[i] + dot(grad_hidden, we_ref[s], 1, 1)
    small = [jnp.zeros((1, sum_ref.shape[1]), F32)] * 3
    one = []
    for at, grad_normed in zip(halves, total):
        norm_one, inverse_one = norm_forward(sum_ref[at, :])
        grad_one = norm_backward(grad_normed, gain_one, norm_one, inverse_one)
        g1_ref[at, :] = grad_one
        one.append(grad_one.astype(BF16))
        small[0] = small[0] + column_sum(grad_one)
        small[1] = small[1] + column_sum(grad_normed * norm_one)
        small[2] = small[2] + column_sum(grad_normed)
    one = jnp.concatenate(one, axis=0)
    dctx = dot(w_ref[...], one, 1, 1)
    dwo_ref[...] += dot(flat(ctx_ref[...]), one, 1, 0)
    dctx_ref[...] = dctx.astype(BF16).reshape(dctx_ref.shape)
    for n, part in enumerate(small):
        small_ref[n : n + 1] += part


def back_to_context(place, residual, grad_two, slope, ctx, w_expand, w_reduce, weights, vectors):
    tokens, width = residual.shape
    shards, _, hidden = w_expand.shape
    every = ctx.shape[0]
    heads = every // shards
    block = 512
    by_token = lambda: pl.BlockSpec((block, width), lambda i, *_: (i, 0))
    return pl.pallas_call(
        return_kernel,
        grid_spec=pltpu.PrefetchScalarGridSpec(
            num_scalar_prefetch=1,
            grid=(tokens // block,),
            in_specs=[
                by_token(),
                by_token(),
                pl.BlockSpec((shards, block, hidden), lambda i, *_: (0, i, 0)),
                own_block(heads, HD, block),
                whole(w_expand.shape),
                whole(w_reduce.shape),
                whole(weights.shape),
                whole(vectors.shape),
            ],
            out_specs=[
                by_token(),
                pl.BlockSpec((every, HD, block), lambda i, *_: (0, 0, i)),
                whole((heads * HD, width)),
                whole((8, width)),
            ],
        ),
        out_shape=[
            jax.ShapeDtypeStruct((tokens, width), F32),
            jax.ShapeDtypeStruct(ctx.shape, BF16),
            jax.ShapeDtypeStruct((heads * HD, width), F32),
            jax.ShapeDtypeStruct((8, width), F32),
        ],
        compiler_params=params(),
        cost_estimate=cost(tokens * width * (4 * shards * hidden + 2 * every * HD), 40e6),
        name="back_to_context",
    )(place, residual, grad_two, slope, ctx, w_expand, w_reduce, weights, vectors)


def spread_kernel(spots, place_ref, *refs):
    parts, outs = refs[: len(spots)], refs[len(spots) :]
    for ref, (index, offset) in zip(parts, spots):
        start = 0
        for i, out_ref in enumerate(outs):
            size = out_ref.shape[0] // GROUP
            if offset <= i * size < offset + ref.shape[1]:
                put(out_ref, place_ref[index] * size, ref[0, start : start + size, :], 8)
                start += size


def spread(place, pieces, sizes):
    spots = [(index, offset) for _, index, offset in pieces]
    parts = [array for array, _, _ in pieces]
    width = parts[0].shape[2]
    shapes = [(GROUP * size, width) for size in sizes]
    return pl.pallas_call(
        lambda *refs: spread_kernel(spots, *refs),
        grid_spec=pltpu.PrefetchScalarGridSpec(
            num_scalar_prefetch=1,
            grid=(1,),
            in_specs=[whole(a.shape) for a in parts],
            out_specs=[whole(s) for s in shapes],
        ),
        out_shape=[jax.ShapeDtypeStruct(s, F32) for s in shapes],
        compiler_params=params(16 << 20),
        cost_estimate=cost(0, 10e6),
        name="spread",
    )(place, *parts)


def spread_late_kernel(heads, place_ref, *refs):
    parts = refs[:GROUP]
    dq_ref, dk_ref, dv_ref, dwo_ref, small_ref, grad_scr = refs[GROUP:]
    height = heads * HD
    size, size_two = 3 * height // GROUP, height // GROUP
    top = size + size_two
    for i, ref in enumerate(parts):
        owner = place_ref[i]
        put(grad_scr, owner * size, ref[:size, :], 8)
        put(dwo_ref, owner * size_two, ref[size:top, :], 8)

        @pl.when(owner == 0)
        def _():
            small_ref[...] = ref[top:, :]

    for i, out_ref in enumerate((dq_ref, dk_ref, dv_ref)):
        out_ref[...] = grad_scr[i * height : (i + 1) * height, :]


def spread_late(place, parts, heads):
    share, width = parts[0].shape
    height = heads * HD
    shapes = [(height, width)] * 4 + [(16, width)]
    return pl.pallas_call(
        lambda *refs: spread_late_kernel(heads, *refs),
        grid_spec=pltpu.PrefetchScalarGridSpec(
            num_scalar_prefetch=1,
            grid=(1,),
            in_specs=[whole(a.shape) for a in parts],
            out_specs=[whole(s) for s in shapes],
            scratch_shapes=[pltpu.VMEM((3 * height, width), F32)],
        ),
        out_shape=[jax.ShapeDtypeStruct(s, F32) for s in shapes],
        compiler_params=params(10 << 20),
        cost_estimate=cost(0, 8 * parts[0].size * 8),
        name="spread_late",
    )(place, *parts)


def input_grads_kernel(place_ref, g1_ref, grad_ref, w_ref, out_ref):
    amount = place_ref[GROUP + 1 + pl.program_id(0)]
    matrix = shift_matrix(amount, g1_ref.shape[0], False)
    total = g1_ref[...] + dot(flat(grad_ref[...]), w_ref[...], 0, 0)
    out_ref[...] = dot(matrix, total.astype(BF16), 1, 0).astype(BF16)


def input_grads(place, length, grad_one, grads, weights):
    tokens, width = grad_one.shape
    every = grads.shape[0]
    by_row = lambda: pl.BlockSpec((length, width), lambda i, *_: (i, 0))
    return pl.pallas_call(
        input_grads_kernel,
        grid_spec=pltpu.PrefetchScalarGridSpec(
            num_scalar_prefetch=1,
            grid=(tokens // length,),
            in_specs=[
                by_row(),
                pl.BlockSpec((every, 3 * HD, length), lambda i, *_: (0, 0, i)),
                whole(weights.shape),
            ],
            out_specs=by_row(),
        ),
        out_shape=jax.ShapeDtypeStruct((tokens, width), BF16),
        compiler_params=params(),
        cost_estimate=cost(2 * tokens * width * (every * 3 * HD + length), 20e6),
        name="input_grads",
    )(place, grad_one, grads, weights)


def after(values, *others):
    return lax.optimization_barrier((values, others))[0]


def solution(mesh):
    peers = mesh.shape["mp"]
    lanes = mesh.shape["dp"]
    rotations = [[(i, (i + k) % peers) for i in range(peers)] for k in range(1, peers)]

    def flip(values, bits):
        return lax.ppermute(values, "dp", [(i, i ^ bits) for i in range(lanes)])

    def from_peers(piece):
        return jnp.stack([lax.ppermute(piece, "mp", perm) for perm in rotations])

    def swapped(piece, *ready):
        copies = jnp.broadcast_to(piece[None], (peers,) + piece.shape)
        got = lax.all_to_all(after(copies, *ready), "mp", 0, 0, tiled=True)
        me = lax.axis_index("mp")
        return jnp.concatenate(
            [
                lax.dynamic_slice_in_dim(got, lax.rem(me + peers - k, peers), 1, 0)
                for k in range(1, peers)
            ]
        )

    def both(near):
        return flip(near, 2), flip(near, 4)

    def corner(by_x, by_y, cut):
        return flip(by_y[:, :cut], 2), flip(by_x[:, cut:], 4)

    def listed(near, by_x, by_y, first, second, cut):
        places = ((near, 0, 0), (by_x, 1, 0), (by_y, 2, 0), (first, 3, 0), (second, 3, cut))
        return with_core(places)

    def with_core(places):
        out = []
        for array, rel, offset in places:
            out.append((array, 2 * rel, offset))
            out.append((flip(array, 1), 2 * rel + 1, offset))
        return out

    def sum_groups(total):
        step = GROUP
        while step < lanes:
            total = total + flip(total, step)
            step *= 2
        return total

    def partial_sums(mine, got, *ready):
        got = after(got, *ready)
        return [mine[rel] + got[rel] for rel in range(4)]

    def exchange(parts):
        return [flip(parts[rel], 2 * rel) for rel in (1, 2, 3)]

    def total_of(first, rest, *ready):
        rest = after(rest, *ready)
        return sum_groups(first + rest[0] + rest[1] + rest[2])

    def finish(arrays, *ready):
        out = []
        for array in after(arrays, *ready):
            out += [array, flip(array, 1)]
        return out

    def local(
        tokens,
        doc_lengths,
        w_query,
        b_query,
        w_key,
        w_value,
        b_value,
        w_output,
        b_output,
        gain_attn,
        shift_attn,
        w_expand,
        b_expand,
        w_reduce,
        b_reduce,
        gain_ffn,
        shift_ffn,
        cotangent,
    ):
        row_count, length, width = tokens.shape
        heads = w_query.shape[1] // HD
        hidden = w_expand.shape[1]
        count = row_count * length
        inside = lax.axis_index("dp") % GROUP
        me = lax.axis_index("mp")
        ends = jnp.cumsum(doc_lengths, axis=-1)
        longest = jnp.max(doc_lengths, axis=-1, keepdims=True)
        offset = jnp.max(jnp.where(doc_lengths == longest, ends - doc_lengths, 0), axis=-1)
        place = jnp.stack([inside ^ i for i in range(GROUP)] + [me])
        place = jnp.concatenate([place, offset]).astype(jnp.int32)

        by_head = lambda w: w.T.reshape(heads, HD, width)
        own_heads = jnp.concatenate([by_head(w_query), by_head(w_key), by_head(w_value)], axis=1)
        own_heads = own_heads.reshape(3 * heads * HD, width)
        blank = jnp.zeros((width - 2 * heads * HD,), BF16)
        own_bias = jnp.stack(
            [jnp.concatenate([b_query, b_value, blank]), b_expand]
            + [jnp.zeros((width,), BF16)] * 6
        ).astype(F32)

        def piece_of(array, bits=0):
            size = array.shape[0] // GROUP
            return lax.dynamic_slice_in_dim(array, (inside ^ bits) * size, size, 0).astype(F32)

        piece = piece_of(own_heads)
        near = from_peers(jnp.concatenate([piece, own_bias]))

        position = (jnp.arange(length, dtype=jnp.int32)[None] + offset[:, None]) % length
        segment = jnp.sum((position[:, :, None] >= ends[:, None, :]).astype(jnp.int32), axis=-1)
        segment = segment.reshape(1, count)
        docs = doc_lengths.shape[1]
        label = jnp.arange(EXTRA, dtype=jnp.int32)[:, None]
        is_doc = label < docs
        qf = jnp.where(is_doc & (segment == label), 1.0, 0.0).astype(BF16)
        kf = jnp.where(
            is_doc,
            jnp.where(segment == label, 0.0, MASK),
            jnp.where(label < docs + 3, 1.0, 0.0),
        ).astype(BF16)
        inputs, cot = shift(
            place, length, tokens.reshape(count, width), cotangent.reshape(count, width)
        )
        own = attend_own(
            length, peers, place, inputs, own_bias, qf, kf, own_heads
        )

        near = after(near, own)
        biases = near[:, -own_bias.shape[0] :]
        all_biases = jnp.concatenate([own_bias[None], biases])
        near = near[:, : -own_bias.shape[0]]
        cut = piece.shape[0] // 16 * 8
        share = jnp.concatenate([piece_of(w_expand), piece_of(w_output)])
        near_expand = swapped(share, near)
        sides = both(near)
        corners = corner(*sides, cut)
        pieces = listed(near, *sides, *corners, cut)
        sides_expand = both(after(near_expand, corners))
        near_reduce = swapped(piece_of(w_reduce), near_expand, [array for array, _, _ in pieces])
        weights, qkv, ctx, aug = attend_peers(
            length, peers, place, inputs, after(biases, near_expand), qf, kf, pieces, own
        )

        sides_expand = after(sides_expand, ctx)
        cut = share.shape[0] // 2 // 16 * 16 + 16
        corners = corner(*sides_expand, cut)
        vectors = jnp.stack(
            [b_output, gain_attn, shift_attn, b_reduce, gain_ffn, shift_ffn]
            + [jnp.zeros((width,), BF16)] * 2
        ).astype(F32)
        pieces = listed(near_expand, *sides_expand, *corners, cut)
        near_reduce = after(near_reduce, sides_expand)
        diagonal = swapped(piece_of(w_reduce, 6), near_reduce)
        sides_reduce = both(near_reduce)
        residual, act, slope, all_expand, all_output = expand(
            place,
            inputs,
            ctx,
            after(all_biases, near_reduce),
            vectors,
            w_expand,
            w_output,
            pieces,
            peers,
        )
        far_reduce = after((*sides_reduce, diagonal), act)
        pieces = with_core([(array, rel, 0) for rel, array in enumerate([near_reduce, *far_reduce])])
        shifted, grad_two, all_reduce, mine, send, small_one = reduce(
            place, residual, cot, act, slope, vectors, w_reduce, pieces
        )
        got = flip(send, 1)
        output = unshift(place, length, shifted)
        chip = partial_sums(mine, got, output)
        early = exchange(chip)
        grad_one, dctx, dwo, small = back_to_context(
            place,
            residual,
            grad_two,
            slope,
            ctx,
            all_expand,
            all_reduce,
            all_output,
            after(vectors, chip),
        )
        early = total_of(chip[0], early, grad_one)[None]
        sides = both(early)
        dqkv, mine, send = attend_back_own(
            length, place, qkv, ctx, aug, dctx, after(kf, early), inputs, dwo, small, small_one
        )
        got = flip(after(send, sides), 1)
        dqkv = attend_back(
            length, peers, 1, 1, place, qkv, ctx, aug, dctx, after(kf, sides), dqkv
        )
        across = flip(after(early, sides), 6)
        beside = [flip(array, 1) for array in (early, *sides)]
        parts = partial_sums(mine, got, dqkv)
        rest = exchange(parts)
        across, beside, kept = after((across, beside, kf), parts)
        dqkv = attend_back(length, peers, 2, peers - 2, place, qkv, ctx, aug, dctx, kept, dqkv)
        total = total_of(parts[0], rest, dqkv)
        second = [total] + exchange([None] + [total] * 3)
        beside.append(flip(across, 1))
        pieces = []
        for rel, (near, far) in enumerate(zip((early, *sides, across), beside)):
            pieces += [(near, 2 * rel, 0), (far, 2 * rel + 1, 0)]
        grad_one = after(grad_one, total, beside)
        grad_tokens = input_grads(place, length, grad_one, dqkv, weights)
        second = finish(second, grad_tokens)
        dwe, dwr = spread(place, pieces, [width // GROUP, hidden // GROUP])
        dq, dk, dv, dwo, small_two = spread_late(place, second, heads)
        sums = lambda i: small_two[3 : 3 + heads, i * HD : (i + 1) * HD].reshape(heads * HD)
        shape = (row_count, length, width)
        return (
            output.reshape(shape),
            grad_tokens.reshape(shape),
            dq.T,
            sums(0),
            dk.T,
            dv.T,
            sums(2),
            dwo,
            small_two[0],
            small_two[1],
            small_two[2],
            dwe,
            small_two[11],
            dwr,
            small_two[8],
            small_two[9],
            small_two[10],
        )

    rows, split = P("dp", None, None), P(None, "mp")
    return jax.shard_map(
        local,
        mesh=mesh,
        in_specs=(
            rows,
            P("dp", None),
            split,
            P("mp"),
            split,
            split,
            P("mp"),
            P("mp", None),
            P(),
            P(),
            P(),
            split,
            P("mp"),
            P("mp", None),
            P(),
            P(),
            P(),
            rows,
        ),
        out_specs=(
            rows,
            rows,
            split,
            P("mp"),
            split,
            split,
            P("mp"),
            P("mp", None),
            P(),
            P(),
            P(),
            split,
            P("mp"),
            P("mp", None),
            P(),
            P(),
            P(),
        ),
        check_vma=False,
    )
```

```python
import jax
import jax.numpy as jnp
from jax import lax
from jax.experimental import pallas as pl
from jax.experimental.pallas import tpu as pltpu
from jax.sharding import PartitionSpec as P

HD = 64
GROUP = 8
EXTRA = 16
MASK = -float(2**30)
EPS = 1e-12
F32 = jnp.float32
BF16 = jnp.bfloat16
LIMIT = 60 << 20


def dot(left, right, left_dim, right_dim):
    return lax.dot_general(
        left, right, (((left_dim,), (right_dim,)), ((), ())), preferred_element_type=F32
    )


def params(limit=LIMIT):
    return pltpu.CompilerParams(vmem_limit_bytes=limit)


def cost(flops, moved):
    return pl.CostEstimate(flops=int(flops), bytes_accessed=int(moved), transcendentals=0)


def whole(shape):
    zeros = (0,) * len(shape)
    return pl.BlockSpec(shape, lambda *_: zeros, pipeline_mode=pl.Buffered(1))


def split3(row):
    high = row.astype(BF16).astype(F32)
    rest = row - high
    mid = rest.astype(BF16).astype(F32)
    return high, mid, rest - mid


def rows_of(height, first, parts, width):
    place = lax.broadcasted_iota(jnp.int32, (height, width), 0)
    out = jnp.zeros((height, width), F32)
    for i, part in enumerate(parts):
        out = jnp.where(place == first + i, part, out)
    return out


def put(out_ref, start, values, step):
    rows = pl.ds(pl.multiple_of(start, step), values.shape[0])
    out_ref[rows, :] = values.astype(out_ref.dtype)


def peer_shard(place_ref, shards, k):
    return lax.rem(place_ref[GROUP] + shards - k, shards)


def own_block(*shape):
    return pl.BlockSpec(shape, lambda i, p: (p[GROUP],) + (0,) * (len(shape) - 2) + (i,))


def peer_block(peers, first, *shape):
    middle = (0,) * (len(shape) - 2)
    return pl.BlockSpec(
        shape, lambda k, i, p: (lax.rem(p[GROUP] + peers - first - k, peers),) + middle + (i,)
    )


ANY = pl.BlockSpec(memory_space=pl.ANY)


def shift_matrix(amount, length, forward):
    row = lax.broadcasted_iota(jnp.int32, (length, length), 0)
    column = lax.broadcasted_iota(jnp.int32, (length, length), 1)
    apart = column - row if forward else row - column
    return jnp.where((apart == amount) | (apart == amount - length), 1.0, 0.0).astype(BF16)


def shift_kernel(place_ref, first_ref, second_ref, first_out, second_out):
    length = first_ref.shape[0]
    amount = place_ref[GROUP + 1 + pl.program_id(0)]
    matrix = shift_matrix(amount, length, True)
    first_out[...] = dot(matrix, first_ref[...], 1, 0).astype(BF16)
    second_out[...] = dot(matrix, second_ref[...], 1, 0).astype(BF16)


def shift(place, length, first, second):
    tokens, width = first.shape
    by_row = lambda: pl.BlockSpec((length, width), lambda i, *_: (i, 0))
    return pl.pallas_call(
        shift_kernel,
        grid_spec=pltpu.PrefetchScalarGridSpec(
            num_scalar_prefetch=1,
            grid=(tokens // length,),
            in_specs=[by_row(), by_row()],
            out_specs=[by_row(), by_row()],
        ),
        out_shape=[jax.ShapeDtypeStruct((tokens, width), BF16)] * 2,
        compiler_params=params(),
        cost_estimate=cost(4 * tokens * length * width, 12e6),
        name="shift",
    )(place, first, second)


def unshift_kernel(place_ref, in_ref, out_ref):
    length = in_ref.shape[0]
    matrix = shift_matrix(place_ref[GROUP + 1 + pl.program_id(0)], length, False)
    out_ref[...] = dot(matrix, in_ref[...], 1, 0).astype(BF16)


def unshift(place, length, shifted):
    tokens, width = shifted.shape
    by_row = lambda: pl.BlockSpec((length, width), lambda i, *_: (i, 0))
    return pl.pallas_call(
        unshift_kernel,
        grid_spec=pltpu.PrefetchScalarGridSpec(
            num_scalar_prefetch=1,
            grid=(tokens // length,),
            in_specs=[by_row()],
            out_specs=by_row(),
        ),
        out_shape=jax.ShapeDtypeStruct((tokens, width), BF16),
        compiler_params=params(),
        cost_estimate=cost(2 * tokens * length * width, 6e6),
        name="unshift",
    )(place, shifted)


def tiles(heads, block):
    return [(h, slice(i * block, (i + 1) * block)) for h in range(heads) for i in range(2)]


def attend_rows(x_ref, bias_ref, qf_ref, kf_ref, w_scr, qkv_ref, ctx_ref, aug_ref):
    heads = ctx_ref.shape[0]
    length = x_ref.shape[0]
    block = length // 2
    span = 3 * HD
    proj = dot(w_scr[...], x_ref[...], 1, 1)
    scale = HD ** (-0.5)
    column = bias_ref[...].T[:, 0:1]
    for h in range(heads):
        part = proj[h * span : (h + 1) * span]
        queries = part[:HD] + column[h * HD : (h + 1) * HD]
        values = part[2 * HD :] + column[(heads + h) * HD : (heads + h + 1) * HD]
        qkv_ref[h, :HD, :] = (queries * scale).astype(BF16)
        qkv_ref[h, HD : 2 * HD, :] = part[HD : 2 * HD].astype(BF16)
        qkv_ref[h, 2 * HD :, :] = values.astype(BF16)
    ones_rows = rows_of(EXTRA, 0, (jnp.ones((1, block), F32),), block).astype(BF16)
    items = tiles(heads, block)
    scores = []
    for h, at in items:
        queries = jnp.concatenate([qkv_ref[h, :HD, at], qf_ref[:, at]], axis=0)
        keys = jnp.concatenate([qkv_ref[h, HD : 2 * HD, at], kf_ref[:, at]], axis=0)
        scores.append(dot(keys, queries, 0, 0))
    highest = [jnp.max(part, axis=0, keepdims=True) for part in scores]
    weight = [jnp.exp(part - top).astype(BF16) for part, top in zip(scores, highest)]
    context = []
    for (h, at), part in zip(items, weight):
        values = jnp.concatenate([qkv_ref[h, 2 * HD :, at], ones_rows], axis=0)
        context.append(dot(values, part, 1, 0))
    for (h, at), part, top in zip(items, context, highest):
        total = part[HD : HD + 1]
        ctx_ref[h, :, at] = (part[:HD] * (1.0 / total)).astype(BF16)
        log_total = top + jnp.log(total)
        extra = rows_of(EXTRA, 4, split3(-log_total), block)
        aug_ref[h, :, at] = (extra + qf_ref[:, at].astype(F32)).astype(BF16)


def attend_own_kernel(place_ref, x_ref, bias_ref, qf_ref, kf_ref, own_ref, *refs):
    w_ref, qkv_ref, ctx_ref, aug_ref = refs

    @pl.when(pl.program_id(0) == 0)
    def _():
        w_ref[...] = own_ref[...]

    attend_rows(x_ref, bias_ref, qf_ref, kf_ref, w_ref, qkv_ref, ctx_ref, aug_ref)


def attend_own(length, peers, place, inputs, bias, qf, kf, own):
    heads = own.shape[0] // (3 * HD)
    tokens, width = inputs.shape
    every = peers * heads
    shapes = [(every * 3 * HD, width)] + [(every, n, tokens) for n in (3 * HD, HD, EXTRA)]
    by_row = pl.BlockSpec((EXTRA, length), lambda i, *_: (0, i))
    return pl.pallas_call(
        attend_own_kernel,
        grid_spec=pltpu.PrefetchScalarGridSpec(
            num_scalar_prefetch=1,
            grid=(tokens // length,),
            in_specs=[
                pl.BlockSpec((length, width), lambda i, *_: (i, 0)),
                whole(bias.shape),
                by_row,
                by_row,
                whole(own.shape),
            ],
            out_specs=[
                pl.BlockSpec((heads * 3 * HD, width), lambda i, p: (p[GROUP], 0)),
                *[own_block(heads, n, length) for n in (3 * HD, HD, EXTRA)],
            ],
        ),
        out_shape=[jax.ShapeDtypeStruct(shape, BF16) for shape in shapes],
        compiler_params=params(),
        cost_estimate=cost(heads * tokens * (6 * HD * width + 16 * 64 * length), 12e6),
        name="attend_own",
    )(place, inputs, bias, qf, kf, own)


def attend_peers_kernel(spots, place_ref, x_ref, bias_ref, qf_ref, kf_ref, *refs):
    count = len(spots)
    parts = refs[:count]
    w_ref, qkv_ref, ctx_ref, aug_ref, wide_scr = refs[count + 4 :]

    @pl.when(pl.program_id(1) == 0)
    def _():
        size = w_ref.shape[0] // GROUP
        for ref, (index, offset) in zip(parts, spots):
            put(wide_scr, place_ref[index] * size + offset, ref[0], 8)
        w_ref[...] = wide_scr[...].astype(BF16)

    attend_rows(x_ref, bias_ref.at[0], qf_ref, kf_ref, w_ref, qkv_ref, ctx_ref, aug_ref)


def attend_peers(length, peers, place, inputs, bias, qf, kf, pieces, arrays):
    heads = arrays[1].shape[0] // peers
    tokens, width = inputs.shape
    spots = [(index, offset) for _, index, offset in pieces]
    parts = [array for array, _, _ in pieces]
    by_row = pl.BlockSpec((EXTRA, length), lambda k, i, *_: (0, i))
    return pl.pallas_call(
        lambda *refs: attend_peers_kernel(spots, *refs),
        grid_spec=pltpu.PrefetchScalarGridSpec(
            num_scalar_prefetch=1,
            grid=(peers - 1, tokens // length),
            in_specs=[
                pl.BlockSpec((length, width), lambda k, i, *_: (i, 0)),
                pl.BlockSpec((1,) + bias.shape[1:], lambda k, i, *_: (k, 0, 0)),
                by_row,
                by_row,
                *[
                    pl.BlockSpec((1,) + a.shape[1:], lambda k, i, *_: (k, 0, 0)) for a in parts
                ],
                *[ANY] * 4,
            ],
            out_specs=[
                pl.BlockSpec(
                    (heads * 3 * HD, width),
                    lambda k, i, p: (lax.rem(p[GROUP] + peers - 1 - k, peers), 0),
                ),
                *[peer_block(peers, 1, heads, n, length) for n in (3 * HD, HD, EXTRA)],
            ],
            scratch_shapes=[pltpu.VMEM((heads * 3 * HD, width), F32)],
        ),
        out_shape=[jax.ShapeDtypeStruct(a.shape, a.dtype) for a in arrays],
        input_output_aliases={5 + len(parts) + i: i for i in range(4)},
        compiler_params=params(),
        cost_estimate=cost(
            (peers - 1) * heads * tokens * (6 * HD * width + 16 * 64 * length), 30e6
        ),
        name="attend_peers",
    )(place, inputs, bias, qf, kf, *parts, *arrays)


def attend_back_rows(qkv_ref, ctx_ref, aug_ref, grad_ref, kf_ref, out_ref):
    heads, _, length = ctx_ref.shape
    block = length // 2
    scale = HD ** (-0.5)
    one = jnp.ones((1, block), F32)
    ones_rows = rows_of(EXTRA, 0, (one, one, one), block).astype(BF16)
    items = tiles(heads, block)
    scores, spreads = [], []
    for h, at in items:
        scores.append(
            dot(
                jnp.concatenate([qkv_ref[h, HD : 2 * HD, at], kf_ref[:, at]], axis=0),
                jnp.concatenate([qkv_ref[h, :HD, at], aug_ref[h, :, at]], axis=0),
                0,
                0,
            )
        )
    for h, at in items:
        grad = grad_ref[h, :, at]
        inner = jnp.sum(grad.astype(F32) * ctx_ref[h, :, at].astype(F32), axis=0, keepdims=True)
        grad_extra = rows_of(EXTRA, 0, split3(-inner), block).astype(BF16)
        spreads.append(
            dot(
                jnp.concatenate([qkv_ref[h, 2 * HD :, at], ones_rows], axis=0),
                jnp.concatenate([grad, grad_extra], axis=0),
                0,
                0,
            )
        )
    probs = [jnp.exp(part) for part in scores]
    slopes = [(part * spread).astype(BF16) for part, spread in zip(probs, spreads)]
    probs = [part.astype(BF16) for part in probs]
    for (h, at), part in zip(items, probs):
        out_ref[h, 2 * HD :, at] = dot(grad_ref[h, :, at], part, 1, 1).astype(BF16)
    for (h, at), part in zip(items, slopes):
        out_ref[h, HD : 2 * HD, at] = dot(qkv_ref[h, :HD, at], part, 1, 1).astype(BF16)
    for (h, at), part in zip(items, slopes):
        grad = dot(qkv_ref[h, HD : 2 * HD, at], part, 1, 0)
        out_ref[h, :HD, at] = (grad * scale).astype(BF16)


def attend_back_own_kernel(place_ref, qkv_ref, ctx_ref, aug_ref, grad_ref, kf_ref, *refs):
    x_ref, dwo_ref, small_ref, early_ref, out_ref, mine_ref, send_ref, grad_scr, sum_scr = refs
    heads = ctx_ref.shape[0]
    height = heads * HD
    step = pl.program_id(0)

    @pl.when(step == 0)
    def _():
        grad_scr[...] = jnp.zeros_like(grad_scr)
        sum_scr[...] = jnp.zeros_like(sum_scr)

    attend_back_rows(qkv_ref, ctx_ref, aug_ref, grad_ref, kf_ref, out_ref)
    ones = jnp.ones((8, x_ref.shape[0]), BF16)
    row = lax.broadcasted_iota(jnp.int32, (8, 3 * HD), 0)
    sums = jnp.zeros((8, 3 * HD), F32)
    for h in range(heads):
        grad = dot(out_ref[h], x_ref[...], 1, 0)
        for i in range(3):
            grad_scr[i * height + h * HD : i * height + (h + 1) * HD, :] += grad[
                i * HD : (i + 1) * HD
            ]
        sums = jnp.where(row == 3 + h, dot(ones, out_ref[h], 1, 1), sums)
    sum_scr[:, : 3 * HD] += sums

    @pl.when(step == pl.num_programs(0) - 1)
    def _():
        size, size_two = 3 * height // GROUP, height // GROUP
        top = size + size_two
        for rel in range(4):
            for source, ref in enumerate((mine_ref, send_ref)):
                owner = place_ref[2 * rel + source]
                ref[rel, :size, :] = grad_scr[pl.ds(pl.multiple_of(owner * size, 8), size), :]
                start = pl.multiple_of(owner * size_two, 8)
                ref[rel, size:top, :] = dwo_ref[pl.ds(start, size_two), :]
                ref[rel, top : top + 8, :] = jnp.where(
                    owner == 0, small_ref[...] + sum_scr[...], 0.0
                )
                ref[rel, top + 8 :, :] = jnp.where(owner == 0, early_ref[...], 0.0)


def attend_back_own(length, place, qkv, ctx, aug, grad, kf, inputs, dwo, small, early):
    height, width = dwo.shape
    heads = height // HD
    tokens = inputs.shape[0]
    share = 4 * height // GROUP + 16
    return pl.pallas_call(
        attend_back_own_kernel,
        grid_spec=pltpu.PrefetchScalarGridSpec(
            num_scalar_prefetch=1,
            grid=(tokens // length,),
            in_specs=[
                own_block(heads, 3 * HD, length),
                own_block(heads, HD, length),
                own_block(heads, EXTRA, length),
                own_block(heads, HD, length),
                pl.BlockSpec((EXTRA, length), lambda i, *_: (0, i)),
                pl.BlockSpec((length, width), lambda i, *_: (i, 0)),
                whole(dwo.shape),
                whole(small.shape),
                whole(early.shape),
            ],
            out_specs=[
                own_block(heads, 3 * HD, length),
                whole((4, share, width)),
                whole((4, share, width)),
            ],
            scratch_shapes=[pltpu.VMEM((3 * height, width), F32), pltpu.VMEM((8, width), F32)],
        ),
        out_shape=[jax.ShapeDtypeStruct(qkv.shape, BF16)]
        + [jax.ShapeDtypeStruct((4, share, width), F32)] * 2,
        compiler_params=params(),
        cost_estimate=cost(heads * tokens * (20 * 64 * length + 6 * HD * width), 12e6),
        name="attend_back_own",
    )(place, qkv, ctx, aug, grad, kf, inputs, dwo, small, early)


def attend_back_kernel(place_ref, qkv_ref, ctx_ref, aug_ref, grad_ref, kf_ref, old_ref, out_ref):
    attend_back_rows(qkv_ref, ctx_ref, aug_ref, grad_ref, kf_ref, out_ref)


def attend_back(length, peers, first, count, place, qkv, ctx, aug, grad, kf, out):
    every, _, tokens = qkv.shape
    heads = every // peers
    by_peer = lambda n: peer_block(peers, first, heads, n, length)
    return pl.pallas_call(
        attend_back_kernel,
        grid_spec=pltpu.PrefetchScalarGridSpec(
            num_scalar_prefetch=1,
            grid=(count, tokens // length),
            in_specs=[
                by_peer(3 * HD),
                by_peer(HD),
                by_peer(EXTRA),
                by_peer(HD),
                pl.BlockSpec((EXTRA, length), lambda k, i, *_: (0, i)),
                ANY,
            ],
            out_specs=by_peer(3 * HD),
        ),
        out_shape=jax.ShapeDtypeStruct(out.shape, BF16),
        input_output_aliases={6: 0},
        compiler_params=params(),
        cost_estimate=cost(count * heads * tokens * 20 * 64 * length, 12e6),
        name="attend_back",
    )(place, qkv, ctx, aug, grad, kf, out)


def norm_forward(hidden):
    center = hidden - jnp.mean(hidden, axis=-1, keepdims=True)
    inverse = lax.rsqrt(jnp.mean(center * center, axis=-1, keepdims=True) + EPS)
    return center * inverse, inverse


def norm_backward(grad, gain, norm, inverse):
    scaled = grad * gain
    first = jnp.mean(scaled, axis=-1, keepdims=True)
    second = jnp.mean(scaled * norm, axis=-1, keepdims=True)
    return (scaled - first - norm * second) * inverse


def column_sum(values):
    return jnp.sum(values, axis=0, keepdims=True)


def flat(values):
    return values.reshape(-1, values.shape[-1])


def fill(place_ref, own_ref, parts, spots, out_ref):
    shards, height, _ = out_ref.shape
    out_ref[place_ref[GROUP]] = own_ref[...]
    for k in range(1, shards):
        shard = peer_shard(place_ref, shards, k)
        for ref, (index, offset) in zip(parts, spots):
            start = place_ref[index] * (height // GROUP) + offset
            put(out_ref.at[shard], start, ref[k - 1], 16)


def expand_kernel(spots, place_ref, x_ref, ctx_ref, bias_ref, vec_ref, own_ref, own_wo_ref, *refs):
    parts, refs = refs[: len(spots)], refs[len(spots) :]
    sum_ref, act_ref, slope_ref, full_ref, wo_ref, we_ref, wide_scr, low_scr, sem = refs
    shards, width, _ = we_ref.shape
    size, size_two = width // GROUP, wo_ref.shape[0] // (shards * GROUP)
    kept = pltpu.make_async_copy(we_ref, full_ref, sem)

    @pl.when(pl.program_id(0) == 0)
    def _():
        me = place_ref[GROUP]
        we_ref[me] = own_ref[...]
        put(wide_scr, me * size_two * GROUP, own_wo_ref[...], 8)
        for k in range(1, shards):
            shard = peer_shard(place_ref, shards, k)
            for ref, (index, offset) in zip(parts, spots):
                part = ref[k - 1]
                count = min(part.shape[0], size - offset)
                put(we_ref.at[shard], place_ref[index] * size + offset, part[:count], 16)
                if count < part.shape[0]:
                    start = (shard * GROUP + place_ref[index]) * size_two
                    put(wide_scr, start, part[count:], 8)
        wo_ref[...] = wide_scr[...].astype(BF16)
        kept.start()

    @pl.when(pl.program_id(0) == pl.num_programs(0) - 1)
    def _():
        kept.wait()

    b_output, gain_one, shift_one = vec_ref[0:1], vec_ref[1:2], vec_ref[2:3]
    half = x_ref.shape[0] // 2
    halves = [slice(0, half), slice(half, 2 * half)]
    attended = [dot(flat(ctx_ref[:, :, at]), wo_ref[...], 0, 0) for at in halves]
    for at, part in zip(halves, attended):
        residual = x_ref[at, :].astype(F32) + (part + b_output)
        sum_ref[at, :] = residual
        norm_one, _ = norm_forward(residual)
        low_scr[at, :] = (norm_one * gain_one + shift_one).astype(BF16)

    def shard_step(s, carry):
        bias = bias_ref[peer_shard(place_ref, shards, s), 1:2]
        products = [dot(low_scr[at, :], we_ref[s], 1, 0) for at in halves]
        for at, product in zip(halves, products):
            hidden = product + bias
            square = hidden * hidden
            bent = jnp.tanh(hidden * (0.7978845608028654 + 0.035677408136300125 * square))
            gate = 0.5 + 0.5 * bent
            active = hidden * gate
            act_ref[s, at, :] = active.astype(BF16)
            slope = gate + (active * (1.0 - gate)) * (
                1.5957691216057308 + 0.21406444881780075 * square
            )
            slope_ref[s, at, :] = slope.astype(BF16)
        return carry

    lax.fori_loop(0, shards, shard_step, 0, unroll=2)


def expand(place, inputs, ctx, biases, vectors, own, own_wo, pieces, shards):
    tokens, width = inputs.shape
    hidden = own.shape[1]
    every = ctx.shape[0]
    block = 512
    spots = [(index, offset) for _, index, offset in pieces]
    parts = [array for array, _, _ in pieces]
    full = (shards, width, hidden)
    by_token = lambda: pl.BlockSpec((block, width), lambda i, *_: (i, 0))
    by_shard = lambda: pl.BlockSpec((shards, block, hidden), lambda i, *_: (0, i, 0))
    return pl.pallas_call(
        lambda *refs: expand_kernel(spots, *refs),
        grid_spec=pltpu.PrefetchScalarGridSpec(
            num_scalar_prefetch=1,
            grid=(tokens // block,),
            in_specs=[
                by_token(),
                pl.BlockSpec((every, HD, block), lambda i, *_: (0, 0, i)),
                whole(biases.shape),
                whole(vectors.shape),
                whole(own.shape),
                whole(own_wo.shape),
                *[whole(a.shape) for a in parts],
            ],
            out_specs=[by_token(), by_shard(), by_shard(), ANY, whole((every * HD, width))],
            scratch_shapes=[
                pltpu.VMEM(full, BF16),
                pltpu.VMEM((every * HD, width), F32),
                pltpu.VMEM((block, width), BF16),
                pltpu.SemaphoreType.DMA,
            ],
        ),
        out_shape=[
            jax.ShapeDtypeStruct((tokens, width), F32),
            jax.ShapeDtypeStruct((shards, tokens, hidden), BF16),
            jax.ShapeDtypeStruct((shards, tokens, hidden), BF16),
            jax.ShapeDtypeStruct(full, BF16),
            jax.ShapeDtypeStruct((every * HD, width), BF16),
        ],
        compiler_params=params(),
        cost_estimate=cost(2 * tokens * width * (shards * hidden + every * HD), 40e6),
        name="expand",
    )(place, inputs, ctx, biases, vectors, own, own_wo, *parts)


def reduce_kernel(spots, place_ref, sum_ref, cot_ref, act_ref, slope_ref, vec_ref, *refs):
    own_ref, refs = refs[0], refs[1:]
    piece_refs, refs = refs[: len(spots)], refs[len(spots) :]
    out_ref, g2_ref, full_ref, mine_ref, send_ref, small_scr = refs[:6]
    dwe_scr, dwr_scr, wr_ref, sems = refs[6:]
    kept = pltpu.make_async_copy(wr_ref, full_ref, sems.at[0])
    step = pl.program_id(0)
    shards = act_ref.shape[0]
    me = place_ref[GROUP]

    @pl.when(step == 0)
    def _():
        fill(place_ref, own_ref, piece_refs, spots, wr_ref)
        kept.start()
        for scr in (dwe_scr, dwr_scr, small_scr):
            scr[...] = jnp.zeros_like(scr)

    gain_one, shift_one = vec_ref[1:2], vec_ref[2:3]
    b_reduce, gain_two, shift_two = vec_ref[3:4], vec_ref[4:5], vec_ref[5:6]
    half = sum_ref.shape[0] // 2
    halves = [slice(0, half), slice(half, 2 * half)]
    quarter = half // 4
    width = sum_ref.shape[1]
    small = [jnp.zeros((1, width), F32)] * 4

    def norm_part(start, mixed):
        at = slice(start, start + quarter)
        norm_one, _ = norm_forward(sum_ref[at, :])
        normed = norm_one * gain_one + shift_one
        norm_two, inverse_two = norm_forward(normed + (mixed + b_reduce))
        out_ref[at, :] = (norm_two * gain_two + shift_two).astype(BF16)
        cot = cot_ref[at, :].astype(F32)
        grad_two = norm_backward(cot, gain_two, norm_two, inverse_two)
        g2_ref[at, :] = grad_two
        small[0] = small[0] + column_sum(grad_two)
        small[1] = small[1] + column_sum(cot * norm_two)
        small[2] = small[2] + column_sum(cot)
        return grad_two.astype(BF16), normed.astype(BF16)

    first, second = halves
    mixed = dot(act_ref[0, first, :], wr_ref[0], 1, 0)
    for s in range(1, shards):
        mixed = mixed + dot(act_ref[s, first, :], wr_ref[s], 1, 0)
    later = None
    parts = []
    for s in range(shards):
        product = dot(act_ref[s, second, :], wr_ref[s], 1, 0)
        later = product if later is None else later + product
        parts.append(norm_part(s * quarter, mixed[s * quarter : (s + 1) * quarter]))
    low_a = jnp.concatenate([part[0] for part in parts], axis=0)
    normed_a = jnp.concatenate([part[1] for part in parts], axis=0)
    active_a = dot(low_a, own_ref[...], 1, 1)
    parts = [norm_part(half + s * quarter, later[s * quarter : (s + 1) * quarter]) for s in (0, 1)]
    dwr_scr[...] += dot(act_ref[me, first, :], low_a, 0, 0)
    parts += [norm_part(half + s * quarter, later[s * quarter : (s + 1) * quarter]) for s in (2, 3)]
    own_a = (active_a * slope_ref[0, first, :].astype(F32)).astype(BF16)
    low_b = jnp.concatenate([part[0] for part in parts], axis=0)
    normed_b = jnp.concatenate([part[1] for part in parts], axis=0)
    active_b = dot(low_b, own_ref[...], 1, 1)
    small[3] = small[3] + column_sum(own_a.astype(F32))
    dwe_scr[...] += dot(normed_a, own_a, 0, 0)
    own_b = (active_b * slope_ref[0, second, :].astype(F32)).astype(BF16)
    dwr_scr[...] += dot(act_ref[me, second, :], low_b, 0, 0)
    small[3] = small[3] + column_sum(own_b.astype(F32))
    dwe_scr[...] += dot(normed_b, own_b, 0, 0)
    for n, part in enumerate(small):
        small_scr[n : n + 1] += part

    @pl.when(step == pl.num_programs(0) - 1)
    def _():
        copies = [kept]
        for rel in range(4):
            for source, ref in ((1, send_ref), (0, mine_ref)):
                owner = place_ref[2 * rel + source]
                top = 0
                for scr in (dwe_scr, dwr_scr):
                    size = scr.shape[0] // GROUP
                    start = pl.multiple_of(owner * size, 8)
                    copy = pltpu.make_async_copy(
                        scr.at[pl.ds(start, size), :],
                        ref.at[rel, top : top + size, :],
                        sems.at[len(copies)],
                    )
                    copy.start()
                    copies.append(copy)
                    top += size
        for copy in copies:
            copy.wait()


def reduce(place, residual, cot, act, slope, vectors, own, pieces):
    tokens, width = residual.shape
    shards, _, hidden = act.shape
    block = 512
    share = (width + hidden) // GROUP
    spots = [(index, offset) for _, index, offset in pieces]
    arrays = [array for array, _, _ in pieces]
    by_token = lambda: pl.BlockSpec((block, width), lambda i, *_: (i, 0))
    return pl.pallas_call(
        lambda *refs: reduce_kernel(spots, *refs),
        grid_spec=pltpu.PrefetchScalarGridSpec(
            num_scalar_prefetch=1,
            grid=(tokens // block,),
            in_specs=[
                by_token(),
                by_token(),
                pl.BlockSpec((shards, block, hidden), lambda i, *_: (0, i, 0)),
                pl.BlockSpec((1, block, hidden), lambda i, p: (p[GROUP], i, 0)),
                whole(vectors.shape),
                whole(own.shape),
                *[whole(a.shape) for a in arrays],
            ],
            out_specs=[
                by_token(),
                by_token(),
                ANY,
                ANY,
                ANY,
                whole((8, width)),
            ],
            scratch_shapes=[
                pltpu.VMEM((width, hidden), F32),
                pltpu.VMEM((hidden, width), F32),
                pltpu.VMEM((shards, hidden, width), BF16),
                pltpu.SemaphoreType.DMA((17,)),
            ],
        ),
        out_shape=[
            jax.ShapeDtypeStruct((tokens, width), BF16),
            jax.ShapeDtypeStruct((tokens, width), F32),
            jax.ShapeDtypeStruct((shards, hidden, width), BF16),
            jax.ShapeDtypeStruct((4, share, width), F32),
            jax.ShapeDtypeStruct((4, share, width), F32),
            jax.ShapeDtypeStruct((8, width), F32),
        ],
        compiler_params=params(),
        cost_estimate=cost(tokens * width * hidden * (2 * shards + 6), 40e6),
        name="reduce",
    )(place, residual, cot, act, slope, vectors, own, *arrays)


def return_kernel(place_ref, sum_ref, g2_ref, slope_ref, ctx_ref, we_ref, wr_ref, w_ref, *refs):
    vec_ref, g1_ref, dctx_ref, dwo_ref, small_ref = refs
    shards = we_ref.shape[0]

    @pl.when(pl.program_id(0) == 0)
    def _():
        dwo_ref[...] = jnp.zeros_like(dwo_ref)
        small_ref[...] = jnp.zeros_like(small_ref)

    half = sum_ref.shape[0] // 2
    halves = [slice(0, half), slice(half, 2 * half)]
    gain_one = vec_ref[1:2]
    low = [g2_ref[at, :].astype(BF16) for at in halves]
    items = [(s, i) for s in range(shards) for i in range(2)]
    total = [g2_ref[at, :] for at in halves]
    ahead = dot(low[0], wr_ref[0], 1, 1)
    for n, (s, i) in enumerate(items):
        grad_active = ahead
        if n + 1 < len(items):
            s_next, i_next = items[n + 1]
            ahead = dot(low[i_next], wr_ref[s_next], 1, 1)
        grad_hidden = (grad_active * slope_ref[s, halves[i], :].astype(F32)).astype(BF16)
        total[i] = total[i] + dot(grad_hidden, we_ref[s], 1, 1)
    small = [jnp.zeros((1, sum_ref.shape[1]), F32)] * 3
    one = []
    for at, grad_normed in zip(halves, total):
        norm_one, inverse_one = norm_forward(sum_ref[at, :])
        grad_one = norm_backward(grad_normed, gain_one, norm_one, inverse_one)
        g1_ref[at, :] = grad_one
        one.append(grad_one.astype(BF16))
        small[0] = small[0] + column_sum(grad_one)
        small[1] = small[1] + column_sum(grad_normed * norm_one)
        small[2] = small[2] + column_sum(grad_normed)
    one = jnp.concatenate(one, axis=0)
    dctx = dot(w_ref[...], one, 1, 1)
    dwo_ref[...] += dot(flat(ctx_ref[...]), one, 1, 0)
    dctx_ref[...] = dctx.astype(BF16).reshape(dctx_ref.shape)
    for n, part in enumerate(small):
        small_ref[n : n + 1] += part


def back_to_context(place, residual, grad_two, slope, ctx, w_expand, w_reduce, weights, vectors):
    tokens, width = residual.shape
    shards, _, hidden = w_expand.shape
    every = ctx.shape[0]
    heads = every // shards
    block = 512
    by_token = lambda: pl.BlockSpec((block, width), lambda i, *_: (i, 0))
    return pl.pallas_call(
        return_kernel,
        grid_spec=pltpu.PrefetchScalarGridSpec(
            num_scalar_prefetch=1,
            grid=(tokens // block,),
            in_specs=[
                by_token(),
                by_token(),
                pl.BlockSpec((shards, block, hidden), lambda i, *_: (0, i, 0)),
                own_block(heads, HD, block),
                whole(w_expand.shape),
                whole(w_reduce.shape),
                whole(weights.shape),
                whole(vectors.shape),
            ],
            out_specs=[
                by_token(),
                pl.BlockSpec((every, HD, block), lambda i, *_: (0, 0, i)),
                whole((heads * HD, width)),
                whole((8, width)),
            ],
        ),
        out_shape=[
            jax.ShapeDtypeStruct((tokens, width), F32),
            jax.ShapeDtypeStruct(ctx.shape, BF16),
            jax.ShapeDtypeStruct((heads * HD, width), F32),
            jax.ShapeDtypeStruct((8, width), F32),
        ],
        compiler_params=params(),
        cost_estimate=cost(tokens * width * (4 * shards * hidden + 2 * every * HD), 40e6),
        name="back_to_context",
    )(place, residual, grad_two, slope, ctx, w_expand, w_reduce, weights, vectors)


def spread_kernel(spots, place_ref, *refs):
    parts, outs = refs[: len(spots)], refs[len(spots) :]
    for ref, (index, offset) in zip(parts, spots):
        start = 0
        for i, out_ref in enumerate(outs):
            size = out_ref.shape[0] // GROUP
            if offset <= i * size < offset + ref.shape[1]:
                put(out_ref, place_ref[index] * size, ref[0, start : start + size, :], 8)
                start += size


def spread(place, pieces, sizes):
    spots = [(index, offset) for _, index, offset in pieces]
    parts = [array for array, _, _ in pieces]
    width = parts[0].shape[2]
    shapes = [(GROUP * size, width) for size in sizes]
    return pl.pallas_call(
        lambda *refs: spread_kernel(spots, *refs),
        grid_spec=pltpu.PrefetchScalarGridSpec(
            num_scalar_prefetch=1,
            grid=(1,),
            in_specs=[whole(a.shape) for a in parts],
            out_specs=[whole(s) for s in shapes],
        ),
        out_shape=[jax.ShapeDtypeStruct(s, F32) for s in shapes],
        compiler_params=params(16 << 20),
        cost_estimate=cost(0, 10e6),
        name="spread",
    )(place, *parts)


def spread_late_kernel(heads, place_ref, *refs):
    parts = refs[:GROUP]
    dq_ref, dk_ref, dv_ref, dwo_ref, small_ref, grad_scr = refs[GROUP:]
    height = heads * HD
    size, size_two = 3 * height // GROUP, height // GROUP
    top = size + size_two
    for i, ref in enumerate(parts):
        owner = place_ref[i]
        put(grad_scr, owner * size, ref[:size, :], 8)
        put(dwo_ref, owner * size_two, ref[size:top, :], 8)

        @pl.when(owner == 0)
        def _():
            small_ref[...] = ref[top:, :]

    for i, out_ref in enumerate((dq_ref, dk_ref, dv_ref)):
        out_ref[...] = grad_scr[i * height : (i + 1) * height, :]


def spread_late(place, parts, heads):
    share, width = parts[0].shape
    height = heads * HD
    shapes = [(height, width)] * 4 + [(16, width)]
    return pl.pallas_call(
        lambda *refs: spread_late_kernel(heads, *refs),
        grid_spec=pltpu.PrefetchScalarGridSpec(
            num_scalar_prefetch=1,
            grid=(1,),
            in_specs=[whole(a.shape) for a in parts],
            out_specs=[whole(s) for s in shapes],
            scratch_shapes=[pltpu.VMEM((3 * height, width), F32)],
        ),
        out_shape=[jax.ShapeDtypeStruct(s, F32) for s in shapes],
        compiler_params=params(10 << 20),
        cost_estimate=cost(0, 8 * parts[0].size * 8),
        name="spread_late",
    )(place, *parts)


def input_grads_kernel(place_ref, g1_ref, grad_ref, w_ref, out_ref):
    amount = place_ref[GROUP + 1 + pl.program_id(0)]
    matrix = shift_matrix(amount, g1_ref.shape[0], False)
    total = g1_ref[...] + dot(flat(grad_ref[...]), w_ref[...], 0, 0)
    out_ref[...] = dot(matrix, total.astype(BF16), 1, 0).astype(BF16)


def input_grads(place, length, grad_one, grads, weights):
    tokens, width = grad_one.shape
    every = grads.shape[0]
    by_row = lambda: pl.BlockSpec((length, width), lambda i, *_: (i, 0))
    return pl.pallas_call(
        input_grads_kernel,
        grid_spec=pltpu.PrefetchScalarGridSpec(
            num_scalar_prefetch=1,
            grid=(tokens // length,),
            in_specs=[
                by_row(),
                pl.BlockSpec((every, 3 * HD, length), lambda i, *_: (0, 0, i)),
                whole(weights.shape),
            ],
            out_specs=by_row(),
        ),
        out_shape=jax.ShapeDtypeStruct((tokens, width), BF16),
        compiler_params=params(56 << 20),
        cost_estimate=cost(2 * tokens * width * (every * 3 * HD + length), 20e6),
        name="input_grads",
    )(place, grad_one, grads, weights)


def after(values, *others):
    return lax.optimization_barrier((values, others))[0]


def solution(mesh):
    peers = mesh.shape["mp"]
    lanes = mesh.shape["dp"]
    rotations = [[(i, (i + k) % peers) for i in range(peers)] for k in range(1, peers)]

    def flip(values, bits):
        return lax.ppermute(values, "dp", [(i, i ^ bits) for i in range(lanes)])

    def from_peers(piece):
        return jnp.stack([lax.ppermute(piece, "mp", perm) for perm in rotations])

    def swapped(piece, *ready):
        copies = jnp.broadcast_to(piece[None], (peers,) + piece.shape)
        got = lax.all_to_all(after(copies, *ready), "mp", 0, 0, tiled=True)
        me = lax.axis_index("mp")
        return jnp.concatenate(
            [
                lax.dynamic_slice_in_dim(got, lax.rem(me + peers - k, peers), 1, 0)
                for k in range(1, peers)
            ]
        )

    def both(near):
        return flip(near, 2), flip(near, 4)

    def corner(by_x, by_y, cut):
        return flip(by_y[:, :cut], 2), flip(by_x[:, cut:], 4)

    def listed(near, by_x, by_y, first, second, cut):
        places = ((near, 0, 0), (by_x, 1, 0), (by_y, 2, 0), (first, 3, 0), (second, 3, cut))
        return with_core(places)

    def with_core(places):
        out = []
        for array, rel, offset in places:
            out.append((array, 2 * rel, offset))
            out.append((flip(array, 1), 2 * rel + 1, offset))
        return out

    def sum_groups(total):
        step = GROUP
        while step < lanes:
            total = total + flip(total, step)
            step *= 2
        return total

    def partial_sums(mine, got, *ready):
        got = after(got, *ready)
        return [mine[rel] + got[rel] for rel in range(4)]

    def exchange(parts):
        return [flip(parts[rel], 2 * rel) for rel in (1, 2, 3)]

    def total_of(first, rest, *ready):
        rest = after(rest, *ready)
        return sum_groups(first + rest[0] + rest[1] + rest[2])

    def finish(arrays, *ready):
        out = []
        for array in after(arrays, *ready):
            out += [array, flip(array, 1)]
        return out

    def local(
        tokens,
        doc_lengths,
        w_query,
        b_query,
        w_key,
        w_value,
        b_value,
        w_output,
        b_output,
        gain_attn,
        shift_attn,
        w_expand,
        b_expand,
        w_reduce,
        b_reduce,
        gain_ffn,
        shift_ffn,
        cotangent,
    ):
        row_count, length, width = tokens.shape
        heads = w_query.shape[1] // HD
        hidden = w_expand.shape[1]
        count = row_count * length
        inside = lax.axis_index("dp") % GROUP
        me = lax.axis_index("mp")
        ends = jnp.cumsum(doc_lengths, axis=-1)
        longest = jnp.max(doc_lengths, axis=-1, keepdims=True)
        offset = jnp.max(jnp.where(doc_lengths == longest, ends - doc_lengths, 0), axis=-1)
        place = jnp.stack([inside ^ i for i in range(GROUP)] + [me])
        place = jnp.concatenate([place, offset]).astype(jnp.int32)

        by_head = lambda w: w.T.reshape(heads, HD, width)
        own_heads = jnp.concatenate([by_head(w_query), by_head(w_key), by_head(w_value)], axis=1)
        own_heads = own_heads.reshape(3 * heads * HD, width)
        blank = jnp.zeros((width - 2 * heads * HD,), BF16)
        own_bias = jnp.stack(
            [jnp.concatenate([b_query, b_value, blank]), b_expand]
            + [jnp.zeros((width,), BF16)] * 6
        ).astype(F32)

        def piece_of(array, bits=0):
            size = array.shape[0] // GROUP
            return lax.dynamic_slice_in_dim(array, (inside ^ bits) * size, size, 0).astype(F32)

        piece = piece_of(own_heads)
        near = from_peers(jnp.concatenate([piece, own_bias]))

        position = (jnp.arange(length, dtype=jnp.int32)[None] + offset[:, None]) % length
        segment = jnp.sum((position[:, :, None] >= ends[:, None, :]).astype(jnp.int32), axis=-1)
        segment = segment.reshape(1, count)
        docs = doc_lengths.shape[1]
        label = jnp.arange(EXTRA, dtype=jnp.int32)[:, None]
        is_doc = label < docs
        qf = jnp.where(is_doc & (segment == label), 1.0, 0.0).astype(BF16)
        kf = jnp.where(
            is_doc,
            jnp.where(segment == label, 0.0, MASK),
            jnp.where(label < docs + 3, 1.0, 0.0),
        ).astype(BF16)
        inputs, cot = shift(
            place, length, tokens.reshape(count, width), cotangent.reshape(count, width)
        )
        own = attend_own(
            length, peers, place, inputs, own_bias, qf, kf, own_heads
        )

        near = after(near, own)
        biases = near[:, -own_bias.shape[0] :]
        all_biases = jnp.concatenate([own_bias[None], biases])
        near = near[:, : -own_bias.shape[0]]
        cut = piece.shape[0] // 16 * 8
        share = jnp.concatenate([piece_of(w_expand), piece_of(w_output)])
        near_expand = swapped(share, near)
        sides = both(near)
        corners = corner(*sides, cut)
        pieces = listed(near, *sides, *corners, cut)
        sides_expand = both(after(near_expand, corners))
        near_reduce = swapped(piece_of(w_reduce), near_expand, [array for array, _, _ in pieces])
        weights, qkv, ctx, aug = attend_peers(
            length, peers, place, inputs, after(biases, near_expand), qf, kf, pieces, own
        )

        sides_expand = after(sides_expand, ctx)
        cut = share.shape[0] // 2 // 16 * 16 + 16
        corners = corner(*sides_expand, cut)
        vectors = jnp.stack(
            [b_output, gain_attn, shift_attn, b_reduce, gain_ffn, shift_ffn]
            + [jnp.zeros((width,), BF16)] * 2
        ).astype(F32)
        pieces = listed(near_expand, *sides_expand, *corners, cut)
        near_reduce = after(near_reduce, sides_expand)
        diagonal = swapped(piece_of(w_reduce, 6), near_reduce)
        sides_reduce = both(near_reduce)
        residual, act, slope, all_expand, all_output = expand(
            place,
            inputs,
            ctx,
            after(all_biases, near_reduce),
            vectors,
            w_expand,
            w_output,
            pieces,
            peers,
        )
        far_reduce = after((*sides_reduce, diagonal), act)
        pieces = with_core([(array, rel, 0) for rel, array in enumerate([near_reduce, *far_reduce])])
        shifted, grad_two, all_reduce, mine, send, small_one = reduce(
            place, residual, cot, act, slope, vectors, w_reduce, pieces
        )
        got = flip(send, 1)
        output = unshift(place, length, shifted)
        chip = partial_sums(mine, got, output)
        early = exchange(chip)
        grad_one, dctx, dwo, small = back_to_context(
            place,
            residual,
            grad_two,
            slope,
            ctx,
            all_expand,
            all_reduce,
            all_output,
            after(vectors, chip),
        )
        early = total_of(chip[0], early, grad_one)[None]
        sides = both(early)
        dqkv, mine, send = attend_back_own(
            length, place, qkv, ctx, aug, dctx, after(kf, early), inputs, dwo, small, small_one
        )
        got = flip(after(send, sides), 1)
        dqkv = attend_back(
            length, peers, 1, 1, place, qkv, ctx, aug, dctx, after(kf, sides), dqkv
        )
        across = flip(after(early, sides), 6)
        beside = [flip(array, 1) for array in (early, *sides)]
        parts = partial_sums(mine, got, dqkv)
        rest = exchange(parts)
        across, beside, kept = after((across, beside, kf), parts)
        dqkv = attend_back(length, peers, 2, peers - 2, place, qkv, ctx, aug, dctx, kept, dqkv)
        total = total_of(parts[0], rest, dqkv)
        second = [total] + exchange([None] + [total] * 3)
        beside.append(flip(across, 1))
        pieces = []
        for rel, (near, far) in enumerate(zip((early, *sides, across), beside)):
            pieces += [(near, 2 * rel, 0), (far, 2 * rel + 1, 0)]
        grad_one = after(grad_one, total, beside)
        grad_tokens = input_grads(place, length, grad_one, dqkv, weights)
        second = finish(second, grad_tokens)
        dwe, dwr = spread(place, pieces, [width // GROUP, hidden // GROUP])
        dq, dk, dv, dwo, small_two = spread_late(place, second, heads)
        sums = lambda i: small_two[3 : 3 + heads, i * HD : (i + 1) * HD].reshape(heads * HD)
        shape = (row_count, length, width)
        return (
            output.reshape(shape),
            grad_tokens.reshape(shape),
            dq.T,
            sums(0),
            dk.T,
            dv.T,
            sums(2),
            dwo,
            small_two[0],
            small_two[1],
            small_two[2],
            dwe,
            small_two[11],
            dwr,
            small_two[8],
            small_two[9],
            small_two[10],
        )

    rows, split = P("dp", None, None), P(None, "mp")
    return jax.shard_map(
        local,
        mesh=mesh,
        in_specs=(
            rows,
            P("dp", None),
            split,
            P("mp"),
            split,
            split,
            P("mp"),
            P("mp", None),
            P(),
            P(),
            P(),
            split,
            P("mp"),
            P("mp", None),
            P(),
            P(),
            P(),
            rows,
        ),
        out_specs=(
            rows,
            rows,
            split,
            P("mp"),
            split,
            split,
            P("mp"),
            P("mp", None),
            P(),
            P(),
            P(),
            split,
            P("mp"),
            P("mp", None),
            P(),
            P(),
            P(),
        ),
        check_vma=False,
    )
```
